32 devices in a mesh: ctx: 8 (over z, x), fsdp: 4 (over y, core).
Axes of the slice: x: 2, y: 2, z: 4, core: 2. Of those that a mesh axis runs over, the one named last changes fastest.
Arguments:
- tokens: bfloat16 [8, 1024, 768], P('fsdp', 'ctx'), may hold values from -6 to 6
- chars: bfloat16 [8, 1360, 768], P('fsdp', 'ctx'), may hold values from -6 to 6
- segment: int32 [8, 1024], P('fsdp', 'ctx'), may hold values from 0 to 3, as said below
- char_end: int32 [8, 1024], P('fsdp', 'ctx'), may hold values from 0 to 169, as said below
- w_qkv: bfloat16 [768, 2304], P('fsdp'), may hold values from -0.21875 to 0.21875
- w_out: bfloat16 [768, 768], P('fsdp'), may hold values from -4 to 4
- norm1_gain: bfloat16 [768], P('fsdp'), may hold values from 0.5 to 1.5
- norm1_bias: bfloat16 [768], P('fsdp'), may hold values from -1.796875 to 1.796875
- w_up: bfloat16 [768, 3072], P('fsdp'), may hold values from -0.21875 to 0.21875
- b_up: bfloat16 [3072], P('fsdp'), may hold values from -1.796875 to 1.796875
- w_down: bfloat16 [3072, 768], P('fsdp'), may hold values from -0.109375 to 0.109375
- norm2_gain: bfloat16 [768], P('fsdp'), may hold values from 0.5 to 1.5
- norm2_bias: bfloat16 [768], P('fsdp'), may hold values from -1.796875 to 1.796875
- w_gru: bfloat16 [768, 1536], P('fsdp'), may hold values from -0.21875 to 0.21875
- b_gate: bfloat16 [768], P('fsdp'), may hold values from 2.5 to 9
- w_ftok: bfloat16 [768, 768], P('fsdp'), may hold values from -0.21875 to 0.21875
- w_fchr: bfloat16 [768, 768], P('fsdp'), may hold values from -1.75 to 1.75
- w_conv: bfloat16 [3, 1536, 1536], P(None, 'fsdp'), may hold values from -0.09375 to 0.09375
- norm3_gain: bfloat16 [768], P('fsdp'), may hold values from 0.5 to 1.5
- norm3_bias: bfloat16 [768], P('fsdp'), may hold values from -1.796875 to 1.796875
- norm4_gain: bfloat16 [768], P('fsdp'), may hold values from 0.5 to 1.5
- norm4_bias: bfloat16 [768], P('fsdp'), may hold values from -1.796875 to 1.796875
- d_token: bfloat16 [8, 1024, 768], P('fsdp', 'ctx'), may hold values from -6 to 6
- d_char: bfloat16 [8, 1024, 768], P('fsdp', 'ctx'), may hold values from -6 to 6
Outputs:
- token_out: bfloat16 [8, 1024, 768], P('fsdp', 'ctx')
- char_out: bfloat16 [8, 1024, 768], P('fsdp', 'ctx')
- d_tokens: bfloat16 [8, 1024, 768], P('fsdp', 'ctx')
- d_chars: bfloat16 [8, 1360, 768], P('fsdp', 'ctx')
- qkv_grad: float32 [768, 2304], P('fsdp')
- wout_grad: float32 [768, 768], P('fsdp')
- gain1_grad: float32 [768], P('fsdp')
- bias1_grad: float32 [768], P('fsdp')
- up_grad: float32 [768, 3072], P('fsdp')
- bup_grad: float32 [3072], P('fsdp')
- down_grad: float32 [3072, 768], P('fsdp')
- gain2_grad: float32 [768], P('fsdp')
- bias2_grad: float32 [768], P('fsdp')
- gru_grad: float32 [768, 1536], P('fsdp')
- bgate_grad: float32 [768], P('fsdp')
- ftok_grad: float32 [768, 768], P('fsdp')
- fchr_grad: float32 [768, 768], P('fsdp')
- conv_grad: float32 [3, 1536, 1536], P(None, 'fsdp')
- gain3_grad: float32 [768], P('fsdp')
- bias3_grad: float32 [768], P('fsdp')
- gain4_grad: float32 [768], P('fsdp')
- bias4_grad: float32 [768], P('fsdp')
The draws below stay inside these ranges and needn't reach their ends.
Inputs may be any that keep to these rules, and one draw needn't show every extreme that they name: Within each sequence the ids start at 0, never fall and rise by one where a new segment begins; the segment with id 1 begins on the first index of ctx and ends on the last, every other segment lies within the first or the last 128 tokens. `char_end`: each aligned block of 128 tokens (one index of ctx) owns the block of 170 characters at the same index; a token's value is its last character as an index within that block, strictly rising along the block, the block's last token ending at 169.
All inputs are finite; a program needn't handle non-finite values.
Results may differ from the reference program's by a relative error of at most 0.02.
Values may be sent and summed in bfloat16 or wider, within the bound.
No kernel may reach another device: no remote copies, remote signals or barrier semaphores. Data moves between devices by JAX's collectives and lax.ppermute only.
A program may use at most 320 MiB of HBM per device.

```python
import jax
import jax.numpy as jnp
from jax import lax

D = 768
HEADS = 12
HEAD_DIM = 64
FF = 3072
GRU_H = 384
TOK_DEV = 128
CH_DEV = 170
SEQ = 1024
CHARS = 1360
BATCH = 8
N_CTX = 8


def draw_segment(key, part):
    keys = jax.random.split(key, 3)
    first = jax.random.randint(keys[0], (BATCH, 1), 1, TOK_DEV)
    tail = jax.random.randint(keys[1], (BATCH, 1), 1, TOK_DEV)
    inside = jax.random.randint(keys[2], (BATCH, 1), 1, TOK_DEV)
    positions = jnp.arange(SEQ, dtype=jnp.int32)[None, :]
    split_tail = jnp.where(inside < tail, SEQ - tail + inside, SEQ)
    ids = (positions >= first).astype(jnp.int32) + (positions >= SEQ - tail).astype(jnp.int32)
    ids = ids + (positions >= split_tail).astype(jnp.int32)
    return ids.astype(jnp.int32)


def draw_char_end(key, part):
    span = CH_DEV - 1
    blocks = SEQ // TOK_DEV
    scores = jax.random.randint(key, (BATCH, blocks, span), 0, 4096) * span + jnp.arange(span, dtype=jnp.int32)
    order = jnp.argsort(scores, axis=-1)
    chosen = jnp.sort(order[:, :, :TOK_DEV - 1], axis=-1).astype(jnp.int32)
    ending = jnp.full((BATCH, blocks, 1), span, jnp.int32)
    return jnp.concatenate([chosen, ending], axis=-1).reshape(BATCH, SEQ).astype(jnp.int32)


def block_levels(own_key, dims, pieces, least, largest):
    level = 1.0
    for axis_at, parts in pieces:
        draws = jax.random.uniform(jax.random.fold_in(jax.random.fold_in(own_key, 6), axis_at), (parts,), jnp.float32, least / len(pieces), largest / len(pieces))
        level = level * jnp.repeat(jnp.exp(draws), dims[axis_at] // parts).reshape((-1,) + (1,) * (len(dims) - 1 - axis_at))
    return level


def noise(rng, dims, scale, reach, cuts=(), kind=jnp.bfloat16):
    array = jax.random.normal(rng, dims, jnp.float32) * scale
    if len(cuts) > 0:
        array = block_levels(rng, dims, cuts, -0.22, 0.18) * array
    return jnp.clip(array, min=-reach, max=reach).astype(kind)


def setup_inputs(seed: int = 0) -> dict:
    key_of = jax.random.split(jax.random.key(seed), 25)
    tokens = noise(key_of[0], (BATCH, SEQ, D), 1.0, 6.0, ((0, 4), (1, 8)))
    chars = noise(key_of[1], (BATCH, CHARS, D), 1.0, 6.0, ((0, 4), (1, 8)))
    segment = draw_segment(jax.random.fold_in(key_of[24], 71), 0)
    char_end = draw_char_end(jax.random.fold_in(key_of[24], 71), 0)
    w_qkv = noise(key_of[4], (D, 3 * D), D ** -0.5, 0.21875, ((0, 4),))
    w_out = noise(key_of[5], (D, D), (max(1, 3 * D // (TOK_DEV * N_CTX))) ** -0.5, 4.0, ((0, 4),))
    norm1_gain = jnp.clip(1.0 + 0.1 * jax.random.normal(key_of[6], (D,), jnp.float32), 0.5, 1.5).astype(jnp.bfloat16)
    norm1_bias = noise(key_of[7], (D,), 0.3, 1.796875, ((0, 4),))
    w_up = noise(key_of[8], (D, FF), D ** -0.5, 0.21875, ((0, 4),))
    b_up = noise(key_of[9], (FF,), 0.3, 1.796875, ((0, 4),))
    w_down = noise(key_of[10], (FF, D), FF ** -0.5, 0.109375, ((0, 4),))
    norm2_gain = jnp.clip(1.0 + 0.1 * jax.random.normal(key_of[11], (D,), jnp.float32), 0.5, 1.5).astype(jnp.bfloat16)
    norm2_bias = noise(key_of[12], (D,), 0.3, 1.796875, ((0, 4),))
    w_gru = noise(key_of[13], (D, 4 * GRU_H), D ** -0.5, 0.21875, ((0, 4),))
    b_gate = jnp.clip(2.5 + 6.5 * jax.random.uniform(key_of[14], (2 * GRU_H,), jnp.float32) ** block_levels(key_of[14], (2 * GRU_H,), ((0, 4),), -0.2, 0.2), 2.5, 9.0).astype(jnp.bfloat16)
    w_ftok = noise(key_of[15], (D, D), D ** -0.5, 0.21875, ((0, 4),))
    w_fchr = noise(key_of[16], (D, D), (max(1, D // 64)) ** -0.5, 1.75, ((0, 4),))
    w_conv = noise(key_of[17], (3, 2 * D, 2 * D), (6 * D) ** -0.5, 0.09375, ((1, 4),))
    norm3_gain = jnp.clip(1.0 + 0.1 * jax.random.normal(key_of[18], (D,), jnp.float32), 0.5, 1.5).astype(jnp.bfloat16)
    norm3_bias = noise(key_of[19], (D,), 0.3, 1.796875, ((0, 4),))
    norm4_gain = jnp.clip(1.0 + 0.1 * jax.random.normal(key_of[20], (D,), jnp.float32), 0.5, 1.5).astype(jnp.bfloat16)
    norm4_bias = noise(key_of[21], (D,), 0.3, 1.796875, ((0, 4),))
    d_token = noise(key_of[22], (BATCH, SEQ, D), 1.0, 6.0, ((0, 4), (1, 8)))
    d_char = noise(key_of[23], (BATCH, SEQ, D), 1.0, 6.0, ((0, 4), (1, 8)))
    return dict(tokens=tokens, chars=chars, segment=segment, char_end=char_end, w_qkv=w_qkv, w_out=w_out, norm1_gain=norm1_gain, norm1_bias=norm1_bias, w_up=w_up, b_up=b_up, w_down=w_down, norm2_gain=norm2_gain, norm2_bias=norm2_bias, w_gru=w_gru, b_gate=b_gate, w_ftok=w_ftok, w_fchr=w_fchr, w_conv=w_conv, norm3_gain=norm3_gain, norm3_bias=norm3_bias, norm4_gain=norm4_gain, norm4_bias=norm4_bias, d_token=d_token, d_char=d_char)


HIGH = lax.Precision.HIGHEST
EPSILON = 1e-05

@jax.custom_vjp
def low(v):
    return lax.optimization_barrier(v.astype(jnp.bfloat16)).astype(jnp.float32)

@jax.custom_vjp
def low_back(v):
    return v

def low_keep(v):
    return (low(v), None)

def low_pass(kept, grad):
    return (grad,)

def back_keep(v):
    return (v, None)

def back_low(kept, grad):
    return (low(grad),)
low.defvjp(low_keep, low_pass)
low_back.defvjp(back_keep, back_low)

def matmul(left, right):
    return jnp.dot(left, right, precision=HIGH)

def layer_norm(value, gain, shift):
    center = value - lax.optimization_barrier(jnp.mean(value, axis=-1, keepdims=True))
    inverse = lax.rsqrt(lax.optimization_barrier(jnp.mean(center * center, axis=-1, keepdims=True)) + EPSILON)
    return center * inverse * gain + shift

def chain(first, second):
    return (first[0] * second[0], second[0] * first[1] + second[1])

def attention(queries, keys_all, values_all, segment):
    scale = HEAD_DIM ** (-0.5)
    blocks = SEQ // TOK_DEV

    def one_block(item):
        query_block, seg_block = item
        scores = low_back(jnp.einsum('qhd,khd->hqk', query_block, keys_all, precision=HIGH) * scale)
        same = (seg_block[:, None] == segment[None, :])[None, :, :]
        expvals = jnp.where(same, jnp.exp(scores), 0.0)
        total = lax.optimization_barrier(jnp.sum(expvals, axis=-1))
        numer = low_back(jnp.einsum('hqk,khd->qhd', low(expvals), values_all, precision=HIGH))
        return numer / jnp.transpose(total)[:, :, None]
    result = lax.map(jax.checkpoint(one_block), (queries.reshape(blocks, TOK_DEV, HEADS, HEAD_DIM), segment.reshape(blocks, TOK_DEV)))
    return result.reshape(SEQ, D)

def layer(tokens, chars, params, segment, glob_end, tok_start, char_first, char_last):
    w_qkv, w_out, norm1_gain, norm1_bias, w_up, b_up, w_down, norm2_gain, norm2_bias, w_gru, b_gate, w_ftok, w_fchr, w_conv, norm3_gain, norm3_bias, norm4_gain, norm4_bias = params
    gate_in = low_back(matmul(low(chars), w_gru))
    fwd_gate = jax.nn.sigmoid(gate_in[:, :GRU_H] + b_gate[:GRU_H])
    fwd_decay = fwd_gate * (1.0 - char_first)[:, None]
    fwd_drive = (1.0 - fwd_gate) * jnp.tanh(gate_in[:, GRU_H:2 * GRU_H])
    fwd_state = lax.associative_scan(chain, (fwd_decay, fwd_drive))[1]
    bwd_gate = jax.nn.sigmoid(gate_in[:, 2 * GRU_H:3 * GRU_H] + b_gate[GRU_H:])
    bwd_decay = bwd_gate * (1.0 - char_last)[:, None]
    bwd_drive = (1.0 - bwd_gate) * jnp.tanh(gate_in[:, 3 * GRU_H:])
    bwd_state = lax.associative_scan(chain, (bwd_decay[::-1], bwd_drive[::-1]))[1][::-1]
    char_tok = jnp.concatenate([fwd_state[glob_end], bwd_state[tok_start]], axis=1)
    qkv = low(low_back(matmul(low(tokens), w_qkv)))
    heads = qkv.reshape(SEQ, 3, HEADS, HEAD_DIM)
    context = attention(heads[:, 0], heads[:, 1], heads[:, 2], segment)
    attn = low_back(matmul(low(context), w_out))
    hidden1 = layer_norm(tokens + attn, norm1_gain, norm1_bias)
    pre = low_back(matmul(low(hidden1), w_up)) + b_up
    inner = low(jax.nn.gelu(pre, approximate=False))
    ffn = low_back(matmul(inner, w_down))
    hidden2 = layer_norm(hidden1 + ffn, norm2_gain, norm2_bias)
    joined = low(low_back(jnp.concatenate([matmul(low(hidden2), w_ftok), matmul(low(char_tok), w_fchr)], axis=1)))
    padded = jnp.pad(joined, ((1, 1), (0, 0)))
    conv = low_back(matmul(padded[:-2], w_conv[0]) + matmul(padded[1:-1], w_conv[1]) + matmul(padded[2:], w_conv[2]))
    token_out = layer_norm(hidden2 + conv[:, :D], norm3_gain, norm3_bias)
    char_out = layer_norm(char_tok + conv[:, D:], norm4_gain, norm4_bias)
    return (token_out, char_out)

def reference(tokens, chars, segment, char_end, w_qkv, w_out, norm1_gain, norm1_bias, w_up, b_up, w_down, norm2_gain, norm2_bias, w_gru, b_gate, w_ftok, w_fchr, w_conv, norm3_gain, norm3_bias, norm4_gain, norm4_bias, d_token, d_char):
    params = tuple((weight.astype(jnp.float32) for weight in (w_qkv, w_out, norm1_gain, norm1_bias, w_up, b_up, w_down, norm2_gain, norm2_bias, w_gru, b_gate, w_ftok, w_fchr, w_conv, norm3_gain, norm3_bias, norm4_gain, norm4_bias)))
    block_id = (jnp.arange(SEQ, dtype=jnp.int32) // TOK_DEV).astype(jnp.int32)

    def one_sequence(totals, item):
        tok_row, chr_row, seg_row, end_row, dtok_row, dchr_row = item
        glob_end = (end_row + block_id * CH_DEV).astype(jnp.int32)
        tok_start = jnp.concatenate([jnp.zeros((1,), jnp.int32), (glob_end[:-1] + 1).astype(jnp.int32)])
        change = seg_row[1:] != seg_row[:-1]
        seg_first = jnp.concatenate([jnp.ones((1,), bool), change]).astype(jnp.float32)
        seg_last = jnp.concatenate([change, jnp.ones((1,), bool)]).astype(jnp.float32)
        char_first = jnp.zeros((CHARS,), jnp.float32).at[tok_start].set(seg_first)
        char_last = jnp.zeros((CHARS,), jnp.float32).at[glob_end].set(seg_last)

        def forward(tok_val, chr_val, *weights):
            return layer(tok_val, chr_val, weights, seg_row, glob_end, tok_start, char_first, char_last)
        outs, pull = jax.vjp(forward, tok_row.astype(jnp.float32), chr_row.astype(jnp.float32), *params)
        grads = pull((dtok_row.astype(jnp.float32), dchr_row.astype(jnp.float32)))
        totals = tuple((running + grad for running, grad in zip(totals, grads[2:])))
        return (totals, (outs[0].astype(jnp.bfloat16), outs[1].astype(jnp.bfloat16), grads[0].astype(jnp.bfloat16), grads[1].astype(jnp.bfloat16)))
    zeros = tuple((jnp.zeros_like(weight) for weight in params))
    totals, results = lax.scan(one_sequence, zeros, (tokens, chars, segment, char_end, d_token, d_char))
    return (results[0], results[1], results[2], results[3], totals[0], totals[1], totals[2], totals[3], totals[4], totals[5], totals[6], totals[7], totals[8], totals[9], totals[10], totals[11], totals[12], totals[13], totals[14], totals[15], totals[16], totals[17])
```

```python
import functools

import jax
import jax.numpy as jnp
from jax import lax
from jax.experimental import pallas as pl
from jax.experimental.pallas import tpu as pltpu
from jax.sharding import PartitionSpec as P

HEADS = 12
HEAD_DIM = 64
GRU_H = 384
EPSILON = 1e-05
BLOCK_LIMIT = 1024
FAR = 1e9
VMEM_BYTES = 40 * 1024 * 1024

F32 = jnp.float32
BF16 = jnp.bfloat16


def matmul(left, right):
    return jnp.dot(left, right, preferred_element_type=F32)


def matmul_nt(left, right):
    return lax.dot_general(left, right, (((1,), (1,)), ((), ())), preferred_element_type=F32)


def matmul_tn(left, right):
    return lax.dot_general(left, right, (((0,), (0,)), ((), ())), preferred_element_type=F32)


def layer_norm(value, gain, shift):
    center = value - jnp.mean(value, axis=-1, keepdims=True)
    inverse = lax.rsqrt(jnp.mean(center * center, axis=-1, keepdims=True) + EPSILON)
    normed = center * inverse
    return normed * gain + shift, (normed, inverse)


def layer_norm_back(grad, gain, kept):
    normed, inverse = kept
    scaled = grad * gain
    into = inverse * (
        scaled
        - jnp.mean(scaled, axis=-1, keepdims=True)
        - normed * jnp.mean(scaled * normed, axis=-1, keepdims=True)
    )
    return into, jnp.sum(grad * normed, axis=0), jnp.sum(grad, axis=0)


def params(**more):
    return pltpu.CompilerParams(vmem_limit_bytes=VMEM_BYTES, **more)


def cost(flops, moved, transcendentals=0):
    return pl.CostEstimate(
        flops=int(flops), bytes_accessed=int(moved), transcendentals=int(transcendentals)
    )


def two_parts(value):
    high = value.astype(BF16)
    return high, (value - high.astype(F32)).astype(BF16)


def shift_rows(value, by, fill, up):
    rows = value.shape[0]
    row = lax.broadcasted_iota(jnp.int32, value.shape, 0)
    if up:
        return jnp.where(row < rows - by, pltpu.roll(value, rows - by, 0), fill)
    return jnp.where(row >= by, pltpu.roll(value, by, 0), fill)


def scan_rows(decay, drive, up):
    by = 1
    while by < decay.shape[0]:
        drive = drive + decay * shift_rows(drive, by, 0.0, up)
        decay = decay * shift_rows(decay, by, 1.0, up)
        by = by * 2
    return decay, drive


def gru_forward_kernel(
    real, chars_ref, w_ref, bias_ref, start_ref, first_ref, end_ref, last_ref,
    gate_ref, cand_ref, decay_ref, cum_ref, state_ref,
):
    columns = matmul(chars_ref[0], w_ref[...])
    rows = columns.shape[0]
    tokens = start_ref.shape[2]
    place = lax.broadcasted_iota(jnp.int32, (rows, tokens), 0)
    inside = lax.broadcasted_iota(jnp.int32, (rows, GRU_H), 0) < real
    resets = [
        jnp.sum(jnp.where(place == at[0], flag[0], 0.0), axis=1, keepdims=True)
        for at, flag in ((start_ref, first_ref), (end_ref, last_ref))
    ]
    for side in (0, 1):
        cols = pl.ds(side * GRU_H, GRU_H)
        base = 2 * side * GRU_H
        gate = jax.nn.sigmoid(columns[:, base : base + GRU_H] + bias_ref[:, cols])
        cand = jnp.tanh(columns[:, base + GRU_H : base + 2 * GRU_H])
        decay = jnp.where(inside, gate * (1.0 - resets[side]), 1.0)
        drive = jnp.where(inside, (1.0 - gate) * cand, 0.0)
        gate_ref[0, :, cols] = gate
        cand_ref[0, :, cols] = cand
        decay_ref[0, :, cols] = decay
        cum, state = scan_rows(decay, drive, side == 1)
        cum_ref[0, :, cols] = cum
        state_ref[0, :, cols] = state


def char_tok_kernel(state_ref, cum_ref, enter_ref, end_ref, start_ref, out_ref):
    state = state_ref[0] + cum_ref[0] * enter_ref[0]
    high, low = two_parts(state)
    tokens = end_ref.shape[1]
    place = lax.broadcasted_iota(jnp.int32, (tokens, state.shape[0]), 1)
    for side, at in ((0, end_ref), (1, start_ref)):
        pick = jnp.where(place == at[0], 1.0, 0.0).astype(BF16)
        cols = slice(side * GRU_H, (side + 1) * GRU_H)
        out_ref[0, :, pl.ds(side * GRU_H, GRU_H)] = matmul(pick, high[:, cols]) + matmul(
            pick, low[:, cols]
        )


def gru_back_kernel(grad_ref, decay_ref, end_ref, start_ref, spread_ref, cum_ref, carried_ref):
    rows = decay_ref.shape[1]
    tokens = end_ref.shape[2]
    place = lax.broadcasted_iota(jnp.int32, (rows, tokens), 0)
    high, low = two_parts(grad_ref[0])
    for side, at in ((0, end_ref), (1, start_ref)):
        put = jnp.where(place == at[0], 1.0, 0.0).astype(BF16)
        cols = slice(side * GRU_H, (side + 1) * GRU_H)
        there = pl.ds(side * GRU_H, GRU_H)
        spread = matmul(put, high[:, cols]) + matmul(put, low[:, cols])
        decay = decay_ref[0, :, there]
        cum, carried = scan_rows(decay, decay * spread, side == 0)
        spread_ref[0, :, there] = spread
        cum_ref[0, :, there] = cum
        carried_ref[0, :, there] = carried


def gru_grad_kernel(
    real, gate_ref, cand_ref, decay_ref, cum_ref, state_ref, enter_ref,
    spread_ref, back_cum_ref, carried_ref, back_enter_ref, out_ref, bias_ref,
):
    rows = gate_ref.shape[1]
    inside = lax.broadcasted_iota(jnp.int32, (rows, GRU_H), 0) < real
    for side in (0, 1):
        there = pl.ds(side * GRU_H, GRU_H)
        gate = gate_ref[0, :, there]
        cand = cand_ref[0, :, there]
        decay = decay_ref[0, :, there]
        enter = enter_ref[0, :, there]
        back_enter = back_enter_ref[0, :, there]
        state = state_ref[0, :, there] + cum_ref[0, :, there] * enter
        carried = carried_ref[0, :, there] + back_cum_ref[0, :, there] * back_enter
        previous = shift_rows(state, 1, enter, side == 1)
        adjoint = spread_ref[0, :, there] + shift_rows(carried, 1, back_enter, side == 0)
        adjoint = jnp.where(inside, adjoint, 0.0)
        rest = adjoint * (1.0 - gate)
        to_gate = rest * (previous * decay - cand * gate)
        to_cand = rest * (1.0 - cand * cand)
        out_ref[0, :, pl.ds(2 * side * GRU_H, GRU_H)] = to_gate.astype(BF16)
        out_ref[0, :, pl.ds((2 * side + 1) * GRU_H, GRU_H)] = to_cand.astype(BF16)
        bias_ref[0, :, there] = jnp.sum(to_gate, axis=0, keepdims=True)


def per_sequence(*tail):
    return pl.BlockSpec((1,) + tail, lambda s: (s,) + (0,) * len(tail))


def whole_block(*shape):
    return pl.BlockSpec(shape, lambda s: (0,) * len(shape))


def gru_forward(chars, w_gru, bias, start, first, end, last, real):
    batch, rows, width = chars.shape
    tokens = start.shape[2]
    two = 2 * GRU_H
    kept = jax.ShapeDtypeStruct((batch, rows, two), F32)
    return pl.pallas_call(
        functools.partial(gru_forward_kernel, real),
        grid=(batch,),
        in_specs=[per_sequence(rows, width), whole_block(width, 2 * two), whole_block(1, two)]
        + [per_sequence(1, tokens)] * 4,
        out_specs=[per_sequence(rows, two)] * 5,
        out_shape=[kept] * 5,
        compiler_params=params(),
        cost_estimate=cost(
            2 * batch * rows * width * 2 * two,
            chars.size * 2 + w_gru.size * 2 + 20 * batch * rows * two,
            2 * batch * rows * two,
        ),
        name="gru_forward",
    )(chars, w_gru, bias, start, first, end, last)


def gather_states(state, cum, enter, end, start):
    batch, rows, two = state.shape
    tokens = end.shape[1]
    return pl.pallas_call(
        char_tok_kernel,
        grid=(batch,),
        in_specs=[per_sequence(rows, two)] * 2
        + [per_sequence(1, two)]
        + [per_sequence(tokens, 1)] * 2,
        out_specs=per_sequence(tokens, two),
        out_shape=jax.ShapeDtypeStruct((batch, tokens, two), F32),
        compiler_params=params(),
        cost_estimate=cost(
            4 * batch * rows * tokens * two, 8 * batch * rows * two + 4 * batch * tokens * two
        ),
        name="gather_states",
    )(state, cum, enter, end, start)


def gru_back(grad, decay, end, start):
    batch, rows, two = decay.shape
    tokens = end.shape[2]
    kept = jax.ShapeDtypeStruct((batch, rows, two), F32)
    return pl.pallas_call(
        gru_back_kernel,
        grid=(batch,),
        in_specs=[per_sequence(tokens, two), per_sequence(rows, two)]
        + [per_sequence(1, tokens)] * 2,
        out_specs=[per_sequence(rows, two)] * 3,
        out_shape=[kept] * 3,
        compiler_params=params(),
        cost_estimate=cost(
            4 * batch * rows * tokens * two, 16 * batch * rows * two + 4 * batch * tokens * two
        ),
        name="gru_back",
    )(grad, decay, end, start)


def gru_grad(gate, cand, decay, cum, state, enter, spread, back_cum, carried, back_enter, real):
    batch, rows, two = decay.shape
    big = per_sequence(rows, two)
    row = per_sequence(1, two)
    return pl.pallas_call(
        functools.partial(gru_grad_kernel, real),
        grid=(batch,),
        in_specs=[big] * 5 + [row] + [big] * 3 + [row],
        out_specs=[per_sequence(rows, 2 * two), row],
        out_shape=[
            jax.ShapeDtypeStruct((batch, rows, 2 * two), BF16),
            jax.ShapeDtypeStruct((batch, 1, two), F32),
        ],
        compiler_params=params(),
        cost_estimate=cost(20 * batch * rows * two, 36 * batch * rows * two),
        name="gru_grad",
    )(gate, cand, decay, cum, state, enter, spread, back_cum, carried, back_enter)


def combine_entering(decays, drives, backward):
    count, mine = lax.axis_size("ctx"), lax.axis_index("ctx")
    if backward:
        decays, drives, mine = decays[::-1], drives[::-1], count - 1 - mine
    if count <= 16:
        total = jnp.zeros_like(drives[0])
        for position in range(count - 1):
            total = jnp.where(
                position < mine, decays[position] * total + drives[position], total
            )
        return total

    def hop(position, total):
        return jnp.where(position < mine, decays[position] * total + drives[position], total)

    return lax.fori_loop(0, count - 1, hop, jnp.zeros_like(drives[0]))


def entering_states(decays, drives, flip):
    left = combine_entering(decays[:, :, :GRU_H], drives[:, :, :GRU_H], flip)
    right = combine_entering(decays[:, :, GRU_H:], drives[:, :, GRU_H:], not flip)
    return jnp.concatenate([left, right], axis=-1)[:, None, :]


def project_kernel(groups, part, tok_ref, w_ref, seg_ref, out_ref):
    qkv = matmul(tok_ref[0], w_ref[...]).astype(BF16)
    rows, width = tok_ref.shape[1], tok_ref.shape[2]
    lane = lax.broadcasted_iota(jnp.int32, (rows, HEAD_DIM), 1)
    marks = jnp.where(lane == seg_ref[0], 1.0, 0.0).astype(BF16)
    for group in range(groups):
        pieces = [
            qkv[:, kind * width + group * part : kind * width + (group + 1) * part]
            for kind in range(3)
        ]
        out_ref[group] = jnp.concatenate(pieces + [marks], axis=1)


def attend_kernel(heads, all_ref, query_ref, edge_ref, out_ref, kept_ref, key_scr, value_scr):
    part = heads * HEAD_DIM
    rows = query_ref.shape[0]

    @pl.when(pl.program_id(0) == 0)
    def build():
        marks = all_ref[:, 3 * part :]
        blocked = ((marks.astype(F32) - 1.0) * FAR).astype(BF16)
        ones = jnp.ones_like(marks)
        for head in range(heads):
            at = head * HEAD_DIM
            key_scr[head] = jnp.concatenate(
                [all_ref[:, part + at : part + at + HEAD_DIM], blocked], axis=1
            )
            value_scr[head] = jnp.concatenate(
                [all_ref[:, 2 * part + at : 2 * part + at + HEAD_DIM], ones], axis=1
            )

    marks = query_ref[:, 3 * part :]
    outs = []
    for head in range(heads):
        at = head * HEAD_DIM
        query = query_ref[:, at : at + HEAD_DIM] * jnp.asarray(HEAD_DIM ** (-0.5), BF16)
        query = jnp.concatenate([query, marks], axis=1)
        expvals = jnp.exp(matmul_nt(query, key_scr[head]))
        both = matmul(expvals.astype(BF16), value_scr[head])
        total = both[:, HEAD_DIM:]
        context = both[:, :HEAD_DIM] / total
        kept_ref[:, pl.ds(head * 2 * HEAD_DIM, 2 * HEAD_DIM)] = jnp.concatenate(
            [context, total], axis=1
        )
        outs.append(context.astype(BF16))
    outs.append(jnp.concatenate([edge_ref[...]] * (rows // edge_ref.shape[0]), axis=0))
    out_ref[...] = jnp.concatenate(outs, axis=1)


def attend_back_kernel(
    heads, all_ref, kept_ref, grad_ref, out_ref, query_scr, key_scr, value_scr, grad_scr
):
    part = heads * HEAD_DIM
    rows = out_ref.shape[0]
    step = pl.program_id(0)

    @pl.when(step == 0)
    def build():
        marks = all_ref[:, 3 * part :]
        blocked = ((marks.astype(F32) - 1.0) * FAR).astype(BF16)
        lane = lax.broadcasted_iota(jnp.int32, marks.shape, 1)
        pair = jnp.where(lane < 2, 1.0, 0.0).astype(BF16)
        for head in range(heads):
            at = head * HEAD_DIM
            query = all_ref[:, at : at + HEAD_DIM] * jnp.asarray(HEAD_DIM ** (-0.5), BF16)
            query_scr[head] = jnp.concatenate([query, marks], axis=1)
            key_scr[head] = jnp.concatenate(
                [all_ref[:, part + at : part + at + HEAD_DIM], blocked], axis=1
            )
            value_scr[head] = jnp.concatenate(
                [all_ref[:, 2 * part + at : 2 * part + at + HEAD_DIM], pair], axis=1
            )
            context = kept_ref[:, 2 * at : 2 * at + HEAD_DIM]
            total = kept_ref[:, 2 * at + HEAD_DIM : 2 * at + 2 * HEAD_DIM]
            grad = grad_ref[:, at : at + HEAD_DIM].astype(F32) / total
            delta = jnp.sum(grad * context, axis=1, keepdims=True)
            high, low = two_parts(-delta)
            extra = jnp.where(
                lane == 0, high.astype(F32), jnp.where(lane == 1, low.astype(F32), 0.0)
            )
            grad_scr[head] = jnp.concatenate([grad, extra], axis=1).astype(BF16)

    here = pl.ds(pl.multiple_of(step * rows, rows), rows)
    scale = HEAD_DIM ** (-0.5)
    d_query, d_key, d_value = [], [], []
    for head in range(heads):
        expvals = jnp.exp(matmul_nt(query_scr[head, here], key_scr[head]))
        inner = matmul_nt(grad_scr[head, here], value_scr[head])
        d_scores = (expvals * inner).astype(BF16)
        d_query.append((matmul(d_scores, key_scr[head])[:, :HEAD_DIM] * scale).astype(BF16))
        expvals = jnp.exp(matmul_nt(key_scr[head, here], query_scr[head]))
        inner = matmul_nt(value_scr[head, here], grad_scr[head])
        d_scores = (expvals * inner).astype(BF16)
        d_key.append(matmul(d_scores, query_scr[head])[:, :HEAD_DIM].astype(BF16))
        d_value.append(
            matmul(expvals.astype(BF16), grad_scr[head])[:, :HEAD_DIM].astype(BF16)
        )
    pad = jnp.zeros((rows, HEAD_DIM), BF16)
    out_ref[...] = jnp.concatenate(d_query + d_key + d_value + [pad], axis=1)


def unpack_kernel(groups, part, kinds, in_ref, out_ref):
    pieces = [
        in_ref[group, :, kind * part : (kind + 1) * part]
        for kind in range(kinds)
        for group in range(groups)
    ]
    out_ref[...] = jnp.concatenate(pieces, axis=1)


def send_grad_kernel(groups, part, grad_ref, w_ref, edge_ref, out_ref):
    d_context = matmul_nt(grad_ref[...], w_ref[...]).astype(BF16)
    for group in range(groups):
        out_ref[group] = jnp.concatenate(
            [d_context[:, group * part : (group + 1) * part], edge_ref[...]], axis=1
        )


def heads_here(batch, count):
    if batch * HEADS % count != 0:
        return 0
    heads = batch * HEADS // count
    if heads > HEADS or HEADS % heads != 0 or heads % 2 == 0:
        return 0
    return heads


def edges_block(pieces, rows):
    flat = jnp.concatenate([half.reshape(-1) for piece in pieces for half in two_parts(piece)])
    block = flat.reshape(-1, HEAD_DIM)
    return jnp.pad(block, ((0, rows - block.shape[0]), (0, 0)))


def edges_from(block, shapes):
    count = block.shape[0]
    flat = block.reshape(count, -1).astype(F32)
    out, at = [], 0
    for shape in shapes:
        size = 1
        for extent in shape:
            size = size * extent
        high = flat[:, at : at + size]
        low = flat[:, at + size : at + 2 * size]
        out.append((high + low).reshape((count,) + shape))
        at = at + 2 * size
    return out


def project_and_pack(tokens, w_qkv, segment, heads):
    batch, rows, width = tokens.shape
    groups, part = HEADS // heads, heads * HEAD_DIM
    wide = 3 * part + HEAD_DIM
    return pl.pallas_call(
        functools.partial(project_kernel, groups, part),
        grid=(batch,),
        in_specs=[
            per_sequence(rows, width),
            whole_block(width, 3 * width),
            per_sequence(rows, 1),
        ],
        out_specs=pl.BlockSpec((groups, rows, wide), lambda s: (s, 0, 0)),
        out_shape=jax.ShapeDtypeStruct((batch * groups, rows, wide), BF16),
        compiler_params=params(),
        cost_estimate=cost(
            6 * batch * rows * width * width,
            tokens.size * 2 + w_qkv.size * 2 + 2 * batch * groups * rows * wide,
        ),
        name="project",
    )(tokens, w_qkv, segment[:, :, None])


def attend(everything, edges, heads):
    length, wide = everything.shape
    block = 256
    part = heads * HEAD_DIM
    out_wide = part + HEAD_DIM
    return pl.pallas_call(
        functools.partial(attend_kernel, heads),
        grid=(length // block,),
        in_specs=[
            pl.BlockSpec((length, wide), lambda i: (0, 0)),
            pl.BlockSpec((block, wide), lambda i: (i, 0)),
            pl.BlockSpec(edges.shape, lambda i: (0, 0)),
        ],
        out_specs=[
            pl.BlockSpec((block, out_wide), lambda i: (i, 0)),
            pl.BlockSpec((block, 2 * part), lambda i: (i, 0)),
        ],
        out_shape=[
            jax.ShapeDtypeStruct((length, out_wide), BF16),
            jax.ShapeDtypeStruct((length, 2 * part), F32),
        ],
        scratch_shapes=[
            pltpu.VMEM((heads, length, 2 * HEAD_DIM), BF16),
            pltpu.VMEM((heads, length, 2 * HEAD_DIM), BF16),
        ],
        compiler_params=params(),
        cost_estimate=cost(
            8 * heads * length * length * HEAD_DIM,
            length * (wide * 2 + out_wide * 2 + 8 * part),
            heads * length * length,
        ),
        name="attend",
    )(everything, everything, edges)


def attend_back(everything, kept, grads, heads):
    length, wide = everything.shape
    block = 256
    part = heads * HEAD_DIM
    scratch = pltpu.VMEM((heads, length, 2 * HEAD_DIM), BF16)
    return pl.pallas_call(
        functools.partial(attend_back_kernel, heads),
        grid=(length // block,),
        in_specs=[
            pl.BlockSpec((length, wide), lambda i: (0, 0)),
            pl.BlockSpec((length, 2 * part), lambda i: (0, 0)),
            pl.BlockSpec((length, part + HEAD_DIM), lambda i: (0, 0)),
        ],
        out_specs=pl.BlockSpec((block, wide), lambda i: (i, 0)),
        out_shape=jax.ShapeDtypeStruct((length, wide), BF16),
        scratch_shapes=[scratch] * 4,
        compiler_params=params(),
        cost_estimate=cost(
            28 * heads * length * length * HEAD_DIM,
            length * (wide * 4 + 8 * part + 2 * part),
            2 * heads * length * length,
        ),
        name="attend_back",
    )(everything, kept, grads)


def unpack(received, heads, kinds, batch):
    count, rows, wide = received.shape
    groups, part = HEADS // heads, heads * HEAD_DIM
    width = kinds * groups * part
    return pl.pallas_call(
        functools.partial(unpack_kernel, groups, part, kinds),
        grid=(batch,),
        in_specs=[pl.BlockSpec((groups, rows, wide), lambda s: (s, 0, 0))],
        out_specs=pl.BlockSpec((rows, width), lambda s: (s, 0)),
        out_shape=jax.ShapeDtypeStruct((batch * rows, width), BF16),
        compiler_params=params(),
        cost_estimate=cost(0, 2 * received.size + 2 * batch * rows * width),
        name="unpack",
    )(received)


def send_grad(d_attn, w_out, edges, heads, batch):
    total, width = d_attn.shape
    rows = total // batch
    groups, part = HEADS // heads, heads * HEAD_DIM
    wide = part + HEAD_DIM
    return pl.pallas_call(
        functools.partial(send_grad_kernel, groups, part),
        grid=(batch,),
        in_specs=[
            pl.BlockSpec((rows, width), lambda s: (s, 0)),
            whole_block(width, width),
            whole_block(rows, HEAD_DIM),
        ],
        out_specs=pl.BlockSpec((groups, rows, wide), lambda s: (s, 0, 0)),
        out_shape=jax.ShapeDtypeStruct((batch * groups, rows, wide), BF16),
        compiler_params=params(),
        cost_estimate=cost(
            2 * total * width * width, 2 * (d_attn.size + w_out.size + total * groups * wide)
        ),
        name="send_grad",
    )(d_attn, w_out, edges)


def block_size(rows):
    size = min(rows, BLOCK_LIMIT)
    while rows % size != 0:
        size = size - 1
    return size


def split_blocks(array, size):
    return array.reshape((array.shape[0] // size, size) + array.shape[1:])


def to_heads(matrix):
    return matrix.reshape(matrix.shape[0], HEADS, HEAD_DIM)


def masked_exp(query_heads, key_heads, query_seg, key_seg):
    scores = jnp.einsum(
        "qhd,khd->hqk", query_heads, key_heads, preferred_element_type=F32
    ) * HEAD_DIM ** (-0.5)
    same = (query_seg[:, None] == key_seg[None, :])[None, :, :]
    return jnp.where(same, jnp.exp(scores), 0.0)


def everyone(rows):
    return lax.all_gather(rows, "ctx", axis=0, tiled=True)


def gathered_attention(qkv, seg_row):
    tok_rows, width = qkv.shape[0], qkv.shape[1] // 3
    query_heads = to_heads(qkv[:, :width])
    pieces = (everyone(qkv[:, width : 2 * width]), everyone(qkv[:, 2 * width :]), everyone(seg_row))
    size = block_size(pieces[0].shape[0])

    def step(acc, item):
        key_block, value_block, seg_block = item
        expvals = masked_exp(query_heads, to_heads(key_block), seg_row, seg_block)
        part_num = jnp.einsum(
            "hqk,khd->qhd", expvals.astype(BF16), to_heads(value_block),
            preferred_element_type=F32,
        )
        return ((acc[0] + part_num, acc[1] + jnp.transpose(jnp.sum(expvals, axis=-1))), None)

    (numer, total), unused = lax.scan(
        step,
        (jnp.zeros((tok_rows, HEADS, HEAD_DIM), F32), jnp.zeros((tok_rows, HEADS), F32)),
        tuple(split_blocks(piece, size) for piece in pieces),
    )
    return numer / total[:, :, None], total


def gathered_attention_back(qkv, seg_row, context, total, d_context):
    tok_rows, width = qkv.shape[0], qkv.shape[1] // 3
    scale = HEAD_DIM ** (-0.5)
    d_context = to_heads(d_context)
    query_rows, key_rows, value_rows = (qkv[:, i * width : (i + 1) * width] for i in range(3))
    grad_heads = (d_context / total[:, :, None]).astype(BF16)
    delta = jnp.sum(d_context * context, axis=-1) / total
    key_heads, value_heads, query_heads = (
        to_heads(key_rows), to_heads(value_rows), to_heads(query_rows)
    )
    zero_heads = jnp.zeros((tok_rows, HEADS, HEAD_DIM), F32)
    seg_all = everyone(seg_row)
    size = block_size(seg_all.shape[0])

    def key_step(acc, item):
        query_block, grad_block, delta_block, seg_block = item
        query_h, grad_h = to_heads(query_block), to_heads(grad_block)
        expvals = masked_exp(query_h, key_heads, seg_block, seg_row)
        dprob = jnp.einsum("qhd,khd->hqk", grad_h, value_heads, preferred_element_type=F32)
        dscore = (expvals * (dprob - jnp.transpose(delta_block)[:, :, None])).astype(BF16)
        dkey = acc[0] + scale * jnp.einsum(
            "hqk,qhd->khd", dscore, query_h, preferred_element_type=F32
        )
        dval = acc[1] + jnp.einsum(
            "hqk,qhd->khd", expvals.astype(BF16), grad_h, preferred_element_type=F32
        )
        return ((dkey, dval), None)

    (dkey, dval), unused = lax.scan(
        key_step,
        (zero_heads, zero_heads),
        tuple(
            split_blocks(piece, size)
            for piece in (
                everyone(query_rows),
                everyone(grad_heads.reshape(tok_rows, width)),
                everyone(delta),
                seg_all,
            )
        ),
    )

    def query_step(acc, item):
        key_block, value_block, seg_block = item
        key_h = to_heads(key_block)
        expvals = masked_exp(query_heads, key_h, seg_row, seg_block)
        dprob = jnp.einsum(
            "qhd,khd->hqk", grad_heads, to_heads(value_block), preferred_element_type=F32
        )
        dscore = (expvals * (dprob - jnp.transpose(delta)[:, :, None])).astype(BF16)
        return (
            acc + scale * jnp.einsum("hqk,khd->qhd", dscore, key_h, preferred_element_type=F32),
            None,
        )

    dquery, unused = lax.scan(
        query_step,
        zero_heads,
        tuple(
            split_blocks(piece, size)
            for piece in (everyone(key_rows), everyone(value_rows), seg_all)
        ),
    )
    return jnp.concatenate(
        [part.reshape(tok_rows, width) for part in (dquery, dkey, dval)], axis=1
    ).astype(BF16)


def neighbours(rows):
    count = lax.axis_size("ctx")
    up = [(i, i + 1) for i in range(count - 1)]
    down = [(j, i) for i, j in up]
    before = lax.ppermute(rows[:, -1], "ctx", up)
    after = lax.ppermute(rows[:, 0], "ctx", down)
    return before[:, None], after[:, None]


def shifted(rows):
    before, after = neighbours(rows)
    later = jnp.concatenate([before, rows[:, :-1]], axis=1)
    earlier = jnp.concatenate([rows[:, 1:], after], axis=1)
    return later, earlier


def sum_over_ctx(value):
    count, me = lax.axis_size("ctx"), lax.axis_index("ctx")
    rows = value.shape[0]
    if count != 8 or rows % (8 * count) != 0:
        return lax.psum(value.astype(F32), "ctx")
    steps = (1, 2, 4)
    piece = value
    for bit in steps:
        mine = (me // bit) % 2
        half = piece.shape[0] // 2
        send = lax.dynamic_slice_in_dim(piece, (1 - mine) * half, half, 0)
        keep = lax.dynamic_slice_in_dim(piece, mine * half, half, 0)
        got = lax.ppermute(send, "ctx", [(i, i ^ bit) for i in range(count)])
        piece = (keep.astype(F32) + got.astype(F32)).astype(BF16)
    for bit in reversed(steps):
        mine = (me // bit) % 2
        half = piece.shape[0]
        got = lax.ppermute(piece, "ctx", [(i, i ^ bit) for i in range(count)])
        both = jnp.zeros((2 * half,) + piece.shape[1:], BF16)
        both = lax.dynamic_update_slice_in_dim(both, piece, mine * half, 0)
        piece = lax.dynamic_update_slice_in_dim(both, got, (1 - mine) * half, 0)
    return piece.astype(F32)


def owned_sum(grads, axis=0):
    share = lax.psum_scatter(grads, "fsdp", scatter_dimension=axis, tiled=True)
    return sum_over_ctx(share.reshape(-1, share.shape[-1]))


def local(
    tokens, chars, segment, char_end, w_qkv, w_out, norm1_gain, norm1_bias, w_up, b_up, w_down,
    norm2_gain, norm2_bias, w_gru, b_gate, w_ftok, w_fchr, w_conv, norm3_gain, norm3_bias,
    norm4_gain, norm4_bias, d_token, d_char,
):
    count, me = lax.axis_size("ctx"), lax.axis_index("ctx")
    shards = lax.axis_size("fsdp")
    batch, rows, width = tokens.shape
    char_rows = chars.shape[1]
    total_rows = batch * rows
    heads = heads_here(batch, count)
    padded_rows = -(-char_rows // 8) * 8

    def gather(weight, axis=0):
        return lax.all_gather(weight, "fsdp", axis=axis, tiled=True)

    vectors = (
        norm1_gain, norm1_bias, norm2_gain, norm2_bias, b_gate, norm3_gain, norm3_bias,
        norm4_gain, norm4_bias, b_up,
    )
    packed = jnp.concatenate(vectors)[None, :]
    packed = lax.all_gather(packed, "fsdp", axis=0, tiled=True).astype(F32)
    share = norm1_gain.shape[0]
    (
        norm1_gain, norm1_bias, norm2_gain, norm2_bias, b_gate, norm3_gain, norm3_bias,
        norm4_gain, norm4_bias,
    ) = (packed[:, i * share : (i + 1) * share].reshape(1, -1) for i in range(9))
    b_up = packed[:, 9 * share :].reshape(1, -1)
    w_qkv = gather(w_qkv)
    w_gru = gather(w_gru)
    w_out = gather(w_out)
    w_up = gather(w_up)
    w_down = gather(w_down)
    w_ftok = gather(w_ftok)
    w_fchr = gather(w_fchr)
    w_conv = gather(w_conv, 1)

    start = jnp.concatenate([jnp.zeros((batch, 1), jnp.int32), char_end[:, :-1] + 1], axis=1)
    change = (segment[:, 1:] != segment[:, :-1]).astype(F32)
    first = jnp.concatenate([jnp.broadcast_to((me == 0).astype(F32), (batch, 1)), change], axis=1)
    last = jnp.concatenate(
        [change, jnp.broadcast_to((me == count - 1).astype(F32), (batch, 1))], axis=1
    )
    chars_pad = jnp.pad(chars, ((0, 0), (0, padded_rows - char_rows), (0, 0)))
    gate, cand, decay, cum, state = gru_forward(
        chars_pad, w_gru, b_gate, start[:, None], first[:, None], char_end[:, None],
        last[:, None], char_rows,
    )
    edge_decay = jnp.concatenate([cum[:, char_rows - 1, :GRU_H], cum[:, 0, GRU_H:]], axis=1)
    edge_state = jnp.concatenate([state[:, char_rows - 1, :GRU_H], state[:, 0, GRU_H:]], axis=1)

    flat_tokens = tokens.reshape(total_rows, width)
    if heads:
        sent = project_and_pack(tokens, w_qkv, segment, heads)
        everything = lax.all_to_all(sent, "ctx", 0, 0, tiled=True)
        everything = everything.reshape(count * rows, -1)
        edges = edges_block((edge_decay, edge_state), rows)
        packed_context, kept = attend(everything, edges, heads)
        received = lax.all_to_all(packed_context.reshape(count, rows, -1), "ctx", 0, 0, tiled=True)
        context_b = unpack(received, heads, 1, batch)
        decays, states = edges_from(
            received[:, :, heads * HEAD_DIM :], ((batch, 2 * GRU_H), (batch, 2 * GRU_H))
        )
    else:
        qkv = matmul(flat_tokens, w_qkv).astype(BF16).reshape(batch, rows, -1)
        results = [gathered_attention(qkv[i], segment[i]) for i in range(batch)]
        context_b = jnp.concatenate([r[0].reshape(rows, width) for r in results]).astype(BF16)
        both = lax.all_gather(jnp.stack([edge_decay, edge_state]), "ctx", axis=0)
        decays, states = both[:, 0], both[:, 1]
    enter = entering_states(decays, states, False)

    attn = matmul(context_b, w_out)
    hidden1, kept1 = layer_norm(flat_tokens.astype(F32) + attn, norm1_gain, norm1_bias)
    hidden1_b = hidden1.astype(BF16)
    pre = matmul(hidden1_b, w_up) + b_up
    inner_b = jax.nn.gelu(pre, approximate=False).astype(BF16)
    ffn = matmul(inner_b, w_down)
    hidden2, kept2 = layer_norm(hidden1 + ffn, norm2_gain, norm2_bias)
    hidden2_b = hidden2.astype(BF16)

    char_tok = gather_states(state, cum, enter, char_end[:, :, None], start[:, :, None])
    char_tok = char_tok.reshape(total_rows, width)
    char_tok_b = char_tok.astype(BF16)
    joined = jnp.concatenate(
        [matmul(hidden2_b, w_ftok), matmul(char_tok_b, w_fchr)], axis=1
    ).astype(BF16)

    two = 2 * width
    later, earlier = shifted(joined.reshape(batch, rows, two))
    taps = (later.reshape(total_rows, two), joined, earlier.reshape(total_rows, two))
    conv = matmul(taps[1], w_conv[1]) + matmul(taps[0], w_conv[0]) + matmul(taps[2], w_conv[2])
    token_out, kept3 = layer_norm(hidden2 + conv[:, :width], norm3_gain, norm3_bias)
    char_out, kept4 = layer_norm(char_tok + conv[:, width:], norm4_gain, norm4_bias)

    d_in3, gain3_grad, bias3_grad = layer_norm_back(
        d_token.reshape(total_rows, width).astype(F32), norm3_gain, kept3
    )
    d_in4, gain4_grad, bias4_grad = layer_norm_back(
        d_char.reshape(total_rows, width).astype(F32), norm4_gain, kept4
    )
    d_conv = jnp.concatenate([d_in3, d_in4], axis=1).astype(BF16)
    d_later, d_earlier = shifted(d_conv.reshape(batch, rows, two))
    d_joined = (
        matmul_nt(d_conv, w_conv[1])
        + matmul_nt(d_earlier.reshape(total_rows, two), w_conv[0])
        + matmul_nt(d_later.reshape(total_rows, two), w_conv[2])
    ).astype(BF16)
    conv_grad = jnp.stack([matmul_tn(tap, d_conv).astype(BF16) for tap in taps])
    conv_sum = owned_sum(conv_grad, 1)

    d_tok_part, d_chr_part = d_joined[:, :width], d_joined[:, width:]
    d_hidden2 = d_in3 + matmul_nt(d_tok_part, w_ftok)
    d_char_tok = d_in4 + matmul_nt(d_chr_part, w_fchr)
    ftok_grad = matmul_tn(hidden2_b, d_tok_part).astype(BF16)
    fchr_grad = matmul_tn(char_tok_b, d_chr_part).astype(BF16)

    end_line, start_line = char_end[:, None], start[:, None]
    spread, back_cum, carried = gru_back(
        d_char_tok.reshape(batch, rows, width), decay, end_line, start_line
    )
    edge_carried = jnp.concatenate(
        [carried[:, 0, :GRU_H], carried[:, char_rows - 1, GRU_H:]], axis=1
    )

    d_in2, gain2_grad, bias2_grad = layer_norm_back(d_hidden2, norm2_gain, kept2)
    d_ffn = d_in2.astype(BF16)
    down_grad = matmul_tn(inner_b, d_ffn).astype(BF16)
    second_sum = owned_sum(
        jnp.concatenate(
            [
                down_grad.reshape(shards, -1, width),
                ftok_grad.reshape(shards, -1, width),
                fchr_grad.reshape(shards, -1, width),
            ],
            axis=1,
        ).reshape(-1, width)
    )
    cdf = (1.0 + lax.erf(pre * (0.5**0.5))) * 0.5
    slope = cdf + pre * jnp.exp(-0.5 * pre * pre) * (0.5 / jnp.pi) ** 0.5
    d_pre = matmul_nt(d_ffn, w_down) * slope
    bup_grad = jnp.sum(d_pre, axis=0)
    d_pre_low = d_pre.astype(BF16)
    up_grad = matmul_tn(hidden1_b, d_pre_low).astype(BF16)
    d_hidden1 = d_in2 + matmul_nt(d_pre_low, w_up)
    d_in1, gain1_grad, bias1_grad = layer_norm_back(d_hidden1, norm1_gain, kept1)
    d_attn = d_in1.astype(BF16)
    wout_grad = matmul_tn(context_b, d_attn).astype(BF16)
    third_sum = owned_sum(jnp.concatenate([up_grad, wout_grad], axis=1))

    if heads:
        edges = edges_block((edge_carried,), rows)
        sent = send_grad(d_attn, w_out, edges, heads, batch)
        received = lax.all_to_all(sent, "ctx", 0, 0, tiled=True)
        (carries,) = edges_from(received[:, :, heads * HEAD_DIM :], ((batch, 2 * GRU_H),))
        packed_grad = attend_back(everything, kept, received.reshape(count * rows, -1), heads)
        returned = lax.all_to_all(packed_grad.reshape(count, rows, -1), "ctx", 0, 0, tiled=True)
        d_qkv = unpack(returned, heads, 3, batch)
    else:
        carries = lax.all_gather(edge_carried, "ctx", axis=0)
        d_context = matmul_nt(d_attn, w_out).reshape(batch, rows, width)
        d_qkv = jnp.concatenate(
            [
                gathered_attention_back(
                    qkv[i], segment[i], results[i][0], results[i][1], d_context[i]
                )
                for i in range(batch)
            ]
        )
    back_enter = entering_states(decays, carries, True)
    d_gate_in, bgate_grad = gru_grad(
        gate, cand, decay, cum, state, enter, spread, back_cum, carried, back_enter, char_rows
    )
    d_gate_in = d_gate_in.reshape(batch * padded_rows, -1)
    gru_weight_grad = matmul_tn(chars_pad.reshape(batch * padded_rows, width), d_gate_in)
    d_chars = matmul_nt(d_gate_in, w_gru).astype(BF16)
    d_chars = d_chars.reshape(batch, padded_rows, width)[:, :char_rows]

    qkv_grad = matmul_tn(flat_tokens, d_qkv).astype(BF16)
    d_tokens = (d_in1 + matmul_nt(d_qkv, w_qkv)).astype(BF16)

    small = jnp.stack(
        [
            gain1_grad, bias1_grad, gain2_grad, bias2_grad, jnp.sum(bgate_grad, axis=(0, 1)),
            gain3_grad, bias3_grad, gain4_grad, bias4_grad,
        ],
        axis=1,
    )
    up_small = bup_grad.reshape(shards, -1, width // shards)
    up_small = jnp.swapaxes(up_small, 1, 2).reshape(width, -1)
    small = jnp.concatenate([small, up_small], axis=1)
    small_count = small.shape[1]
    small = jnp.pad(small, ((0, 0), (0, 128 - small_count)))
    fourth_sum = owned_sum(
        jnp.concatenate([qkv_grad, gru_weight_grad.astype(BF16), small.astype(BF16)], axis=1)
    )

    wide_up, wide_qkv, wide_gru = w_up.shape[1], w_qkv.shape[1], w_gru.shape[1]
    own = width // shards
    own_down = w_down.shape[0] // shards
    vector = fourth_sum[:, wide_qkv + wide_gru :]
    return (
        token_out.astype(BF16).reshape(batch, rows, width),
        char_out.astype(BF16).reshape(batch, rows, width),
        d_tokens.reshape(batch, rows, width),
        d_chars,
        fourth_sum[:, :wide_qkv],
        third_sum[:, wide_up:],
        vector[:, 0],
        vector[:, 1],
        third_sum[:, :wide_up],
        jnp.swapaxes(vector[:, 9:small_count], 0, 1).reshape(-1),
        second_sum[:own_down],
        vector[:, 2],
        vector[:, 3],
        fourth_sum[:, wide_qkv : wide_qkv + wide_gru],
        vector[:, 4],
        second_sum[own_down : own_down + own],
        second_sum[own_down + own :],
        conv_sum.reshape(w_conv.shape[0], -1, two),
        vector[:, 5],
        vector[:, 6],
        vector[:, 7],
        vector[:, 8],
    )


def solution(mesh):
    rows = P("fsdp", "ctx", None)
    pairs = P("fsdp", "ctx")
    matrix = P("fsdp", None)
    vector = P("fsdp")
    weights = (
        matrix, matrix, vector, vector, matrix, vector, matrix, vector, vector, matrix, vector,
        matrix, matrix, P(None, "fsdp", None), vector, vector, vector, vector,
    )
    return jax.shard_map(
        local,
        mesh=mesh,
        in_specs=(rows, rows, pairs, pairs) + weights + (rows, rows),
        out_specs=(rows,) * 4 + weights,
        check_vma=False,
    )
```

```python
import functools

import jax
import jax.numpy as jnp
from jax import lax
from jax.experimental import pallas as pl
from jax.experimental.pallas import tpu as pltpu
from jax.sharding import PartitionSpec as P

HEADS = 12
HEAD_DIM = 64
GRU_H = 384
EPSILON = 1e-05
BLOCK_LIMIT = 1024
FAR = 1e9
VMEM_BYTES = 40 * 1024 * 1024

F32 = jnp.float32
BF16 = jnp.bfloat16


def matmul(left, right):
    return jnp.dot(left, right, preferred_element_type=F32)


def matmul_nt(left, right):
    return lax.dot_general(left, right, (((1,), (1,)), ((), ())), preferred_element_type=F32)


def matmul_tn(left, right):
    return lax.dot_general(left, right, (((0,), (0,)), ((), ())), preferred_element_type=F32)


def layer_norm(value, gain, shift):
    center = value - jnp.mean(value, axis=-1, keepdims=True)
    inverse = lax.rsqrt(jnp.mean(center * center, axis=-1, keepdims=True) + EPSILON)
    normed = center * inverse
    return normed * gain + shift, (normed, inverse)


def layer_norm_back(grad, gain, kept):
    normed, inverse = kept
    scaled = grad * gain
    into = inverse * (
        scaled
        - jnp.mean(scaled, axis=-1, keepdims=True)
        - normed * jnp.mean(scaled * normed, axis=-1, keepdims=True)
    )
    return into, jnp.sum(grad * normed, axis=0), jnp.sum(grad, axis=0)


def params(**more):
    return pltpu.CompilerParams(vmem_limit_bytes=VMEM_BYTES, **more)


def cost(flops, moved, transcendentals=0):
    return pl.CostEstimate(
        flops=int(flops), bytes_accessed=int(moved), transcendentals=int(transcendentals)
    )


def two_parts(value):
    high = value.astype(BF16)
    return high, (value - high.astype(F32)).astype(BF16)


KINDS = 4


def store_edges(edge_ref, cols, rows):
    parts = [half.astype(F32) for row in rows for half in two_parts(row)]
    parts = parts + [jnp.zeros_like(parts[0])] * (KINDS - len(parts))
    parts = jnp.concatenate(parts, axis=0)
    for sequence in range(edge_ref.shape[0] // KINDS):

        @pl.when(pl.program_id(0) == sequence)
        def store():
            edge_ref[pl.ds(sequence * KINDS, KINDS), cols] = parts


def edges_to_block(edges, rows):
    count = edges.shape[1] // HEAD_DIM
    pieces = [edges[:, i * HEAD_DIM : (i + 1) * HEAD_DIM] for i in range(count)]
    pieces.append(jnp.zeros((rows - count * edges.shape[0], HEAD_DIM), F32))
    return jnp.concatenate(pieces, axis=0).astype(BF16)


def edges_of_block(block):
    block = block.astype(F32)
    count = 2 * GRU_H // HEAD_DIM
    return jnp.concatenate([block[i * 8 : (i + 1) * 8] for i in range(count)], axis=1)


def entering_row(decays, drives, sequence, count, flip):
    me = lax.axis_index("ctx")
    halves = []
    for side in (0, 1):
        cols = slice(side * GRU_H, (side + 1) * GRU_H)
        total = jnp.zeros((1, GRU_H), F32)
        backward = (side == 1) != flip
        order = range(count - 1, 0, -1) if backward else range(count - 1)
        for other in order:
            decay, drive = decays(other, sequence, cols), drives(other, sequence, cols)
            there = me < other if backward else me > other
            total = jnp.where(there, decay * total + drive, total)
        halves.append(total)
    return jnp.concatenate(halves, axis=1)


def edge_reader(ref, kind):
    def read(other, sequence, cols):
        at = sequence * KINDS + 2 * kind
        return ref[other, at : at + 1, cols] + ref[other, at + 1 : at + 2, cols]

    return read


def shift_rows(value, by, fill, up):
    rows = value.shape[0]
    row = lax.broadcasted_iota(jnp.int32, value.shape, 0)
    if up:
        return jnp.where(row < rows - by, pltpu.roll(value, rows - by, 0), fill)
    return jnp.where(row >= by, pltpu.roll(value, by, 0), fill)


def scan_rows(decay, drive, up):
    by = 1
    while by < decay.shape[0]:
        drive = drive + decay * shift_rows(drive, by, 0.0, up)
        decay = decay * shift_rows(decay, by, 1.0, up)
        by = by * 2
    return decay, drive


def gru_forward_kernel(
    real, chars_ref, w_ref, bias_ref, start_ref, first_ref, end_ref, last_ref,
    gate_ref, cand_ref, decay_ref, cum_ref, state_ref, edge_ref,
):
    columns = matmul(chars_ref[0], w_ref[:, : 4 * GRU_H])
    rows = columns.shape[0]
    tokens = start_ref.shape[2]
    place = lax.broadcasted_iota(jnp.int32, (rows, tokens), 0)
    inside = lax.broadcasted_iota(jnp.int32, (rows, GRU_H), 0) < real
    resets = [
        jnp.sum(jnp.where(place == at[0], flag[0], 0.0), axis=1, keepdims=True)
        for at, flag in ((start_ref, first_ref), (end_ref, last_ref))
    ]
    for side in (0, 1):
        cols = pl.ds(side * GRU_H, GRU_H)
        base = 2 * side * GRU_H
        gate = jax.nn.sigmoid(columns[:, base : base + GRU_H] + bias_ref[:, cols])
        cand = jnp.tanh(columns[:, base + GRU_H : base + 2 * GRU_H])
        decay = jnp.where(inside, gate * (1.0 - resets[side]), 1.0)
        drive = jnp.where(inside, (1.0 - gate) * cand, 0.0)
        gate_ref[0, :, cols] = gate
        cand_ref[0, :, cols] = cand
        decay_ref[0, :, cols] = decay
        cum, state = scan_rows(decay, drive, side == 1)
        cum_ref[0, :, cols] = cum
        state_ref[0, :, cols] = state
        at = 0 if side else real - 1
        store_edges(edge_ref, cols, (cum[at : at + 1], state[at : at + 1]))


def char_tok_kernel(state_ref, cum_ref, edges_ref, end_ref, start_ref, out_ref, enter_ref):
    batch, tokens = end_ref.shape[:2]
    for sequence in range(batch):
        enter = entering_row(
            edge_reader(edges_ref, 0), edge_reader(edges_ref, 1), sequence, edges_ref.shape[0],
            False,
        )
        enter_ref[sequence] = enter
        state = state_ref[sequence] + cum_ref[sequence] * enter
        high, low = two_parts(state)
        place = lax.broadcasted_iota(jnp.int32, (tokens, state.shape[0]), 1)
        for side, at in ((0, end_ref), (1, start_ref)):
            pick = jnp.where(place == at[sequence], 1.0, 0.0).astype(BF16)
            cols = slice(side * GRU_H, (side + 1) * GRU_H)
            out_ref[pl.ds(sequence * tokens, tokens), pl.ds(side * GRU_H, GRU_H)] = matmul(
                pick, high[:, cols]
            ) + matmul(pick, low[:, cols])


def gru_back_kernel(
    real, grad_ref, decay_ref, end_ref, start_ref, spread_ref, cum_ref, carried_ref, edge_ref
):
    rows = decay_ref.shape[1]
    tokens = end_ref.shape[2]
    place = lax.broadcasted_iota(jnp.int32, (rows, tokens), 0)
    high, low = two_parts(grad_ref[0])
    for side, at in ((0, end_ref), (1, start_ref)):
        put = jnp.where(place == at[0], 1.0, 0.0).astype(BF16)
        cols = slice(side * GRU_H, (side + 1) * GRU_H)
        there = pl.ds(side * GRU_H, GRU_H)
        spread = matmul(put, high[:, cols]) + matmul(put, low[:, cols])
        decay = decay_ref[0, :, there]
        cum, carried = scan_rows(decay, decay * spread, side == 0)
        spread_ref[0, :, there] = spread
        cum_ref[0, :, there] = cum
        carried_ref[0, :, there] = carried
        at = real - 1 if side else 0
        store_edges(edge_ref, there, (carried[at : at + 1],))


def gru_grad_kernel(
    real, gate_ref, cand_ref, decay_ref, cum_ref, state_ref, enter_ref,
    spread_ref, back_cum_ref, carried_ref, back_enter_ref, out_ref, bias_ref,
):
    rows = gate_ref.shape[1]
    inside = lax.broadcasted_iota(jnp.int32, (rows, GRU_H), 0) < real
    for side in (0, 1):
        there = pl.ds(side * GRU_H, GRU_H)
        gate = gate_ref[0, :, there]
        cand = cand_ref[0, :, there]
        decay = decay_ref[0, :, there]
        enter = enter_ref[0, :, there]
        back_enter = back_enter_ref[0, :, there]
        state = state_ref[0, :, there] + cum_ref[0, :, there] * enter
        carried = carried_ref[0, :, there] + back_cum_ref[0, :, there] * back_enter
        previous = shift_rows(state, 1, enter, side == 1)
        adjoint = spread_ref[0, :, there] + shift_rows(carried, 1, back_enter, side == 0)
        adjoint = jnp.where(inside, adjoint, 0.0)
        rest = adjoint * (1.0 - gate)
        to_gate = rest * (previous * decay - cand * gate)
        to_cand = rest * (1.0 - cand * cand)
        out_ref[0, :, pl.ds(2 * side * GRU_H, GRU_H)] = to_gate.astype(BF16)
        out_ref[0, :, pl.ds((2 * side + 1) * GRU_H, GRU_H)] = to_cand.astype(BF16)
        bias_ref[0, :, there] = jnp.sum(to_gate, axis=0, keepdims=True)


def per_sequence(*tail):
    return pl.BlockSpec((1,) + tail, lambda s: (s,) + (0,) * len(tail))


def whole_block(*shape):
    return pl.BlockSpec(shape, lambda s: (0,) * len(shape))


def gru_forward(chars, w_gru, bias, start, first, end, last, real):
    batch, rows, width = chars.shape
    tokens = start.shape[2]
    two = 2 * GRU_H
    kept = jax.ShapeDtypeStruct((batch, rows, two), F32)
    return pl.pallas_call(
        functools.partial(gru_forward_kernel, real),
        grid=(batch,),
        in_specs=[per_sequence(rows, width), whole_block(width, w_gru.shape[1]), whole_block(1, two)]
        + [per_sequence(1, tokens)] * 4,
        out_specs=[per_sequence(rows, two)] * 5 + [whole_block(KINDS * batch, two)],
        out_shape=[kept] * 5 + [jax.ShapeDtypeStruct((KINDS * batch, two), F32)],
        compiler_params=params(),
        cost_estimate=cost(
            2 * batch * rows * width * 2 * two,
            chars.size * 2 + w_gru.size * 2 + 20 * batch * rows * two,
            2 * batch * rows * two,
        ),
        name="gru_forward",
    )(chars, w_gru, bias, start, first, end, last)


def gather_states(state, cum, edges, end, start):
    batch, rows, two = state.shape
    tokens = end.shape[1]
    return pl.pallas_call(
        char_tok_kernel,
        out_shape=[
            jax.ShapeDtypeStruct((batch * tokens, two), F32),
            jax.ShapeDtypeStruct((batch, 1, two), F32),
        ],
        compiler_params=params(),
        cost_estimate=cost(
            4 * batch * rows * tokens * two, 8 * batch * rows * two + 4 * batch * tokens * two
        ),
        name="gather_states",
    )(state, cum, edges, end, start)


def gru_back(grad, decay, end, start, real):
    batch, rows, two = decay.shape
    tokens = end.shape[2]
    kept = jax.ShapeDtypeStruct((batch, rows, two), F32)
    return pl.pallas_call(
        functools.partial(gru_back_kernel, real),
        grid=(batch,),
        in_specs=[per_sequence(tokens, two), per_sequence(rows, two)]
        + [per_sequence(1, tokens)] * 2,
        out_specs=[per_sequence(rows, two)] * 3 + [whole_block(KINDS * batch, two)],
        out_shape=[kept] * 3 + [jax.ShapeDtypeStruct((KINDS * batch, two), F32)],
        compiler_params=params(),
        cost_estimate=cost(
            4 * batch * rows * tokens * two, 16 * batch * rows * two + 4 * batch * tokens * two
        ),
        name="gru_back",
    )(grad, decay, end, start)


def gru_grad(gate, cand, decay, cum, state, enter, spread, back_cum, carried, back_enter, real):
    batch, rows, two = decay.shape
    big = per_sequence(rows, two)
    row = per_sequence(1, two)
    return pl.pallas_call(
        functools.partial(gru_grad_kernel, real),
        grid=(batch,),
        in_specs=[big] * 5 + [row] + [big] * 3 + [row],
        out_specs=[per_sequence(rows, 2 * two), row],
        out_shape=[
            jax.ShapeDtypeStruct((batch, rows, 2 * two), BF16),
            jax.ShapeDtypeStruct((batch, 1, two), F32),
        ],
        compiler_params=params(),
        cost_estimate=cost(20 * batch * rows * two, 36 * batch * rows * two),
        name="gru_grad",
    )(gate, cand, decay, cum, state, enter, spread, back_cum, carried, back_enter)


def all_edges(edges):
    return lax.all_gather(edges, "ctx", axis=0)


def entering_kernel(decay_ref, drive_ref, out_ref):
    for sequence in range(out_ref.shape[0]):
        out_ref[sequence] = entering_row(
            edge_reader(decay_ref, 0), edge_reader(drive_ref, 0), sequence, decay_ref.shape[0],
            True,
        )


def back_entering(decays, drives):
    batch, two = decays.shape[1] // KINDS, decays.shape[2]
    return pl.pallas_call(
        entering_kernel,
        out_shape=jax.ShapeDtypeStruct((batch, 1, two), F32),
        compiler_params=params(),
        name="back_entering",
    )(decays, drives)


def project_kernel(groups, part, tok_ref, w_ref, seg_ref, out_ref):
    qkv = matmul(tok_ref[0], w_ref[...]).astype(BF16)
    rows, width = tok_ref.shape[1], tok_ref.shape[2]
    lane = lax.broadcasted_iota(jnp.int32, (rows, HEAD_DIM), 1)
    marks = jnp.where(lane == seg_ref[0], 1.0, 0.0).astype(BF16)
    for group in range(groups):
        pieces = [
            qkv[:, kind * width + group * part : kind * width + (group + 1) * part]
            for kind in range(3)
        ]
        out_ref[group] = jnp.concatenate(pieces + [marks], axis=1)


def attend_kernel(heads, tokens, all_ref, query_ref, edge_ref, out_ref, kept_ref, key_scr, value_scr):
    part = heads * HEAD_DIM
    rows = query_ref.shape[0]

    @pl.when(pl.program_id(0) == 0)
    def build():
        marks = all_ref[:, 3 * part :]
        blocked = ((marks.astype(F32) - 1.0) * FAR).astype(BF16)
        ones = jnp.ones_like(marks)
        for head in range(heads):
            at = head * HEAD_DIM
            key_scr[head] = jnp.concatenate(
                [all_ref[:, part + at : part + at + HEAD_DIM], blocked], axis=1
            )
            value_scr[head] = jnp.concatenate(
                [all_ref[:, 2 * part + at : 2 * part + at + HEAD_DIM], ones], axis=1
            )

    marks = query_ref[:, 3 * part :]
    outs = []
    for head in range(heads):
        at = head * HEAD_DIM
        query = query_ref[:, at : at + HEAD_DIM] * jnp.asarray(HEAD_DIM ** (-0.5), BF16)
        query = jnp.concatenate([query, marks], axis=1)
        expvals = jnp.exp(matmul_nt(query, key_scr[head]))
        both = matmul(expvals.astype(BF16), value_scr[head])
        total = both[:, HEAD_DIM:]
        context = both[:, :HEAD_DIM] / total
        kept_ref[:, pl.ds(head * 2 * HEAD_DIM, 2 * HEAD_DIM)] = jnp.concatenate(
            [context, total], axis=1
        )
        outs.append(context.astype(BF16))
    block = edges_to_block(edge_ref[...], tokens)
    outs.append(jnp.concatenate([block] * (rows // tokens), axis=0))
    out_ref[...] = jnp.concatenate(outs, axis=1)


def attend_back_kernel(
    heads, tokens, all_ref, kept_ref, grad_ref, edges_ref, out_ref, enter_ref,
    query_scr, key_scr, value_scr, grad_scr, edge_scr,
):
    part = heads * HEAD_DIM
    rows = out_ref.shape[0]
    step = pl.program_id(0)

    @pl.when(step == 0)
    def build():
        marks = all_ref[:, 3 * part :]
        blocked = ((marks.astype(F32) - 1.0) * FAR).astype(BF16)
        lane = lax.broadcasted_iota(jnp.int32, marks.shape, 1)
        pair = jnp.where(lane < 2, 1.0, 0.0).astype(BF16)
        for head in range(heads):
            at = head * HEAD_DIM
            query = all_ref[:, at : at + HEAD_DIM] * jnp.asarray(HEAD_DIM ** (-0.5), BF16)
            query_scr[head] = jnp.concatenate([query, marks], axis=1)
            key_scr[head] = jnp.concatenate(
                [all_ref[:, part + at : part + at + HEAD_DIM], blocked], axis=1
            )
            value_scr[head] = jnp.concatenate(
                [all_ref[:, 2 * part + at : 2 * part + at + HEAD_DIM], pair], axis=1
            )
            context = kept_ref[:, 2 * at : 2 * at + HEAD_DIM]
            total = kept_ref[:, 2 * at + HEAD_DIM : 2 * at + 2 * HEAD_DIM]
            grad = grad_ref[:, at : at + HEAD_DIM].astype(F32) / total
            delta = jnp.sum(grad * context, axis=1, keepdims=True)
            high, low = two_parts(-delta)
            extra = jnp.where(
                lane == 0, high.astype(F32), jnp.where(lane == 1, low.astype(F32), 0.0)
            )
            grad_scr[head] = jnp.concatenate([grad, extra], axis=1).astype(BF16)
        for other in range(edges_ref.shape[0]):
            edge_scr[other] = edges_of_block(
                grad_ref[other * tokens : (other + 1) * tokens, part : part + HEAD_DIM]
            )
        for sequence in range(enter_ref.shape[0]):
            enter_ref[sequence] = entering_row(
                edge_reader(edges_ref, 0), edge_reader(edge_scr, 0), sequence,
                edges_ref.shape[0], True,
            )

    here = pl.ds(pl.multiple_of(step * rows, rows), rows)
    scale = HEAD_DIM ** (-0.5)
    d_query, d_key, d_value = [], [], []
    for head in range(heads):
        expvals = jnp.exp(matmul_nt(query_scr[head, here], key_scr[head]))
        inner = matmul_nt(grad_scr[head, here], value_scr[head])
        d_scores = (expvals * inner).astype(BF16)
        d_query.append((matmul(d_scores, key_scr[head])[:, :HEAD_DIM] * scale).astype(BF16))
        expvals = jnp.exp(matmul_nt(key_scr[head, here], query_scr[head]))
        inner = matmul_nt(value_scr[head, here], grad_scr[head])
        d_scores = (expvals * inner).astype(BF16)
        d_key.append(matmul(d_scores, query_scr[head])[:, :HEAD_DIM].astype(BF16))
        d_value.append(
            matmul(expvals.astype(BF16), grad_scr[head])[:, :HEAD_DIM].astype(BF16)
        )
    pad = jnp.zeros((rows, HEAD_DIM), BF16)
    out_ref[...] = jnp.concatenate(d_query + d_key + d_value + [pad], axis=1)


def unpack_kernel(groups, part, kinds, in_ref, out_ref, *edge_refs):
    for edge_ref in edge_refs:
        for group in range(groups):
            edge_ref[group] = edges_of_block(in_ref[group, :, kinds * part :])
    pieces = [
        in_ref[group, :, kind * part : (kind + 1) * part]
        for kind in range(kinds)
        for group in range(groups)
    ]
    out_ref[...] = jnp.concatenate(pieces, axis=1)


def send_grad_kernel(groups, part, grad_ref, w_ref, edge_ref, out_ref):
    d_context = matmul_nt(grad_ref[...], w_ref[...]).astype(BF16)
    block = edges_to_block(edge_ref[...], grad_ref.shape[0])
    for group in range(groups):
        out_ref[group] = jnp.concatenate(
            [d_context[:, group * part : (group + 1) * part], block], axis=1
        )


def heads_here(batch, count):
    if batch * HEADS % count != 0:
        return 0
    heads = batch * HEADS // count
    if heads > HEADS or HEADS % heads != 0 or heads % 2 == 0 or batch * KINDS != 8:
        return 0
    return heads


def project_and_pack(tokens, w_qkv, segment, heads):
    batch, rows, width = tokens.shape
    groups, part = HEADS // heads, heads * HEAD_DIM
    wide = 3 * part + HEAD_DIM
    return pl.pallas_call(
        functools.partial(project_kernel, groups, part),
        grid=(batch,),
        in_specs=[
            per_sequence(rows, width),
            whole_block(width, 3 * width),
            per_sequence(rows, 1),
        ],
        out_specs=pl.BlockSpec((groups, rows, wide), lambda s: (s, 0, 0)),
        out_shape=jax.ShapeDtypeStruct((batch * groups, rows, wide), BF16),
        compiler_params=params(),
        cost_estimate=cost(
            6 * batch * rows * width * width,
            tokens.size * 2 + w_qkv.size * 2 + 2 * batch * groups * rows * wide,
        ),
        name="project",
    )(tokens, w_qkv, segment[:, :, None])


def attend(everything, edges, heads, tokens):
    length, wide = everything.shape
    block = 256
    part = heads * HEAD_DIM
    out_wide = part + HEAD_DIM
    return pl.pallas_call(
        functools.partial(attend_kernel, heads, tokens),
        grid=(length // block,),
        in_specs=[
            pl.BlockSpec((length, wide), lambda i: (0, 0)),
            pl.BlockSpec((block, wide), lambda i: (i, 0)),
            pl.BlockSpec(edges.shape, lambda i: (0, 0)),
        ],
        out_specs=[
            pl.BlockSpec((block, out_wide), lambda i: (i, 0)),
            pl.BlockSpec((block, 2 * part), lambda i: (i, 0)),
        ],
        out_shape=[
            jax.ShapeDtypeStruct((length, out_wide), BF16),
            jax.ShapeDtypeStruct((length, 2 * part), F32),
        ],
        scratch_shapes=[
            pltpu.VMEM((heads, length, 2 * HEAD_DIM), BF16),
            pltpu.VMEM((heads, length, 2 * HEAD_DIM), BF16),
        ],
        compiler_params=params(),
        cost_estimate=cost(
            8 * heads * length * length * HEAD_DIM,
            length * (wide * 2 + out_wide * 2 + 8 * part),
            heads * length * length,
        ),
        name="attend",
    )(everything, everything, edges)


def attend_back(everything, kept, grads, edges, heads, tokens):
    length, wide = everything.shape
    block = 256
    part = heads * HEAD_DIM
    batch, two = edges.shape[1] // KINDS, edges.shape[2]
    scratch = pltpu.VMEM((heads, length, 2 * HEAD_DIM), BF16)
    return pl.pallas_call(
        functools.partial(attend_back_kernel, heads, tokens),
        grid=(length // block,),
        in_specs=[
            pl.BlockSpec((length, wide), lambda i: (0, 0)),
            pl.BlockSpec((length, 2 * part), lambda i: (0, 0)),
            pl.BlockSpec((length, part + HEAD_DIM), lambda i: (0, 0)),
            pl.BlockSpec(edges.shape, lambda i: (0, 0, 0)),
        ],
        out_specs=[
            pl.BlockSpec((block, wide), lambda i: (i, 0)),
            pl.BlockSpec((batch, 1, two), lambda i: (0, 0, 0)),
        ],
        out_shape=[
            jax.ShapeDtypeStruct((length, wide), BF16),
            jax.ShapeDtypeStruct((batch, 1, two), F32),
        ],
        scratch_shapes=[scratch] * 4 + [pltpu.VMEM(edges.shape, F32)],
        compiler_params=params(),
        cost_estimate=cost(
            28 * heads * length * length * HEAD_DIM,
            length * (wide * 4 + 8 * part + 2 * part),
            2 * heads * length * length,
        ),
        name="attend_back",
    )(everything, kept, grads, edges)


def unpack(received, heads, kinds, batch, edges):
    count, rows, wide = received.shape
    groups, part = HEADS // heads, heads * HEAD_DIM
    width = kinds * groups * part
    out_specs = [pl.BlockSpec((rows, width), lambda s: (s, 0))]
    out_shape = [jax.ShapeDtypeStruct((batch * rows, width), BF16)]
    if edges:
        out_specs.append(pl.BlockSpec((groups, KINDS * batch, 2 * GRU_H), lambda s: (s, 0, 0)))
        out_shape.append(jax.ShapeDtypeStruct((count, KINDS * batch, 2 * GRU_H), F32))
    return pl.pallas_call(
        functools.partial(unpack_kernel, groups, part, kinds),
        grid=(batch,),
        in_specs=[pl.BlockSpec((groups, rows, wide), lambda s: (s, 0, 0))],
        out_specs=out_specs,
        out_shape=out_shape,
        compiler_params=params(),
        cost_estimate=cost(0, 2 * received.size + 2 * batch * rows * width),
        name="unpack",
    )(received)


def send_grad(d_attn, w_out, edges, heads, batch):
    total, width = d_attn.shape
    rows = total // batch
    groups, part = HEADS // heads, heads * HEAD_DIM
    wide = part + HEAD_DIM
    return pl.pallas_call(
        functools.partial(send_grad_kernel, groups, part),
        grid=(batch,),
        in_specs=[
            pl.BlockSpec((rows, width), lambda s: (s, 0)),
            whole_block(width, width),
            whole_block(*edges.shape),
        ],
        out_specs=pl.BlockSpec((groups, rows, wide), lambda s: (s, 0, 0)),
        out_shape=jax.ShapeDtypeStruct((batch * groups, rows, wide), BF16),
        compiler_params=params(),
        cost_estimate=cost(
            2 * total * width * width, 2 * (d_attn.size + w_out.size + total * groups * wide)
        ),
        name="send_grad",
    )(d_attn, w_out, edges)


def feed_forward_kernel(hidden_ref, w_ref, bias_ref, inner_ref, slope_ref):
    pre = matmul(hidden_ref[...], w_ref[...]) + bias_ref[...]
    at = jnp.abs(pre) * (0.5**0.5)
    near = 1.0 / (1.0 + 0.3275911 * at)
    gauss = jnp.exp(-at * at)
    series = 1.061405429
    for term in (-1.453152027, 1.421413741, -0.284496736, 0.254829592):
        series = series * near + term
    tail = 0.5 * series * near * gauss
    below = jnp.where(pre < 0.0, tail, 1.0 - tail)
    inner_ref[...] = (pre * below).astype(BF16)
    slope_ref[...] = (below + pre * gauss * (2.0 * jnp.pi) ** -0.5).astype(BF16)


def feed_forward(hidden, w_up, bias):
    rows, width = hidden.shape
    wide = w_up.shape[1]
    block = 512
    column = pl.BlockSpec((rows, block), lambda i: (0, i))
    return pl.pallas_call(
        feed_forward_kernel,
        grid=(wide // block,),
        in_specs=[
            whole_block(rows, width),
            pl.BlockSpec((width, block), lambda i: (0, i)),
            pl.BlockSpec((1, block), lambda i: (0, i)),
        ],
        out_specs=[column, column],
        out_shape=[jax.ShapeDtypeStruct((rows, wide), BF16)] * 2,
        compiler_params=params(),
        cost_estimate=cost(
            2 * rows * width * wide, 2 * (hidden.size + w_up.size + 2 * rows * wide), rows * wide
        ),
        name="feed_forward",
    )(hidden, w_up, bias)


def block_size(rows):
    size = min(rows, BLOCK_LIMIT)
    while rows % size != 0:
        size = size - 1
    return size


def split_blocks(array, size):
    return array.reshape((array.shape[0] // size, size) + array.shape[1:])


def to_heads(matrix):
    return matrix.reshape(matrix.shape[0], HEADS, HEAD_DIM)


def masked_exp(query_heads, key_heads, query_seg, key_seg):
    scores = jnp.einsum(
        "qhd,khd->hqk", query_heads, key_heads, preferred_element_type=F32
    ) * HEAD_DIM ** (-0.5)
    same = (query_seg[:, None] == key_seg[None, :])[None, :, :]
    return jnp.where(same, jnp.exp(scores), 0.0)


def everyone(rows):
    return lax.all_gather(rows, "ctx", axis=0, tiled=True)


def gathered_attention(qkv, seg_row):
    tok_rows, width = qkv.shape[0], qkv.shape[1] // 3
    query_heads = to_heads(qkv[:, :width])
    pieces = (everyone(qkv[:, width : 2 * width]), everyone(qkv[:, 2 * width :]), everyone(seg_row))
    size = block_size(pieces[0].shape[0])

    def step(acc, item):
        key_block, value_block, seg_block = item
        expvals = masked_exp(query_heads, to_heads(key_block), seg_row, seg_block)
        part_num = jnp.einsum(
            "hqk,khd->qhd", expvals.astype(BF16), to_heads(value_block),
            preferred_element_type=F32,
        )
        return ((acc[0] + part_num, acc[1] + jnp.transpose(jnp.sum(expvals, axis=-1))), None)

    (numer, total), unused = lax.scan(
        step,
        (jnp.zeros((tok_rows, HEADS, HEAD_DIM), F32), jnp.zeros((tok_rows, HEADS), F32)),
        tuple(split_blocks(piece, size) for piece in pieces),
    )
    return numer / total[:, :, None], total


def gathered_attention_back(qkv, seg_row, context, total, d_context):
    tok_rows, width = qkv.shape[0], qkv.shape[1] // 3
    scale = HEAD_DIM ** (-0.5)
    d_context = to_heads(d_context)
    query_rows, key_rows, value_rows = (qkv[:, i * width : (i + 1) * width] for i in range(3))
    grad_heads = (d_context / total[:, :, None]).astype(BF16)
    delta = jnp.sum(d_context * context, axis=-1) / total
    key_heads, value_heads, query_heads = (
        to_heads(key_rows), to_heads(value_rows), to_heads(query_rows)
    )
    zero_heads = jnp.zeros((tok_rows, HEADS, HEAD_DIM), F32)
    seg_all = everyone(seg_row)
    size = block_size(seg_all.shape[0])

    def key_step(acc, item):
        query_block, grad_block, delta_block, seg_block = item
        query_h, grad_h = to_heads(query_block), to_heads(grad_block)
        expvals = masked_exp(query_h, key_heads, seg_block, seg_row)
        dprob = jnp.einsum("qhd,khd->hqk", grad_h, value_heads, preferred_element_type=F32)
        dscore = (expvals * (dprob - jnp.transpose(delta_block)[:, :, None])).astype(BF16)
        dkey = acc[0] + scale * jnp.einsum(
            "hqk,qhd->khd", dscore, query_h, preferred_element_type=F32
        )
        dval = acc[1] + jnp.einsum(
            "hqk,qhd->khd", expvals.astype(BF16), grad_h, preferred_element_type=F32
        )
        return ((dkey, dval), None)

    (dkey, dval), unused = lax.scan(
        key_step,
        (zero_heads, zero_heads),
        tuple(
            split_blocks(piece, size)
            for piece in (
                everyone(query_rows),
                everyone(grad_heads.reshape(tok_rows, width)),
                everyone(delta),
                seg_all,
            )
        ),
    )

    def query_step(acc, item):
        key_block, value_block, seg_block = item
        key_h = to_heads(key_block)
        expvals = masked_exp(query_heads, key_h, seg_row, seg_block)
        dprob = jnp.einsum(
            "qhd,khd->hqk", grad_heads, to_heads(value_block), preferred_element_type=F32
        )
        dscore = (expvals * (dprob - jnp.transpose(delta)[:, :, None])).astype(BF16)
        return (
            acc + scale * jnp.einsum("hqk,khd->qhd", dscore, key_h, preferred_element_type=F32),
            None,
        )

    dquery, unused = lax.scan(
        query_step,
        zero_heads,
        tuple(
            split_blocks(piece, size)
            for piece in (everyone(key_rows), everyone(value_rows), seg_all)
        ),
    )
    return jnp.concatenate(
        [part.reshape(tok_rows, width) for part in (dquery, dkey, dval)], axis=1
    ).astype(BF16)


def neighbours(rows):
    count = lax.axis_size("ctx")
    up = [(i, i + 1) for i in range(count - 1)]
    down = [(j, i) for i, j in up]
    before = lax.ppermute(rows[:, -1], "ctx", up)
    after = lax.ppermute(rows[:, 0], "ctx", down)
    return before[:, None], after[:, None]


def shifted(rows, before, after):
    later = jnp.concatenate([before, rows[:, :-1]], axis=1)
    earlier = jnp.concatenate([rows[:, 1:], after], axis=1)
    return later, earlier


def routed():
    return lax.axis_size("ctx") == 8 and lax.axis_size("fsdp") == 4


STEPS = (1, 2, 4)
ORDER = "DCDCDTCDTCDTQCDQTQTQCTDQQTQ"


def flip(value, axis, bit):
    return lax.ppermute(value, axis, [(i, i ^ bit) for i in range(lax.axis_size(axis))])


def slot():
    me = lax.axis_index("ctx")
    return (me % 2) * 4 + ((me // 2) % 2) * 2 + me // 4


class CtxSum:
    def __init__(self, value):
        self.value = value
        self.axis = value.ndim - 2
        self.stage = 0

    def halve(self, value, bit):
        mine = (lax.axis_index("ctx") // bit) % 2
        half = value.shape[self.axis] // 2
        send = lax.dynamic_slice_in_dim(value, (1 - mine) * half, half, self.axis)
        self.keep = lax.dynamic_slice_in_dim(value, mine * half, half, self.axis)
        self.send(send, bit)

    def send(self, value, bit):
        self.sent = value
        self.got = flip(value, "ctx", bit)

    def advance(self, *others):
        stage = self.stage
        self.stage = stage + 1
        if stage == 0:
            self.halve(after(self.value, *others), STEPS[0])
        elif stage <= 3:
            got = after(self.got, *others).astype(F32)
            piece = (self.keep.astype(F32) + got).astype(BF16)
            if stage < 3:
                self.halve(piece, STEPS[stage])
            else:
                self.send(piece[None], STEPS[2])
        else:
            piece = jnp.concatenate([self.sent, after(self.got, *others)], axis=0)
            if stage < 6:
                self.send(piece, STEPS[5 - stage])
            else:
                self.result = self.sent = piece
        return self.sent


def run_in_order(events, waits):
    last = ()
    for event, chain in enumerate(events):
        last = (chain.advance(*last, *waits.get(event, ())),)


def settle_kernel(order_ref, in_ref, *out_refs):
    at = 0
    for out_ref in out_refs:
        wide = out_ref.shape[-1]
        out_ref[...] = in_ref[0, ..., at : at + wide].astype(F32)
        at = at + wide


def settle(pieces, widths):
    lead = pieces.shape[1:-2]
    rows, total = pieces.shape[-2:]
    order = jnp.bitwise_xor(slot(), jnp.arange(8, dtype=jnp.int32))
    none = (0,) * len(lead)
    return pl.pallas_call(
        settle_kernel,
        grid_spec=pltpu.PrefetchScalarGridSpec(
            num_scalar_prefetch=1,
            grid=(8,),
            in_specs=[
                pl.BlockSpec((1,) + lead + (rows, total), lambda r, o: (r,) + none + (0, 0))
            ],
            out_specs=[
                pl.BlockSpec(lead + (rows, width), lambda r, o: none + (o[r], 0))
                for width in widths
            ],
        ),
        out_shape=[jax.ShapeDtypeStruct(lead + (8 * rows, width), F32) for width in widths],
        compiler_params=params(),
        cost_estimate=cost(pieces.size, 6 * pieces.size),
        name="settle",
    )(order, pieces)


def place_own_kernel(spans, own_ref, core_ref, *rest):
    outs, sems = rest[:-1], rest[-1]
    mine = lax.axis_index("fsdp")
    copies, at = [], 0
    for span, out_ref in zip(spans, outs):
        for source, shard in ((own_ref, mine), (core_ref, jnp.bitwise_xor(mine, 1))):
            copies.append(
                pltpu.make_async_copy(
                    source.at[pl.ds(at, span)], out_ref.at[shard], sems.at[len(copies)]
                )
            )
        at = at + span
    for copy in copies:
        copy.start()
    for copy in copies:
        copy.wait()


def place_kernel(spans, order, piece_ref, core_ref, *rest):
    outs, sems = rest[len(spans) : -1], rest[-1]
    place = slot()
    mine = lax.axis_index("fsdp")
    copies = []
    for source, shard in (
        (piece_ref, jnp.bitwise_xor(mine, 2)),
        (core_ref, jnp.bitwise_xor(mine, 3)),
    ):
        for position, other in enumerate(order):
            at = 0
            for span, out_ref in zip(spans, outs):
                part = span // 8
                there = pl.multiple_of(jnp.bitwise_xor(place, other) * part, part)
                copies.append(
                    pltpu.make_async_copy(
                        source.at[position, pl.ds(at, part)],
                        out_ref.at[shard, pl.ds(there, part)],
                        sems.at[len(copies)],
                    )
                )
                at = at + part
    for copy in copies:
        copy.start()
    for copy in copies:
        copy.wait()


def after(value, *others):
    return lax.optimization_barrier((value,) + others)[0]


class SpreadGather:
    def __init__(self, shards):
        self.spans = tuple(shard.shape[0] for shard in shards)
        self.width = shards[0].shape[1]
        place = slot()
        self.own = jnp.concatenate(shards, axis=0) if len(shards) > 1 else shards[0]
        piece = [
            lax.dynamic_slice_in_dim(shard, place * (span // 8), span // 8, 0)
            for shard, span in zip(shards, self.spans)
        ]
        self.piece = flip(jnp.concatenate(piece, axis=0), "fsdp", 2)[None]
        self.core = flip(self.own, "fsdp", 1)
        self.order = [0]

    def double(self, bit, *others):
        piece = after(self.piece, *others) if others else self.piece
        self.piece = jnp.concatenate([piece, flip(piece, "ctx", bit)], axis=0)
        self.order = self.order + [other ^ (4 // bit) for other in self.order]

    def cores(self, *others):
        piece = after(self.piece, *others) if others else self.piece
        self.core_piece = flip(piece, "fsdp", 1)

    def place_own(self):
        spans, width = self.spans, self.own.shape[1]
        self.whole = pl.pallas_call(
            functools.partial(place_own_kernel, spans),
            in_specs=[pl.BlockSpec(memory_space=pltpu.VMEM)] * 2,
            out_specs=[pl.BlockSpec(memory_space=pl.ANY)] * len(spans),
            out_shape=[jax.ShapeDtypeStruct((4, span, width), BF16) for span in spans],
            scratch_shapes=[pltpu.SemaphoreType.DMA((2 * len(spans),))],
            compiler_params=params(),
            cost_estimate=cost(0, 8 * sum(spans) * width),
            name="place_own",
        )(self.own, self.core)

    def finish(self):
        spans, width = self.spans, self.own.shape[1]
        anywhere = [pl.BlockSpec(memory_space=pl.ANY)] * len(spans)
        return pl.pallas_call(
            functools.partial(place_kernel, spans, self.order),
            in_specs=[pl.BlockSpec(memory_space=pltpu.VMEM)] * 2 + anywhere,
            out_specs=anywhere,
            out_shape=[jax.ShapeDtypeStruct((4, span, width), BF16) for span in spans],
            scratch_shapes=[pltpu.SemaphoreType.DMA((16 * len(spans),))],
            input_output_aliases={2 + i: i for i in range(len(spans))},
            compiler_params=params(),
            cost_estimate=cost(0, 8 * sum(spans) * width),
            name="place",
        )(self.piece, self.core_piece, *self.whole)


def over_fsdp(grads):
    return lax.psum_scatter(grads, "fsdp", scatter_dimension=0, tiled=True)


def plain_sum(grads, axis=0):
    share = lax.psum_scatter(grads, "fsdp", scatter_dimension=axis, tiled=True)
    return lax.psum(share.astype(F32), "ctx")


def local(
    tokens, chars, segment, char_end, w_qkv, w_out, norm1_gain, norm1_bias, w_up, b_up, w_down,
    norm2_gain, norm2_bias, w_gru, b_gate, w_ftok, w_fchr, w_conv, norm3_gain, norm3_bias,
    norm4_gain, norm4_bias, d_token, d_char,
):
    count, me = lax.axis_size("ctx"), lax.axis_index("ctx")
    shards = lax.axis_size("fsdp")
    batch, rows, width = tokens.shape
    char_rows = chars.shape[1]
    total_rows = batch * rows
    heads = heads_here(batch, count)
    padded_rows = -(-char_rows // 8) * 8

    def gather(weight, axis=0):
        return lax.all_gather(weight, "fsdp", axis=axis, tiled=True)

    own_width = norm1_gain.shape[0]
    vectors = (
        norm1_gain, norm1_bias, norm2_gain, norm2_bias, b_gate, norm3_gain, norm3_bias,
        norm4_gain, norm4_bias,
    )
    columns = jnp.stack(vectors, axis=1)
    columns = jnp.concatenate([columns, b_up.reshape(-1, own_width).T], axis=1)
    small_count = columns.shape[1]
    wide_gru = w_gru.shape[1]
    columns = jnp.pad(columns, ((0, 0), (0, 128 - small_count)))
    w_qkv = gather(w_qkv)
    w_gru = gather(jnp.concatenate([w_gru, columns], axis=1))
    w_out = gather(w_out)
    w_up = gather(w_up)
    columns = w_gru[:, wide_gru : wide_gru + small_count].astype(F32)
    (
        norm1_gain, norm1_bias, norm2_gain, norm2_bias, b_gate, norm3_gain, norm3_bias,
        norm4_gain, norm4_bias,
    ) = (columns[:, i][None, :] for i in range(9))
    b_up = jnp.swapaxes(columns[:, 9:].reshape(shards, own_width, -1), 1, 2).reshape(1, -1)
    w_down = gather(w_down)
    if routed():
        first_taps = SpreadGather([w_conv[0], w_conv[1]])
        last_tap = SpreadGather([w_conv[2], jnp.concatenate([w_ftok, w_fchr], axis=1)])
    else:
        w_ftok = gather(w_ftok)
        w_fchr = gather(w_fchr)
        w_conv = gather(w_conv, 1)

    start = jnp.concatenate([jnp.zeros((batch, 1), jnp.int32), char_end[:, :-1] + 1], axis=1)
    change = (segment[:, 1:] != segment[:, :-1]).astype(F32)
    first = jnp.concatenate([jnp.broadcast_to((me == 0).astype(F32), (batch, 1)), change], axis=1)
    last = jnp.concatenate(
        [change, jnp.broadcast_to((me == count - 1).astype(F32), (batch, 1))], axis=1
    )
    flat_tokens = tokens.reshape(total_rows, width)
    chars_pad = jnp.pad(chars, ((0, 0), (0, padded_rows - char_rows), (0, 0)))
    chars_in = chars_pad
    if heads:
        sent = project_and_pack(tokens, w_qkv, segment, heads)
        chars_in = after(chars_pad, sent)
    gate, cand, decay, cum, state, edges = gru_forward(
        chars_in, w_gru, b_gate, start[:, None], first[:, None], char_end[:, None],
        last[:, None], char_rows,
    )

    if heads:
        everything = lax.all_to_all(sent, "ctx", 0, 0, tiled=True)
        everything = everything.reshape(count * rows, -1)
        packed_context, kept = attend(everything, edges, heads, rows)
        received = lax.all_to_all(packed_context.reshape(count, rows, -1), "ctx", 0, 0, tiled=True)
        context_b, edges_all = unpack(received, heads, 1, batch, True)
    else:
        qkv = matmul(flat_tokens, w_qkv).astype(BF16).reshape(batch, rows, -1)
        results = [gathered_attention(qkv[i], segment[i]) for i in range(batch)]
        context_b = jnp.concatenate([r[0].reshape(rows, width) for r in results]).astype(BF16)
        edges_all = all_edges(edges)

    attn = matmul(context_b, w_out)
    hidden1, kept1 = layer_norm(flat_tokens.astype(F32) + attn, norm1_gain, norm1_bias)
    hidden1_b = hidden1.astype(BF16)
    if routed():
        first_taps.double(4, sent)
        last_tap.double(1, sent)
        first_taps.place_own()
        last_tap.place_own()
        first_taps.double(2, state)
        last_tap.double(4, state)
        first_taps.double(1, packed_context)
        last_tap.double(2, packed_context)
        first_taps.cores(hidden1_b)
        last_tap.cores(hidden1_b)
        w_conv = [
            weight.reshape(-1, 2 * width) for weight in first_taps.finish() + last_tap.finish()
        ]
        w_ftok, w_fchr = w_conv[3][:, :width], w_conv[3][:, width:]
    inner_b, slope = feed_forward(hidden1_b, w_up, b_up)
    ffn = matmul(inner_b, w_down)
    hidden2, kept2 = layer_norm(hidden1 + ffn, norm2_gain, norm2_bias)
    hidden2_b = hidden2.astype(BF16)

    char_tok, enter = gather_states(
        state, cum, edges_all, char_end[:, :, None], start[:, :, None]
    )
    char_tok_b = char_tok.astype(BF16)
    joined = jnp.concatenate(
        [matmul(hidden2_b, w_ftok), matmul(char_tok_b, w_fchr)], axis=1
    ).astype(BF16)

    two = 2 * width
    blocks = joined.reshape(batch, rows, two)
    later, earlier = shifted(blocks, *neighbours(blocks))
    taps = (later.reshape(total_rows, two), joined, earlier.reshape(total_rows, two))
    conv = matmul(taps[1], w_conv[1]) + matmul(taps[0], w_conv[0]) + matmul(taps[2], w_conv[2])
    token_out, kept3 = layer_norm(hidden2 + conv[:, :width], norm3_gain, norm3_bias)
    char_out, kept4 = layer_norm(char_tok + conv[:, width:], norm4_gain, norm4_bias)

    d_in3, gain3_grad, bias3_grad = layer_norm_back(
        d_token.reshape(total_rows, width).astype(F32), norm3_gain, kept3
    )
    d_in4, gain4_grad, bias4_grad = layer_norm_back(
        d_char.reshape(total_rows, width).astype(F32), norm4_gain, kept4
    )
    d_conv = jnp.concatenate([d_in3, d_in4], axis=1).astype(BF16)
    d_before, d_after = neighbours(d_conv.reshape(batch, rows, two))
    d_later, d_earlier = shifted(d_conv.reshape(batch, rows, two), d_before, d_after)
    d_joined = (
        matmul_nt(d_conv, w_conv[1])
        + matmul_nt(d_earlier.reshape(total_rows, two), w_conv[0])
        + matmul_nt(d_later.reshape(total_rows, two), w_conv[2])
    ).astype(BF16)
    if routed():
        own_in = two // shards
        joined_own = after(joined, d_joined)
        joined_own = jnp.swapaxes(joined_own.reshape(total_rows, shards, own_in), 0, 1)
        joined_own = lax.all_to_all(joined_own, "fsdp", 0, 0, tiled=True).reshape(-1, own_in)
        d_all = gather(
            jnp.concatenate([d_conv.reshape(batch, rows, two), d_before, d_after], axis=1)
        )
        d_mid = d_all[:, :rows]
        d_sides = (
            jnp.concatenate([d_mid[:, 1:], d_all[:, rows + 1 :]], axis=1),
            d_mid,
            jnp.concatenate([d_all[:, rows : rows + 1], d_mid[:, :-1]], axis=1),
        )
    else:
        joined_own = joined
        conv_sum = plain_sum(jnp.stack([matmul_tn(tap, d_conv).astype(BF16) for tap in taps]), 1)

    d_tok_part, d_chr_part = d_joined[:, :width], d_joined[:, width:]
    d_hidden2 = d_in3 + matmul_nt(d_tok_part, w_ftok)
    d_char_tok = d_in4 + matmul_nt(d_chr_part, w_fchr)
    ftok_grad = matmul_tn(hidden2_b, d_tok_part).astype(BF16)
    fchr_grad = matmul_tn(char_tok_b, d_chr_part).astype(BF16)

    end_line, start_line = char_end[:, None], start[:, None]
    spread, back_cum, carried, back_edges = gru_back(
        d_char_tok.reshape(batch, rows, width), decay, end_line, start_line, char_rows
    )

    d_in2, gain2_grad, bias2_grad = layer_norm_back(d_hidden2, norm2_gain, kept2)
    d_ffn = d_in2.astype(BF16)
    down_grad = matmul_tn(inner_b, d_ffn).astype(BF16)
    reduced = over_fsdp if routed() else plain_sum
    second_sum = reduced(down_grad)
    d_pre = matmul_nt(d_ffn, w_down) * slope.astype(F32)
    bup_grad = jnp.sum(d_pre, axis=0)
    d_pre_low = d_pre.astype(BF16)
    d_hidden1 = d_in2 + matmul_nt(d_pre_low, w_up)
    d_in1, gain1_grad, bias1_grad = layer_norm_back(d_hidden1, norm1_gain, kept1)
    d_attn = d_in1.astype(BF16)
    if heads:
        sent = send_grad(d_attn, w_out, back_edges, heads, batch)
        hidden1_b, joined_own = after((hidden1_b, joined_own), sent)
    up_grad = matmul_tn(hidden1_b, d_pre_low).astype(BF16)
    wout_grad = matmul_tn(context_b, d_attn).astype(BF16)
    third_sum = reduced(jnp.concatenate([up_grad, wout_grad, ftok_grad, fchr_grad], axis=1))
    if routed():
        conv_chain = CtxSum(
            jnp.stack(
                [matmul_tn(joined_own, side.reshape(-1, two)).astype(BF16) for side in d_sides]
            )
        )
        conv_sent = conv_chain.advance()

    if heads:
        received = lax.all_to_all(sent, "ctx", 0, 0, tiled=True)
        if routed():
            received = after(received, conv_sent)
        packed_grad, back_enter = attend_back(
            everything, kept, received.reshape(count * rows, -1), edges_all, heads, rows
        )
        returned = lax.all_to_all(packed_grad.reshape(count, rows, -1), "ctx", 0, 0, tiled=True)
        (d_qkv,) = unpack(returned, heads, 3, batch, False)
    else:
        back_enter = back_entering(edges_all, all_edges(back_edges))
        d_context = matmul_nt(d_attn, w_out).reshape(batch, rows, width)
        d_qkv = jnp.concatenate(
            [
                gathered_attention_back(
                    qkv[i], segment[i], results[i][0], results[i][1], d_context[i]
                )
                for i in range(batch)
            ]
        )
    d_gate_in, bgate_grad = gru_grad(
        gate, cand, decay, cum, state, enter, spread, back_cum, carried, back_enter, char_rows
    )
    d_gate_in = d_gate_in.reshape(batch * padded_rows, -1)
    gru_weight_grad = matmul_tn(chars_pad.reshape(batch * padded_rows, width), d_gate_in)
    d_chars = matmul_nt(d_gate_in, w_gru[:, :wide_gru]).astype(BF16)
    d_chars = d_chars.reshape(batch, padded_rows, width)[:, :char_rows]

    qkv_grad = matmul_tn(flat_tokens, d_qkv).astype(BF16)
    d_tokens = (d_in1 + matmul_nt(d_qkv, w_qkv)).astype(BF16)

    small = jnp.stack(
        [
            gain1_grad, bias1_grad, gain2_grad, bias2_grad, jnp.sum(bgate_grad, axis=(0, 1)),
            gain3_grad, bias3_grad, gain4_grad, bias4_grad,
        ],
        axis=1,
    )
    up_small = bup_grad.reshape(shards, -1, width // shards)
    up_small = jnp.swapaxes(up_small, 1, 2).reshape(width, -1)
    small = jnp.concatenate([small, up_small], axis=1)
    small = jnp.pad(small, ((0, 0), (0, 128 - small_count)))
    fourth = jnp.concatenate([qkv_grad, gru_weight_grad.astype(BF16), small.astype(BF16)], axis=1)
    fourth_sum = reduced(fourth)

    widths = ((width,), (w_up.shape[1],) + (width,) * 3, (w_qkv.shape[1], wide_gru, 128))
    if routed():
        second_chain, third_chain, fourth_chain = (
            CtxSum(value) for value in (second_sum, third_sum, fourth_sum)
        )
        chains = dict(C=conv_chain, D=second_chain, T=third_chain, Q=fourth_chain)
        events = [chains[name] for name in ORDER]
        run_in_order(events, {ORDER.index("T"): (fourth,)})
        second_sum, third_sum, fourth_sum = (
            chain.result for chain in (second_chain, third_chain, fourth_chain)
        )
        (conv_sum,) = settle(conv_chain.result, (two,))
        (down_sum,), third, fourth = (
            settle(value, split)
            for value, split in zip((second_sum, third_sum, fourth_sum), widths)
        )
    else:
        (down_sum,), third, fourth = (
            jnp.split(value, [sum(split[:i]) for i in range(1, len(split))], axis=1)
            for value, split in zip((second_sum, third_sum, fourth_sum), widths)
        )
    vector = fourth[2]
    return (
        token_out.astype(BF16).reshape(batch, rows, width),
        char_out.astype(BF16).reshape(batch, rows, width),
        d_tokens.reshape(batch, rows, width),
        d_chars,
        fourth[0],
        third[1],
        vector[:, 0],
        vector[:, 1],
        third[0],
        jnp.swapaxes(vector[:, 9:small_count], 0, 1).reshape(-1),
        down_sum,
        vector[:, 2],
        vector[:, 3],
        fourth[1],
        vector[:, 4],
        third[2],
        third[3],
        conv_sum,
        vector[:, 5],
        vector[:, 6],
        vector[:, 7],
        vector[:, 8],
    )


def solution(mesh):
    rows = P("fsdp", "ctx", None)
    pairs = P("fsdp", "ctx")
    matrix = P("fsdp", None)
    vector = P("fsdp")
    weights = (
        matrix, matrix, vector, vector, matrix, vector, matrix, vector, vector, matrix, vector,
        matrix, matrix, P(None, "fsdp", None), vector, vector, vector, vector,
    )
    return jax.shard_map(
        local,
        mesh=mesh,
        in_specs=(rows, rows, pairs, pairs) + weights + (rows, rows),
        out_specs=(rows,) * 4 + weights,
        check_vma=False,
    )
```

```python
import functools

import jax
import jax.numpy as jnp
from jax import lax
from jax.experimental import pallas as pl
from jax.experimental.pallas import tpu as pltpu
from jax.sharding import PartitionSpec as P

HEADS = 12
HEAD_DIM = 64
GRU_H = 384
EPSILON = 1e-05
BLOCK_LIMIT = 1024
FAR = 1e9
VMEM_BYTES = 40 * 1024 * 1024

F32 = jnp.float32
BF16 = jnp.bfloat16


def matmul(left, right):
    return jnp.dot(left, right, preferred_element_type=F32)


def matmul_nt(left, right):
    return lax.dot_general(left, right, (((1,), (1,)), ((), ())), preferred_element_type=F32)


def matmul_tn(left, right):
    return lax.dot_general(left, right, (((0,), (0,)), ((), ())), preferred_element_type=F32)


def layer_norm(value, gain, shift):
    center = value - jnp.mean(value, axis=-1, keepdims=True)
    inverse = lax.rsqrt(jnp.mean(center * center, axis=-1, keepdims=True) + EPSILON)
    normed = center * inverse
    return normed * gain + shift, (normed, inverse)


def layer_norm_back(grad, gain, kept):
    normed, inverse = kept
    scaled = grad * gain
    into = inverse * (
        scaled
        - jnp.mean(scaled, axis=-1, keepdims=True)
        - normed * jnp.mean(scaled * normed, axis=-1, keepdims=True)
    )
    return into, jnp.sum(grad * normed, axis=0), jnp.sum(grad, axis=0)


def params(**more):
    return pltpu.CompilerParams(vmem_limit_bytes=VMEM_BYTES, **more)


def cost(flops, moved, transcendentals=0):
    return pl.CostEstimate(
        flops=1, bytes_accessed=1, transcendentals=0
    )


def two_parts(value):
    high = value.astype(BF16)
    return high, (value - high.astype(F32)).astype(BF16)


KINDS = 4


def store_edges(edge_ref, cols, rows):
    parts = [half.astype(F32) for row in rows for half in two_parts(row)]
    parts = parts + [jnp.zeros_like(parts[0])] * (KINDS - len(parts))
    parts = jnp.concatenate(parts, axis=0)
    for sequence in range(edge_ref.shape[0] // KINDS):

        @pl.when(pl.program_id(0) == sequence)
        def store():
            edge_ref[pl.ds(sequence * KINDS, KINDS), cols] = parts


def edges_to_block(edges, rows):
    count = edges.shape[1] // HEAD_DIM
    pieces = [edges[:, i * HEAD_DIM : (i + 1) * HEAD_DIM] for i in range(count)]
    pieces.append(jnp.zeros((rows - count * edges.shape[0], HEAD_DIM), F32))
    return jnp.concatenate(pieces, axis=0).astype(BF16)


def edges_of_block(block):
    block = block.astype(F32)
    count = 2 * GRU_H // HEAD_DIM
    return jnp.concatenate([block[i * 8 : (i + 1) * 8] for i in range(count)], axis=1)


def entering_row(decays, drives, sequence, count, flip):
    me = lax.axis_index("ctx")
    halves = []
    for side in (0, 1):
        cols = slice(side * GRU_H, (side + 1) * GRU_H)
        total = jnp.zeros((1, GRU_H), F32)
        backward = (side == 1) != flip
        order = range(count - 1, 0, -1) if backward else range(count - 1)
        for other in order:
            decay, drive = decays(other, sequence, cols), drives(other, sequence, cols)
            there = me < other if backward else me > other
            total = jnp.where(there, decay * total + drive, total)
        halves.append(total)
    return jnp.concatenate(halves, axis=1)


def edge_reader(ref, kind):
    def read(other, sequence, cols):
        at = sequence * KINDS + 2 * kind
        return ref[other, at : at + 1, cols] + ref[other, at + 1 : at + 2, cols]

    return read


def shift_rows(value, by, fill, up):
    rows = value.shape[0]
    row = lax.broadcasted_iota(jnp.int32, value.shape, 0)
    if up:
        return jnp.where(row < rows - by, pltpu.roll(value, rows - by, 0), fill)
    return jnp.where(row >= by, pltpu.roll(value, by, 0), fill)


def scan_rows(decay, drive, up):
    by = 1
    while by < decay.shape[0]:
        drive = drive + decay * shift_rows(drive, by, 0.0, up)
        decay = decay * shift_rows(decay, by, 1.0, up)
        by = by * 2
    return decay, drive


def gru_forward_kernel(
    real, chars_ref, w_ref, bias_ref, start_ref, first_ref, end_ref, last_ref,
    gate_ref, cand_ref, decay_ref, cum_ref, state_ref, edge_ref,
):
    columns = matmul(chars_ref[0], w_ref[:, : 4 * GRU_H])
    rows = columns.shape[0]
    tokens = start_ref.shape[2]
    place = lax.broadcasted_iota(jnp.int32, (rows, tokens), 0)
    inside = lax.broadcasted_iota(jnp.int32, (rows, GRU_H), 0) < real
    resets = [
        jnp.sum(jnp.where(place == at[0], flag[0], 0.0), axis=1, keepdims=True)
        for at, flag in ((start_ref, first_ref), (end_ref, last_ref))
    ]
    for side in (0, 1):
        cols = pl.ds(side * GRU_H, GRU_H)
        base = 2 * side * GRU_H
        gate = jax.nn.sigmoid(columns[:, base : base + GRU_H] + bias_ref[:, cols])
        cand = jnp.tanh(columns[:, base + GRU_H : base + 2 * GRU_H])
        decay = jnp.where(inside, gate * (1.0 - resets[side]), 1.0)
        drive = jnp.where(inside, (1.0 - gate) * cand, 0.0)
        gate_ref[0, :, cols] = gate
        cand_ref[0, :, cols] = cand
        decay_ref[0, :, cols] = decay
        cum, state = scan_rows(decay, drive, side == 1)
        cum_ref[0, :, cols] = cum
        state_ref[0, :, cols] = state
        at = 0 if side else real - 1
        store_edges(edge_ref, cols, (cum[at : at + 1], state[at : at + 1]))


def char_tok_kernel(state_ref, cum_ref, edges_ref, end_ref, start_ref, out_ref, enter_ref):
    batch, tokens = end_ref.shape[:2]
    for sequence in range(batch):
        enter = entering_row(
            edge_reader(edges_ref, 0), edge_reader(edges_ref, 1), sequence, edges_ref.shape[0],
            False,
        )
        enter_ref[sequence] = enter
        state = state_ref[sequence] + cum_ref[sequence] * enter
        high, low = two_parts(state)
        place = lax.broadcasted_iota(jnp.int32, (tokens, state.shape[0]), 1)
        for side, at in ((0, end_ref), (1, start_ref)):
            pick = jnp.where(place == at[sequence], 1.0, 0.0).astype(BF16)
            cols = slice(side * GRU_H, (side + 1) * GRU_H)
            out_ref[pl.ds(sequence * tokens, tokens), pl.ds(side * GRU_H, GRU_H)] = matmul(
                pick, high[:, cols]
            ) + matmul(pick, low[:, cols])


def gru_back_kernel(
    real, grad_ref, decay_ref, end_ref, start_ref, spread_ref, cum_ref, carried_ref, edge_ref
):
    rows = decay_ref.shape[1]
    tokens = end_ref.shape[2]
    place = lax.broadcasted_iota(jnp.int32, (rows, tokens), 0)
    high, low = two_parts(grad_ref[0])
    for side, at in ((0, end_ref), (1, start_ref)):
        put = jnp.where(place == at[0], 1.0, 0.0).astype(BF16)
        cols = slice(side * GRU_H, (side + 1) * GRU_H)
        there = pl.ds(side * GRU_H, GRU_H)
        spread = matmul(put, high[:, cols]) + matmul(put, low[:, cols])
        decay = decay_ref[0, :, there]
        cum, carried = scan_rows(decay, decay * spread, side == 0)
        spread_ref[0, :, there] = spread
        cum_ref[0, :, there] = cum
        carried_ref[0, :, there] = carried
        at = real - 1 if side else 0
        store_edges(edge_ref, there, (carried[at : at + 1],))


def gru_grad_kernel(
    real, gate_ref, cand_ref, decay_ref, cum_ref, state_ref, enter_ref,
    spread_ref, back_cum_ref, carried_ref, back_enter_ref, out_ref, bias_ref,
):
    rows = gate_ref.shape[1]
    inside = lax.broadcasted_iota(jnp.int32, (rows, GRU_H), 0) < real
    for side in (0, 1):
        there = pl.ds(side * GRU_H, GRU_H)
        gate = gate_ref[0, :, there]
        cand = cand_ref[0, :, there]
        decay = decay_ref[0, :, there]
        enter = enter_ref[0, :, there]
        back_enter = back_enter_ref[0, :, there]
        state = state_ref[0, :, there] + cum_ref[0, :, there] * enter
        carried = carried_ref[0, :, there] + back_cum_ref[0, :, there] * back_enter
        previous = shift_rows(state, 1, enter, side == 1)
        adjoint = spread_ref[0, :, there] + shift_rows(carried, 1, back_enter, side == 0)
        adjoint = jnp.where(inside, adjoint, 0.0)
        rest = adjoint * (1.0 - gate)
        to_gate = rest * (previous * decay - cand * gate)
        to_cand = rest * (1.0 - cand * cand)
        out_ref[0, :, pl.ds(2 * side * GRU_H, GRU_H)] = to_gate.astype(BF16)
        out_ref[0, :, pl.ds((2 * side + 1) * GRU_H, GRU_H)] = to_cand.astype(BF16)
        bias_ref[0, :, there] = jnp.sum(to_gate, axis=0, keepdims=True)


def per_sequence(*tail):
    return pl.BlockSpec((1,) + tail, lambda s: (s,) + (0,) * len(tail))


def whole_block(*shape):
    return pl.BlockSpec(shape, lambda s: (0,) * len(shape))


def gru_forward(chars, w_gru, bias, start, first, end, last, real):
    batch, rows, width = chars.shape
    tokens = start.shape[2]
    two = 2 * GRU_H
    kept = jax.ShapeDtypeStruct((batch, rows, two), F32)
    return pl.pallas_call(
        functools.partial(gru_forward_kernel, real),
        grid=(batch,),
        in_specs=[per_sequence(rows, width), whole_block(width, w_gru.shape[1]), whole_block(1, two)]
        + [per_sequence(1, tokens)] * 4,
        out_specs=[per_sequence(rows, two)] * 5 + [whole_block(KINDS * batch, two)],
        out_shape=[kept] * 5 + [jax.ShapeDtypeStruct((KINDS * batch, two), F32)],
        compiler_params=params(),
        cost_estimate=cost(
            2 * batch * rows * width * 2 * two,
            chars.size * 2 + w_gru.size * 2 + 20 * batch * rows * two,
            2 * batch * rows * two,
        ),
        name="gru_forward",
    )(chars, w_gru, bias, start, first, end, last)


def gather_states(state, cum, edges, end, start):
    batch, rows, two = state.shape
    tokens = end.shape[1]
    return pl.pallas_call(
        char_tok_kernel,
        out_shape=[
            jax.ShapeDtypeStruct((batch * tokens, two), F32),
            jax.ShapeDtypeStruct((batch, 1, two), F32),
        ],
        compiler_params=params(),
        cost_estimate=cost(
            4 * batch * rows * tokens * two, 8 * batch * rows * two + 4 * batch * tokens * two
        ),
        name="gather_states",
    )(state, cum, edges, end, start)


def gru_back(grad, decay, end, start, real):
    batch, rows, two = decay.shape
    tokens = end.shape[2]
    kept = jax.ShapeDtypeStruct((batch, rows, two), F32)
    return pl.pallas_call(
        functools.partial(gru_back_kernel, real),
        grid=(batch,),
        in_specs=[per_sequence(tokens, two), per_sequence(rows, two)]
        + [per_sequence(1, tokens)] * 2,
        out_specs=[per_sequence(rows, two)] * 3 + [whole_block(KINDS * batch, two)],
        out_shape=[kept] * 3 + [jax.ShapeDtypeStruct((KINDS * batch, two), F32)],
        compiler_params=params(),
        cost_estimate=cost(
            4 * batch * rows * tokens * two, 16 * batch * rows * two + 4 * batch * tokens * two
        ),
        name="gru_back",
    )(grad, decay, end, start)


def gru_grad(gate, cand, decay, cum, state, enter, spread, back_cum, carried, back_enter, real):
    batch, rows, two = decay.shape
    big = per_sequence(rows, two)
    row = per_sequence(1, two)
    return pl.pallas_call(
        functools.partial(gru_grad_kernel, real),
        grid=(batch,),
        in_specs=[big] * 5 + [row] + [big] * 3 + [row],
        out_specs=[per_sequence(rows, 2 * two), row],
        out_shape=[
            jax.ShapeDtypeStruct((batch, rows, 2 * two), BF16),
            jax.ShapeDtypeStruct((batch, 1, two), F32),
        ],
        compiler_params=params(),
        cost_estimate=cost(20 * batch * rows * two, 36 * batch * rows * two),
        name="gru_grad",
    )(gate, cand, decay, cum, state, enter, spread, back_cum, carried, back_enter)


def all_edges(edges):
    return lax.all_gather(edges, "ctx", axis=0)


def entering_kernel(decay_ref, drive_ref, out_ref):
    for sequence in range(out_ref.shape[0]):
        out_ref[sequence] = entering_row(
            edge_reader(decay_ref, 0), edge_reader(drive_ref, 0), sequence, decay_ref.shape[0],
            True,
        )


def back_entering(decays, drives):
    batch, two = decays.shape[1] // KINDS, decays.shape[2]
    return pl.pallas_call(
        entering_kernel,
        out_shape=jax.ShapeDtypeStruct((batch, 1, two), F32),
        compiler_params=params(),
        name="back_entering",
    )(decays, drives)


def attend_kernel(
    heads, tokens, tok_ref, own_ref, core_ref, far_ref, far_core_ref, edge_ref, out_ref, kept_ref,
    query_ref, key_ref, value_ref, w_ref,
):
    part = heads * HEAD_DIM
    rows = out_ref.shape[0]
    step = pl.program_id(0)

    @pl.when(step == 0)
    def build():
        eye = jnp.where(
            lax.broadcasted_iota(jnp.int32, (HEAD_DIM, HEAD_DIM), 0)
            == lax.broadcasted_iota(jnp.int32, (HEAD_DIM, HEAD_DIM), 1),
            1.0,
            0.0,
        ).astype(BF16)
        number = lax.broadcasted_iota(jnp.int32, (HEAD_DIM, tokens), 0).astype(F32)
        shard = own_ref.shape[0]
        for other, piece_ref in enumerate((own_ref, core_ref, far_ref, far_core_ref)):
            at = jnp.bitwise_xor(lax.axis_index("fsdp"), other) * shard
            w_ref[pl.ds(pl.multiple_of(at, shard), shard)] = piece_ref[...]
        ones = jnp.ones((tokens, HEAD_DIM), BF16)

        def block(source, carry):
            qkv = matmul(tok_ref[source, :tokens], w_ref[...])
            ids = tok_ref[source, tokens:].astype(F32)[0:1, :tokens]
            marks = matmul_tn(jnp.where(number == ids, 1.0, 0.0).astype(BF16), eye)
            blocked = ((marks - 1.0) * FAR).astype(BF16)
            marks = marks.astype(BF16)
            here = pl.ds(pl.multiple_of(source * tokens, tokens), tokens)
            for head in range(heads):
                query, key, value = (
                    qkv[:, kind * part + head * HEAD_DIM : kind * part + (head + 1) * HEAD_DIM]
                    for kind in range(3)
                )
                query = query.astype(BF16) * jnp.asarray(HEAD_DIM ** (-0.5), BF16)
                query_ref[head, here] = jnp.concatenate([query, marks], axis=1)
                key_ref[head, here] = jnp.concatenate([key.astype(BF16), blocked], axis=1)
                value_ref[head, here] = jnp.concatenate([value.astype(BF16), ones], axis=1)
            return carry

        lax.fori_loop(0, tok_ref.shape[0], block, 0)

    here = pl.ds(pl.multiple_of(step * rows, rows), rows)
    outs = []
    for head in range(heads):
        expvals = jnp.exp(matmul_nt(query_ref[head, here], key_ref[head]))
        both = matmul(expvals.astype(BF16), value_ref[head])
        total = both[:, HEAD_DIM:]
        context = both[:, :HEAD_DIM] / total
        kept_ref[:, pl.ds(head * 2 * HEAD_DIM, 2 * HEAD_DIM)] = jnp.concatenate(
            [context, total], axis=1
        )
        outs.append(context.astype(BF16))
    block = edges_to_block(edge_ref[...], tokens)
    outs.append(jnp.concatenate([block] * (rows // tokens), axis=0))
    out_ref[...] = jnp.concatenate(outs, axis=1)


def attend_back_kernel(
    heads, tokens, tok_ref, w_ref, query_ref, key_ref, value_ref, kept_ref, grad_ref, edges_ref,
    out_ref, w_grad_ref, enter_ref, grad_scr, edge_scr,
):
    part = heads * HEAD_DIM
    rows = out_ref.shape[0]
    step = pl.program_id(0)

    @pl.when(step == 0)
    def build():
        lane = lax.broadcasted_iota(jnp.int32, (grad_ref.shape[0], HEAD_DIM), 1)
        for head in range(heads):
            at = head * HEAD_DIM
            context = kept_ref[:, 2 * at : 2 * at + HEAD_DIM]
            total = kept_ref[:, 2 * at + HEAD_DIM : 2 * at + 2 * HEAD_DIM]
            grad = grad_ref[:, at : at + HEAD_DIM].astype(F32) / total
            delta = jnp.sum(grad * context, axis=1, keepdims=True)
            high, low = two_parts(-delta)
            extra = jnp.where(
                lane == 0, high.astype(F32), jnp.where(lane == 1, low.astype(F32), 0.0)
            )
            grad_scr[head] = jnp.concatenate([grad, extra], axis=1).astype(BF16)
        for other in range(edges_ref.shape[0]):
            edge_scr[other] = edges_of_block(
                grad_ref[other * tokens : (other + 1) * tokens, part : part + HEAD_DIM]
            )
        for sequence in range(enter_ref.shape[0]):
            enter_ref[sequence] = entering_row(
                edge_reader(edges_ref, 0), edge_reader(edge_scr, 0), sequence,
                edges_ref.shape[0], True,
            )
        w_grad_ref[...] = jnp.zeros_like(w_grad_ref)

    here = pl.ds(pl.multiple_of(step * rows, rows), rows)
    scale = HEAD_DIM ** (-0.5)
    d_query, d_key, d_value = [], [], []
    for head in range(heads):
        expvals = jnp.exp(matmul_nt(query_ref[head, here], key_ref[head]))
        inner = matmul_nt(grad_scr[head, here], value_ref[head])
        d_scores = (expvals * inner).astype(BF16)
        d_query.append((matmul(d_scores, key_ref[head])[:, :HEAD_DIM] * scale).astype(BF16))
        expvals = jnp.exp(matmul_nt(key_ref[head, here], query_ref[head]))
        inner = matmul_nt(value_ref[head, here], grad_scr[head])
        d_scores = (expvals * inner).astype(BF16)
        d_key.append(matmul(d_scores, query_ref[head])[:, :HEAD_DIM].astype(BF16))
        d_value.append(
            matmul(expvals.astype(BF16), grad_scr[head])[:, :HEAD_DIM].astype(BF16)
        )
    d_qkv = jnp.concatenate(d_query + d_key + d_value, axis=1)
    out_ref[...] = matmul_nt(d_qkv, w_ref[...]).astype(BF16)
    blocks = rows // tokens
    tok = jnp.concatenate(
        [tok_ref[step * blocks + block, :tokens] for block in range(blocks)], axis=0
    )
    w_grad_ref[...] += matmul_tn(tok, d_qkv)


def unpack_kernel(groups, part, in_ref, out_ref, edge_ref):
    for group in range(groups):
        edge_ref[group] = edges_of_block(in_ref[group, :, part:])
    out_ref[...] = jnp.concatenate([in_ref[group, :, :part] for group in range(groups)], axis=1)


def spread_columns_kernel(heads, in_ref, out_ref):
    groups, part = in_ref.shape[0], heads * HEAD_DIM
    width = groups * part
    mine = lax.rem(lax.axis_index("ctx"), groups)
    for case in range(groups):

        @pl.when(mine == case)
        def place():
            for kind in range(3):
                pieces = [
                    in_ref[case ^ group, :, kind * part : (kind + 1) * part].astype(F32)
                    for group in range(groups)
                ]
                out_ref[:, pl.ds(kind * width, width)] = jnp.concatenate(pieces, axis=1)


def send_grad_kernel(groups, part, grad_ref, w_ref, edge_ref, out_ref):
    d_context = matmul_nt(grad_ref[...], w_ref[...]).astype(BF16)
    block = edges_to_block(edge_ref[...], grad_ref.shape[0])
    for group in range(groups):
        out_ref[group] = jnp.concatenate(
            [d_context[:, group * part : (group + 1) * part], block], axis=1
        )


def heads_here(batch, count):
    if batch * HEADS % count != 0 or not routed():
        return 0
    heads = batch * HEADS // count
    if heads > HEADS or HEADS % heads != 0 or heads % 2 == 0 or batch * KINDS != 8:
        return 0
    return heads


def attend(tokens_all, w_pieces, edges, heads, tokens):
    count, rows, width = tokens_all.shape
    length = count * tokens
    block = 256
    part = heads * HEAD_DIM
    out_wide = part + HEAD_DIM
    wide = jax.ShapeDtypeStruct((heads, length, 2 * HEAD_DIM), BF16)
    return pl.pallas_call(
        functools.partial(attend_kernel, heads, tokens),
        grid=(length // block,),
        in_specs=[
            pl.BlockSpec((count, rows, width), lambda i: (0, 0, 0)),
        ]
        + [pl.BlockSpec(w_pieces[0].shape, lambda i: (0, 0))] * 4
        + [pl.BlockSpec(edges.shape, lambda i: (0, 0))],
        out_specs=[
            pl.BlockSpec((block, out_wide), lambda i: (i, 0)),
            pl.BlockSpec((block, 2 * part), lambda i: (i, 0)),
        ]
        + [pl.BlockSpec(wide.shape, lambda i: (0, 0, 0))] * 3
        + [pl.BlockSpec((width, 3 * part), lambda i: (0, 0))],
        out_shape=[
            jax.ShapeDtypeStruct((length, out_wide), BF16),
            jax.ShapeDtypeStruct((length, 2 * part), F32),
            wide,
            wide,
            wide,
            jax.ShapeDtypeStruct((width, 3 * part), BF16),
        ],
        compiler_params=params(),
        cost_estimate=cost(
            8 * heads * length * length * HEAD_DIM,
            length * (width * 2 + out_wide * 2 + 8 * part),
            heads * length * length,
        ),
        name="attend",
    )(tokens_all, *w_pieces, edges)


def attend_back(tokens_all, w_heads, saved, kept, grads, edges, heads, tokens):
    count, rows, width = tokens_all.shape
    length = count * tokens
    block = 256
    part = heads * HEAD_DIM
    batch, two = edges.shape[1] // KINDS, edges.shape[2]
    wide = (heads, length, 2 * HEAD_DIM)
    return pl.pallas_call(
        functools.partial(attend_back_kernel, heads, tokens),
        grid=(length // block,),
        in_specs=[
            pl.BlockSpec((count, rows, width), lambda i: (0, 0, 0)),
            pl.BlockSpec(w_heads.shape, lambda i: (0, 0)),
        ]
        + [pl.BlockSpec(wide, lambda i: (0, 0, 0))] * 3
        + [
            pl.BlockSpec((length, 2 * part), lambda i: (0, 0)),
            pl.BlockSpec((length, part + HEAD_DIM), lambda i: (0, 0)),
            pl.BlockSpec(edges.shape, lambda i: (0, 0, 0)),
        ],
        out_specs=[
            pl.BlockSpec((block, width), lambda i: (i, 0)),
            pl.BlockSpec(w_heads.shape, lambda i: (0, 0)),
            pl.BlockSpec((batch, 1, two), lambda i: (0, 0, 0)),
        ],
        out_shape=[
            jax.ShapeDtypeStruct((length, width), BF16),
            jax.ShapeDtypeStruct(w_heads.shape, F32),
            jax.ShapeDtypeStruct((batch, 1, two), F32),
        ],
        scratch_shapes=[pltpu.VMEM(wide, BF16), pltpu.VMEM(edges.shape, F32)],
        compiler_params=params(),
        cost_estimate=cost(
            28 * heads * length * length * HEAD_DIM,
            length * (width * 4 + 8 * part + 2 * part),
            2 * heads * length * length,
        ),
        name="attend_back",
    )(tokens_all, w_heads, *saved, kept, grads, edges)


def unpack(received, heads, batch):
    count, rows, wide = received.shape
    groups, part = HEADS // heads, heads * HEAD_DIM
    width = groups * part
    return pl.pallas_call(
        functools.partial(unpack_kernel, groups, part),
        grid=(batch,),
        in_specs=[pl.BlockSpec((groups, rows, wide), lambda s: (s, 0, 0))],
        out_specs=[
            pl.BlockSpec((rows, width), lambda s: (s, 0)),
            pl.BlockSpec((groups, KINDS * batch, 2 * GRU_H), lambda s: (s, 0, 0)),
        ],
        out_shape=[
            jax.ShapeDtypeStruct((batch * rows, width), BF16),
            jax.ShapeDtypeStruct((count, KINDS * batch, 2 * GRU_H), F32),
        ],
        compiler_params=params(),
        cost_estimate=cost(0, 2 * received.size + 2 * batch * rows * width),
        name="unpack",
    )(received)


def spread_columns(pieces, heads):
    groups, rows, wide = pieces.shape
    return pl.pallas_call(
        functools.partial(spread_columns_kernel, heads),
        out_shape=jax.ShapeDtypeStruct((rows, groups * wide), F32),
        compiler_params=params(),
        cost_estimate=cost(1, 1),
        name="spread_columns",
    )(pieces)


def send_grad(d_attn, w_out, edges, heads, batch):
    total, width = d_attn.shape
    rows = total // batch
    groups, part = HEADS // heads, heads * HEAD_DIM
    wide = part + HEAD_DIM
    return pl.pallas_call(
        functools.partial(send_grad_kernel, groups, part),
        grid=(batch,),
        in_specs=[
            pl.BlockSpec((rows, width), lambda s: (s, 0)),
            whole_block(width, width),
            whole_block(*edges.shape),
        ],
        out_specs=pl.BlockSpec((groups, rows, wide), lambda s: (s, 0, 0)),
        out_shape=jax.ShapeDtypeStruct((batch * groups, rows, wide), BF16),
        compiler_params=params(),
        cost_estimate=cost(
            2 * total * width * width, 2 * (d_attn.size + w_out.size + total * groups * wide)
        ),
        name="send_grad",
    )(d_attn, w_out, edges)


def feed_forward_kernel(hidden_ref, w_ref, bias_ref, inner_ref, slope_ref):
    pre = matmul(hidden_ref[...], w_ref[...]) + bias_ref[...]
    at = jnp.abs(pre) * (0.5**0.5)
    near = 1.0 / (1.0 + 0.3275911 * at)
    gauss = jnp.exp(-at * at)
    series = 1.061405429
    for term in (-1.453152027, 1.421413741, -0.284496736, 0.254829592):
        series = series * near + term
    tail = 0.5 * series * near * gauss
    below = jnp.where(pre < 0.0, tail, 1.0 - tail)
    inner_ref[...] = (pre * below).astype(BF16)
    slope_ref[...] = (below + pre * gauss * (2.0 * jnp.pi) ** -0.5).astype(BF16)


def feed_forward(hidden, w_up, bias):
    rows, width = hidden.shape
    wide = w_up.shape[1]
    block = 512
    column = pl.BlockSpec((rows, block), lambda i: (0, i))
    return pl.pallas_call(
        feed_forward_kernel,
        grid=(wide // block,),
        in_specs=[
            whole_block(rows, width),
            pl.BlockSpec((width, block), lambda i: (0, i)),
            pl.BlockSpec((1, block), lambda i: (0, i)),
        ],
        out_specs=[column, column],
        out_shape=[jax.ShapeDtypeStruct((rows, wide), BF16)] * 2,
        compiler_params=params(),
        cost_estimate=cost(
            2 * rows * width * wide, 2 * (hidden.size + w_up.size + 2 * rows * wide), rows * wide
        ),
        name="feed_forward",
    )(hidden, w_up, bias)


def gradients_kernel(
    blocks, hidden1_ref, context_ref, hidden2_ref, char_ref, pre_ref, attn_ref, joined_ref, out_ref
):
    step = pl.program_id(0)
    width = hidden2_ref.shape[1]

    def put(at, left_ref, right):
        @pl.when((step < blocks) if at is None else (step == blocks + at))
        def store():
            out_ref[...] = matmul_tn(left_ref[...], right()).astype(BF16)

    put(None, hidden1_ref, lambda: pre_ref[...])
    put(0, context_ref, lambda: attn_ref[...])
    put(1, hidden2_ref, lambda: joined_ref[:, :width])
    put(2, char_ref, lambda: joined_ref[:, width:])


def gradients(hidden1, context, hidden2, chars, d_pre, d_attn, d_joined):
    rows, width = hidden1.shape
    blocks = d_pre.shape[1] // width
    whole = whole_block(rows, width)
    return pl.pallas_call(
        functools.partial(gradients_kernel, blocks),
        grid=(blocks + 3,),
        in_specs=[whole] * 4
        + [
            pl.BlockSpec((rows, width), lambda i: (0, jnp.minimum(i, blocks - 1))),
            whole,
            whole_block(rows, 2 * width),
        ],
        out_specs=pl.BlockSpec((width, width), lambda i: (0, i)),
        out_shape=jax.ShapeDtypeStruct((width, (blocks + 3) * width), BF16),
        compiler_params=params(),
        cost_estimate=cost(1, 1),
        name="gradients",
    )(hidden1, context, hidden2, chars, d_pre, d_attn, d_joined)


def down_grad_kernel(own_ref, core_ref, far_ref, far_core_ref, grad_ref, out_ref):
    total = jnp.zeros(out_ref.shape, F32)
    for other, inner_ref in enumerate((own_ref, core_ref, far_ref, far_core_ref)):
        source = jnp.bitwise_xor(lax.axis_index("fsdp"), other)
        total = total + matmul_tn(inner_ref[...], grad_ref[source])
    out_ref[...] = total.astype(BF16)


def down_gradient(inner, grads):
    return pl.pallas_call(
        down_grad_kernel,
        out_shape=jax.ShapeDtypeStruct((inner[0].shape[1], grads.shape[2]), BF16),
        compiler_params=params(),
        cost_estimate=cost(1, 1),
        name="down_gradient",
    )(*inner, grads)


def conv_grad_kernel(
    own_ref, core_ref, far_ref, far_core_ref, grad_ref, keep_ref, send_ref, side_scr
):
    tap = pl.program_id(0)
    refs = (own_ref, core_ref, far_ref, far_core_ref)
    batch = grad_ref.shape[0] // len(refs)
    rows = side_scr.shape[0] // batch
    shape = (rows, grad_ref.shape[2])
    row = lax.broadcasted_iota(jnp.int32, shape, 0)
    total = jnp.zeros((own_ref.shape[1], grad_ref.shape[2]), F32)
    for other, joined_ref in enumerate(refs):
        first = jnp.bitwise_xor(lax.axis_index("fsdp"), other) * batch
        for block in range(batch):
            here = pl.ds(block * rows, rows)
            grad = grad_ref[first + block].astype(F32)
            mid = grad[:rows]

            @pl.when(tap == 0)
            def earlier():
                moved = pltpu.roll(mid, rows - 1, 0)
                last = jnp.broadcast_to(grad[rows + 1 : rows + 2], shape)
                side_scr[here] = jnp.where(row == rows - 1, last, moved).astype(BF16)

            @pl.when(tap == 1)
            def same():
                side_scr[here] = mid.astype(BF16)

            @pl.when(tap == 2)
            def later():
                moved = pltpu.roll(mid, 1, 0)
                before = jnp.broadcast_to(grad[rows : rows + 1], shape)
                side_scr[here] = jnp.where(row == 0, before, moved).astype(BF16)

        total = total + matmul_tn(joined_ref[...], side_scr[...])
    half = keep_ref.shape[1]
    halves = (total[:half].astype(BF16), total[half:].astype(BF16))
    for mine in (0, 1):

        @pl.when(lax.rem(lax.axis_index("ctx"), 2) == mine)
        def store():
            keep_ref[0] = halves[mine]
            send_ref[0] = halves[1 - mine]


def conv_gradient(joined, grads, rows, part):
    count, tall, wide = grads.shape
    wide = wide // 2
    own = joined[0].shape
    out = jax.ShapeDtypeStruct((3, own[1] // 2, wide), BF16)
    return pl.pallas_call(
        conv_grad_kernel,
        grid=(3,),
        in_specs=[pl.BlockSpec(own, lambda k: (0, 0))] * 4
        + [pl.BlockSpec((count, tall, wide), lambda k: (0, 0, part))],
        out_specs=[pl.BlockSpec((1,) + out.shape[1:], lambda k: (k, 0, 0))] * 2,
        out_shape=[out, out],
        scratch_shapes=[pltpu.VMEM((own[0], wide), BF16)],
        compiler_params=params(),
        cost_estimate=cost(1, 1),
        name="conv_gradient",
    )(*joined, grads)


def last_grads_kernel(chars_ref, gates_ref, small_ref, heads_ref, out_ref):
    wide = gates_ref.shape[1]
    narrow = small_ref.shape[1]
    out_ref[:, :wide] = matmul_tn(chars_ref[...], gates_ref[...]).astype(BF16)
    out_ref[:, wide : wide + narrow] = small_ref[...].astype(BF16)
    out_ref[:, wide + narrow :] = heads_ref[...].astype(BF16)


def last_gradients(chars, d_gates, small, heads_grad):
    width = chars.shape[1]
    wide = d_gates.shape[1] + small.shape[1] + heads_grad.shape[1]
    return pl.pallas_call(
        last_grads_kernel,
        out_shape=jax.ShapeDtypeStruct((width, wide), BF16),
        compiler_params=params(),
        cost_estimate=cost(1, 1),
        name="last_gradients",
    )(chars, d_gates, small, heads_grad)


def block_size(rows):
    size = min(rows, BLOCK_LIMIT)
    while rows % size != 0:
        size = size - 1
    return size


def split_blocks(array, size):
    return array.reshape((array.shape[0] // size, size) + array.shape[1:])


def to_heads(matrix):
    return matrix.reshape(matrix.shape[0], HEADS, HEAD_DIM)


def masked_exp(query_heads, key_heads, query_seg, key_seg):
    scores = jnp.einsum(
        "qhd,khd->hqk", query_heads, key_heads, preferred_element_type=F32
    ) * HEAD_DIM ** (-0.5)
    same = (query_seg[:, None] == key_seg[None, :])[None, :, :]
    return jnp.where(same, jnp.exp(scores), 0.0)


def everyone(rows):
    return lax.all_gather(rows, "ctx", axis=0, tiled=True)


def gathered_attention(qkv, seg_row):
    tok_rows, width = qkv.shape[0], qkv.shape[1] // 3
    query_heads = to_heads(qkv[:, :width])
    pieces = (everyone(qkv[:, width : 2 * width]), everyone(qkv[:, 2 * width :]), everyone(seg_row))
    size = block_size(pieces[0].shape[0])

    def step(acc, item):
        key_block, value_block, seg_block = item
        expvals = masked_exp(query_heads, to_heads(key_block), seg_row, seg_block)
        part_num = jnp.einsum(
            "hqk,khd->qhd", expvals.astype(BF16), to_heads(value_block),
            preferred_element_type=F32,
        )
        return ((acc[0] + part_num, acc[1] + jnp.transpose(jnp.sum(expvals, axis=-1))), None)

    (numer, total), unused = lax.scan(
        step,
        (jnp.zeros((tok_rows, HEADS, HEAD_DIM), F32), jnp.zeros((tok_rows, HEADS), F32)),
        tuple(split_blocks(piece, size) for piece in pieces),
    )
    return numer / total[:, :, None], total


def gathered_attention_back(qkv, seg_row, context, total, d_context):
    tok_rows, width = qkv.shape[0], qkv.shape[1] // 3
    scale = HEAD_DIM ** (-0.5)
    d_context = to_heads(d_context)
    query_rows, key_rows, value_rows = (qkv[:, i * width : (i + 1) * width] for i in range(3))
    grad_heads = (d_context / total[:, :, None]).astype(BF16)
    delta = jnp.sum(d_context * context, axis=-1) / total
    key_heads, value_heads, query_heads = (
        to_heads(key_rows), to_heads(value_rows), to_heads(query_rows)
    )
    zero_heads = jnp.zeros((tok_rows, HEADS, HEAD_DIM), F32)
    seg_all = everyone(seg_row)
    size = block_size(seg_all.shape[0])

    def key_step(acc, item):
        query_block, grad_block, delta_block, seg_block = item
        query_h, grad_h = to_heads(query_block), to_heads(grad_block)
        expvals = masked_exp(query_h, key_heads, seg_block, seg_row)
        dprob = jnp.einsum("qhd,khd->hqk", grad_h, value_heads, preferred_element_type=F32)
        dscore = (expvals * (dprob - jnp.transpose(delta_block)[:, :, None])).astype(BF16)
        dkey = acc[0] + scale * jnp.einsum(
            "hqk,qhd->khd", dscore, query_h, preferred_element_type=F32
        )
        dval = acc[1] + jnp.einsum(
            "hqk,qhd->khd", expvals.astype(BF16), grad_h, preferred_element_type=F32
        )
        return ((dkey, dval), None)

    (dkey, dval), unused = lax.scan(
        key_step,
        (zero_heads, zero_heads),
        tuple(
            split_blocks(piece, size)
            for piece in (
                everyone(query_rows),
                everyone(grad_heads.reshape(tok_rows, width)),
                everyone(delta),
                seg_all,
            )
        ),
    )

    def query_step(acc, item):
        key_block, value_block, seg_block = item
        key_h = to_heads(key_block)
        expvals = masked_exp(query_heads, key_h, seg_row, seg_block)
        dprob = jnp.einsum(
            "qhd,khd->hqk", grad_heads, to_heads(value_block), preferred_element_type=F32
        )
        dscore = (expvals * (dprob - jnp.transpose(delta)[:, :, None])).astype(BF16)
        return (
            acc + scale * jnp.einsum("hqk,khd->qhd", dscore, key_h, preferred_element_type=F32),
            None,
        )

    dquery, unused = lax.scan(
        query_step,
        zero_heads,
        tuple(
            split_blocks(piece, size)
            for piece in (everyone(key_rows), everyone(value_rows), seg_all)
        ),
    )
    return jnp.concatenate(
        [part.reshape(tok_rows, width) for part in (dquery, dkey, dval)], axis=1
    ).astype(BF16)


def neighbours(rows):
    count = lax.axis_size("ctx")
    up = [(i, i + 1) for i in range(count - 1)]
    down = [(j, i) for i, j in up]
    before = lax.ppermute(rows[:, -1], "ctx", up)
    after = lax.ppermute(rows[:, 0], "ctx", down)
    return before[:, None], after[:, None]


def shifted(rows, before, after):
    later = jnp.concatenate([before, rows[:, :-1]], axis=1)
    earlier = jnp.concatenate([rows[:, 1:], after], axis=1)
    return later, earlier


def routed():
    return lax.axis_size("ctx") == 8 and lax.axis_size("fsdp") == 4


STEPS = (1, 2, 4)
OTHER_STEPS = (1, 4, 2)
ORDER = "DABXDABTABXDTABDXTGKDTGKDTGKABTGKDGGTG"


def flip(value, axis, bit):
    return lax.ppermute(value, axis, [(i, i ^ bit) for i in range(lax.axis_size(axis))])


def slot(steps=STEPS):
    me = lax.axis_index("ctx")
    first, second, third = ((me // bit) % 2 for bit in steps)
    return first * 4 + second * 2 + third


def own_columns(value):
    count, mine = lax.axis_size("fsdp"), lax.axis_index("fsdp")
    wide = value.shape[1] // count
    pieces = []
    for other in range(count):
        piece = lax.dynamic_slice_in_dim(value, jnp.bitwise_xor(mine, other) * wide, wide, 1)
        pieces.append(flip(piece, "fsdp", other) if other else piece)
    return pieces


class CtxSum:
    def __init__(self, value, steps=STEPS):
        self.value = value
        self.axis = value.ndim - 2
        self.stage = 0
        self.steps = steps

    @classmethod
    def begun(cls, keep, send, steps=STEPS):
        chain = cls(keep, steps)
        chain.keep = keep
        chain.send(send, steps[0])
        chain.stage = 1
        return chain

    def halve(self, value, bit):
        mine = (lax.axis_index("ctx") // bit) % 2
        half = value.shape[self.axis] // 2
        send = lax.dynamic_slice_in_dim(value, (1 - mine) * half, half, self.axis)
        self.keep = lax.dynamic_slice_in_dim(value, mine * half, half, self.axis)
        self.send(send, bit)

    def send(self, value, bit):
        self.sent = value
        self.got = flip(value, "ctx", bit)

    def advance(self, *others):
        stage = self.stage
        self.stage = stage + 1
        if stage == 0:
            self.halve(after(self.value, *others), self.steps[0])
        elif stage <= 3:
            got = after(self.got, *others).astype(F32)
            piece = (self.keep.astype(F32) + got).astype(BF16)
            if stage < 3:
                self.halve(piece, self.steps[stage])
            else:
                self.send(piece[None], self.steps[2])
        else:
            piece = jnp.concatenate([self.sent, after(self.got, *others)], axis=0)
            if stage < 6:
                self.send(piece, self.steps[5 - stage])
            else:
                self.result = self.sent = piece
        return self.sent


class HeadSum(CtxSum):
    def advance(self, *others):
        stage = self.stage
        self.stage = stage + 1
        if stage == 0:
            self.send(after(self.value, *others), 4)
        elif stage == 1:
            piece = self.sent.astype(F32) + after(self.got, *others).astype(F32)
            self.send(piece.astype(BF16)[None], 1)
        else:
            piece = jnp.concatenate([self.sent, after(self.got, *others)], axis=0)
            if stage == 2:
                self.send(piece, 2)
            else:
                self.result = self.sent = piece
        return self.sent


class TokenSum(CtxSum):
    def advance(self, *others):
        me = lax.axis_index("ctx")
        stage = self.stage
        self.stage = stage + 1
        if stage == 0:
            piece = after(self.value, *others)
        else:
            got = after(self.got, *others).astype(F32)
            if stage == 3:
                keep = self.keep.astype(F32)
                ordered = (jnp.concatenate([keep, got]), jnp.concatenate([got, keep]))
                self.result = self.sent = jnp.where(me // 4 == 0, *ordered)
                return self.sent
            piece = (self.keep.astype(F32) + got).astype(BF16)
            piece = jnp.squeeze(piece, axis=3 - stage)
        bit = STEPS[stage]
        mine = (me // bit) % 2
        axis = 2 - stage
        self.keep = lax.dynamic_slice_in_dim(piece, mine, 1, axis)
        self.send(lax.dynamic_slice_in_dim(piece, 1 - mine, 1, axis), bit)
        return self.sent


def run_in_order(chains, finish, ready):
    last, done = (), {}
    for event, name in enumerate(ORDER):
        chain = chains[name]
        others = last
        if event == ORDER.index("T"):
            others = others + (ready,)
        if event == len(ORDER) - 3:
            others = others + tuple(done["D"]) + (done["K"],)
        last = (chain.advance(*others),)
        if hasattr(chain, "result"):
            done[name] = finish[name](chain.result)
    return done


def settle_kernel(order_ref, in_ref, *out_refs):
    at = 0
    for out_ref in out_refs:
        wide = out_ref.shape[-1]
        out_ref[...] = in_ref[0, ..., at : at + wide].astype(F32)
        at = at + wide


def settle_half_kernel(order_ref, in_ref, *refs):
    refs[-1][...] = in_ref[0].astype(F32)


def settle_half(pieces, steps, part, whole=None):
    lead = pieces.shape[1:-2]
    rows, width = pieces.shape[-2:]
    none = (0,) * len(lead)
    order = jnp.bitwise_xor(slot(steps), jnp.arange(8, dtype=jnp.int32))
    given = [] if whole is None else [whole]
    return pl.pallas_call(
        settle_half_kernel,
        grid_spec=pltpu.PrefetchScalarGridSpec(
            num_scalar_prefetch=1,
            grid=(8,),
            in_specs=[
                pl.BlockSpec((1,) + lead + (rows, width), lambda r, o: (r,) + none + (0, 0))
            ]
            + [pl.BlockSpec(memory_space=pl.ANY)] * len(given),
            out_specs=pl.BlockSpec(lead + (rows, width), lambda r, o: none + (o[r], part)),
        ),
        out_shape=jax.ShapeDtypeStruct(lead + (8 * rows, 2 * width), F32),
        input_output_aliases={2: 0} if given else {},
        compiler_params=params(),
        cost_estimate=cost(1, 1),
        name="settle_half",
    )(order, pieces, *given)


def settle(pieces, widths):
    lead = pieces.shape[1:-2]
    rows, total = pieces.shape[-2:]
    order = jnp.bitwise_xor(slot(), jnp.arange(8, dtype=jnp.int32))
    none = (0,) * len(lead)
    return pl.pallas_call(
        settle_kernel,
        grid_spec=pltpu.PrefetchScalarGridSpec(
            num_scalar_prefetch=1,
            grid=(8,),
            in_specs=[
                pl.BlockSpec((1,) + lead + (rows, total), lambda r, o: (r,) + none + (0, 0))
            ],
            out_specs=[
                pl.BlockSpec(lead + (rows, width), lambda r, o: none + (o[r], 0))
                for width in widths
            ],
        ),
        out_shape=[jax.ShapeDtypeStruct(lead + (8 * rows, width), F32) for width in widths],
        compiler_params=params(),
        cost_estimate=cost(pieces.size, 6 * pieces.size),
        name="settle",
    )(order, pieces)


def move(sources, stages, targets, arrived, left):
    ins = [
        pltpu.make_async_copy(source, stage, arrived.at[i])
        for i, (source, stage) in enumerate(zip(sources, stages))
    ]
    for copy in ins:
        copy.start()
    outs = []
    for i, (copy, stage, target) in enumerate(zip(ins, stages, targets)):
        copy.wait()
        outs.append(pltpu.make_async_copy(stage, target, left.at[i]))
        outs[-1].start()
    for copy in outs:
        copy.wait()


def place_own_kernel(spans, own_ref, core_ref, *rest):
    outs, (own_scr, core_scr, arrived, left) = rest[:-4], rest[-4:]
    mine = lax.axis_index("fsdp")
    sources, stages, targets, at = [], [], [], 0
    for span, out_ref in zip(spans, outs):
        there = pl.ds(at, span)
        for ref, scr, shard in (
            (own_ref, own_scr, mine),
            (core_ref, core_scr, jnp.bitwise_xor(mine, 1)),
        ):
            sources.append(ref.at[there])
            stages.append(scr.at[there])
            targets.append(out_ref.at[shard])
        at = at + span
    move(sources, stages, targets, arrived, left)


def place_kernel(spans, order, piece_ref, core_ref, *rest):
    outs, (piece_scr, core_scr, arrived, left) = rest[len(spans) : -4], rest[-4:]
    place = slot()
    mine = lax.axis_index("fsdp")
    sources, stages, targets = [], [], []
    for ref, scr, shard in (
        (piece_ref, piece_scr, jnp.bitwise_xor(mine, 2)),
        (core_ref, core_scr, jnp.bitwise_xor(mine, 3)),
    ):
        for position, other in enumerate(order):
            at = 0
            for span, out_ref in zip(spans, outs):
                part = span // 8
                there = pl.multiple_of(jnp.bitwise_xor(place, other) * part, part)
                sources.append(ref.at[position, pl.ds(at, part)])
                stages.append(scr.at[position, pl.ds(at, part)])
                targets.append(out_ref.at[shard, pl.ds(there, part)])
                at = at + part
    move(sources, stages, targets, arrived, left)


def after(value, *others):
    return lax.optimization_barrier((value,) + others)[0]


class SpreadGather:
    def __init__(self, shards):
        self.spans = tuple(shard.shape[0] for shard in shards)
        self.width = shards[0].shape[1]
        place = slot()
        self.own = jnp.concatenate(shards, axis=0) if len(shards) > 1 else shards[0]
        piece = [
            lax.dynamic_slice_in_dim(shard, place * (span // 8), span // 8, 0)
            for shard, span in zip(shards, self.spans)
        ]
        self.base = None
        self.got = flip(jnp.concatenate(piece, axis=0), "fsdp", 2)[None]
        self.core = flip(self.own, "fsdp", 1)
        self.order = [0]

    def take(self, others):
        got = after(self.got, *others) if others else self.got
        return got if self.base is None else jnp.concatenate([self.base, got], axis=0)

    def double(self, bit, *others):
        self.base = self.take(others)
        self.got = flip(self.base, "ctx", bit)
        self.order = self.order + [other ^ (4 // bit) for other in self.order]

    def cores(self, *others):
        self.piece = self.take(others)
        self.core_piece = flip(self.piece, "fsdp", 1)

    def place_own(self, *others):
        spans, width = self.spans, self.own.shape[1]
        self.whole = pl.pallas_call(
            functools.partial(place_own_kernel, spans),
            in_specs=[pl.BlockSpec(memory_space=pl.ANY)] * 2,
            out_specs=[pl.BlockSpec(memory_space=pl.ANY)] * len(spans),
            out_shape=[jax.ShapeDtypeStruct((4, span, width), BF16) for span in spans],
            scratch_shapes=[pltpu.VMEM(self.own.shape, BF16)] * 2
            + [pltpu.SemaphoreType.DMA((2 * len(spans),))] * 2,
            compiler_params=params(),
            cost_estimate=cost(0, 8 * sum(spans) * width),
            name="place_own",
        )(after(self.own, *others), self.core)

    def finish(self):
        spans, width = self.spans, self.own.shape[1]
        anywhere = [pl.BlockSpec(memory_space=pl.ANY)] * len(spans)
        return pl.pallas_call(
            functools.partial(place_kernel, spans, self.order),
            in_specs=[pl.BlockSpec(memory_space=pl.ANY)] * 2 + anywhere,
            out_specs=anywhere,
            out_shape=[jax.ShapeDtypeStruct((4, span, width), BF16) for span in spans],
            scratch_shapes=[pltpu.VMEM(self.piece.shape, BF16)] * 2
            + [pltpu.SemaphoreType.DMA((16 * len(spans),))] * 2,
            input_output_aliases={2 + i: i for i in range(len(spans))},
            compiler_params=params(),
            cost_estimate=cost(0, 8 * sum(spans) * width),
            name="place",
        )(self.piece, self.core_piece, *self.whole)


def over_fsdp(grads):
    return lax.psum_scatter(grads, "fsdp", scatter_dimension=0, tiled=True)


def plain_sum(grads, axis=0):
    share = lax.psum_scatter(grads, "fsdp", scatter_dimension=axis, tiled=True)
    return lax.psum(share.astype(F32), "ctx")


def local(
    tokens, chars, segment, char_end, w_qkv, w_out, norm1_gain, norm1_bias, w_up, b_up, w_down,
    norm2_gain, norm2_bias, w_gru, b_gate, w_ftok, w_fchr, w_conv, norm3_gain, norm3_bias,
    norm4_gain, norm4_bias, d_token, d_char,
):
    count, me = lax.axis_size("ctx"), lax.axis_index("ctx")
    shards = lax.axis_size("fsdp")
    batch, rows, width = tokens.shape
    char_rows = chars.shape[1]
    total_rows = batch * rows
    heads = heads_here(batch, count)
    padded_rows = -(-char_rows // 8) * 8

    def gather(weight, axis=0):
        return lax.all_gather(weight, "fsdp", axis=axis, tiled=True)

    own_width = norm1_gain.shape[0]
    vectors = (
        norm1_gain, norm1_bias, norm2_gain, norm2_bias, b_gate, norm3_gain, norm3_bias,
        norm4_gain, norm4_bias,
    )
    columns = jnp.stack(vectors, axis=1)
    columns = jnp.concatenate([columns, b_up.reshape(-1, own_width).T], axis=1)
    small_count = columns.shape[1]
    wide_gru = w_gru.shape[1]
    columns = jnp.pad(columns, ((0, 0), (0, 128 - small_count)))
    width_qkv = w_qkv.shape[1]
    if heads:
        group, part = me % (HEADS // heads), heads * HEAD_DIM
        w_heads = jnp.concatenate(
            [
                lax.dynamic_slice_in_dim(w_qkv, kind * width + group * part, part, 1)
                for kind in range(3)
            ],
            axis=1,
        )
        w_pieces = [w_heads] + [flip(w_heads, "fsdp", other) for other in (1, 2, 3)]
    else:
        w_qkv = gather(w_qkv)
    w_gru = gather(jnp.concatenate([w_gru, columns], axis=1))
    w_out = gather(w_out)
    w_up = gather(w_up)
    columns = w_gru[:, wide_gru : wide_gru + small_count].astype(F32)
    (
        norm1_gain, norm1_bias, norm2_gain, norm2_bias, b_gate, norm3_gain, norm3_bias,
        norm4_gain, norm4_bias,
    ) = (columns[:, i][None, :] for i in range(9))
    b_up = jnp.swapaxes(columns[:, 9:].reshape(shards, own_width, -1), 1, 2).reshape(1, -1)
    w_down = gather(w_down)
    if routed():
        first_taps = SpreadGather([w_conv[0], w_conv[1]])
        last_tap = SpreadGather([w_conv[2], jnp.concatenate([w_ftok, w_fchr], axis=1)])
    else:
        w_ftok = gather(w_ftok)
        w_fchr = gather(w_fchr)
        w_conv = gather(w_conv, 1)

    start = jnp.concatenate([jnp.zeros((batch, 1), jnp.int32), char_end[:, :-1] + 1], axis=1)
    change = (segment[:, 1:] != segment[:, :-1]).astype(F32)
    first = jnp.concatenate([jnp.broadcast_to((me == 0).astype(F32), (batch, 1)), change], axis=1)
    last = jnp.concatenate(
        [change, jnp.broadcast_to((me == count - 1).astype(F32), (batch, 1))], axis=1
    )
    flat_tokens = tokens.reshape(total_rows, width)
    chars_pad = jnp.pad(chars, ((0, 0), (0, padded_rows - char_rows), (0, 0)))
    if routed():
        first_taps.double(4)
        last_tap.double(1)
    gate, cand, decay, cum, state, edges = gru_forward(
        chars_pad, w_gru, b_gate, start[:, None], first[:, None], char_end[:, None],
        last[:, None], char_rows,
    )

    if heads:
        ids = segment.astype(BF16)[:, None, :]
        ids = jnp.pad(ids, ((0, 0), (0, 7), (0, width - rows)))
        sent = jnp.repeat(jnp.concatenate([tokens, ids], axis=1), HEADS // heads, axis=0)
        tokens_all = lax.all_to_all(sent, "ctx", 0, 0, tiled=True)
        packed_context, kept, *saved, w_heads = attend(tokens_all, w_pieces, edges, heads, rows)
        first_taps.double(2, state)
        last_tap.double(4, state)
        first_taps.place_own(packed_context)
        last_tap.place_own(packed_context)
        received = lax.all_to_all(packed_context.reshape(count, rows, -1), "ctx", 0, 0, tiled=True)
        received = after(received, *first_taps.whole, *last_tap.whole)
        context_b, edges_all = unpack(received, heads, batch)
    else:
        qkv = matmul(flat_tokens, w_qkv).astype(BF16).reshape(batch, rows, -1)
        results = [gathered_attention(qkv[i], segment[i]) for i in range(batch)]
        context_b = jnp.concatenate([r[0].reshape(rows, width) for r in results]).astype(BF16)
        edges_all = all_edges(edges)

    attn = matmul(context_b, w_out)
    hidden1, kept1 = layer_norm(flat_tokens.astype(F32) + attn, norm1_gain, norm1_bias)
    hidden1_b = hidden1.astype(BF16)
    inner_b, slope = feed_forward(hidden1_b, w_up, b_up)
    ffn = matmul(inner_b, w_down)
    hidden2, kept2 = layer_norm(hidden1 + ffn, norm2_gain, norm2_bias)
    hidden2_b = hidden2.astype(BF16)
    if routed():
        first_taps.double(1, context_b)
        last_tap.double(2, context_b)
        first_taps.cores(inner_b)
        last_tap.cores(inner_b)
        w_conv = [
            weight.reshape(-1, 2 * width) for weight in first_taps.finish() + last_tap.finish()
        ]
        w_ftok, w_fchr = w_conv[3][:, :width], w_conv[3][:, width:]

    char_tok, enter = gather_states(
        state, cum, edges_all, char_end[:, :, None], start[:, :, None]
    )
    char_tok_b = char_tok.astype(BF16)
    joined = jnp.concatenate(
        [matmul(hidden2_b, w_ftok), matmul(char_tok_b, w_fchr)], axis=1
    ).astype(BF16)

    two = 2 * width
    if routed():
        inner_own = own_columns(inner_b)
        joined = after(joined, *inner_own[1:])
        joined_own = own_columns(joined)
    blocks = joined.reshape(batch, rows, two)
    later, earlier = shifted(blocks, *neighbours(blocks))
    taps = (later.reshape(total_rows, two), joined, earlier.reshape(total_rows, two))
    conv = matmul(taps[1], w_conv[1]) + matmul(taps[0], w_conv[0]) + matmul(taps[2], w_conv[2])
    token_out, kept3 = layer_norm(hidden2 + conv[:, :width], norm3_gain, norm3_bias)
    char_out, kept4 = layer_norm(char_tok + conv[:, width:], norm4_gain, norm4_bias)

    d_in3, gain3_grad, bias3_grad = layer_norm_back(
        d_token.reshape(total_rows, width).astype(F32), norm3_gain, kept3
    )
    d_in4, gain4_grad, bias4_grad = layer_norm_back(
        d_char.reshape(total_rows, width).astype(F32), norm4_gain, kept4
    )
    d_conv = jnp.concatenate([d_in3, d_in4], axis=1).astype(BF16)
    d_before, d_after = neighbours(d_conv.reshape(batch, rows, two))
    if routed():
        d_conv = after(d_conv, *joined_own[1:])
    d_later, d_earlier = shifted(d_conv.reshape(batch, rows, two), d_before, d_after)
    d_joined = (
        matmul_nt(d_conv, w_conv[1])
        + matmul_nt(d_earlier.reshape(total_rows, two), w_conv[0])
        + matmul_nt(d_later.reshape(total_rows, two), w_conv[2])
    ).astype(BF16)
    if routed():
        d_all = gather(
            jnp.concatenate([d_conv.reshape(batch, rows, two), d_before, d_after], axis=1)
        )
    else:
        conv_sum = plain_sum(jnp.stack([matmul_tn(tap, d_conv).astype(BF16) for tap in taps]), 1)

    d_tok_part, d_chr_part = d_joined[:, :width], d_joined[:, width:]
    d_hidden2 = d_in3 + matmul_nt(d_tok_part, w_ftok)
    d_char_tok = d_in4 + matmul_nt(d_chr_part, w_fchr)

    end_line, start_line = char_end[:, None], start[:, None]
    spread, back_cum, carried, back_edges = gru_back(
        d_char_tok.reshape(batch, rows, width), decay, end_line, start_line, char_rows
    )

    d_in2, gain2_grad, bias2_grad = layer_norm_back(d_hidden2, norm2_gain, kept2)
    d_ffn = d_in2.astype(BF16)
    reduced = over_fsdp if routed() else plain_sum
    if routed():
        d_ffn_all = gather(d_ffn[None])
    else:
        second_sum = plain_sum(matmul_tn(inner_b, d_ffn).astype(BF16))
    d_pre = matmul_nt(d_ffn, w_down) * slope.astype(F32)
    bup_grad = jnp.sum(d_pre, axis=0)
    d_pre_low = d_pre.astype(BF16)
    d_hidden1 = d_in2 + matmul_nt(d_pre_low, w_up)
    d_in1, gain1_grad, bias1_grad = layer_norm_back(d_hidden1, norm1_gain, kept1)
    d_attn = d_in1.astype(BF16)
    if heads:
        sent = send_grad(d_attn, w_out, back_edges, heads, batch)
        conv_pieces = [after(joined_own[0], sent)] + joined_own[1:]
        first_chain = CtxSum.begun(*conv_gradient(conv_pieces, d_all, rows, 0))
        other_chain = CtxSum.begun(*conv_gradient(conv_pieces, d_all, rows, 1), OTHER_STEPS)
        hidden1_b = after(hidden1_b, first_chain.sent, other_chain.sent)
    third_sum = reduced(
        gradients(hidden1_b, context_b, hidden2_b, char_tok_b, d_pre_low, d_attn, d_joined)
    )

    if heads:
        received = lax.all_to_all(sent, "ctx", 0, 0, tiled=True)
        d_tok_part, heads_grad, back_enter = attend_back(
            tokens_all, w_heads, saved, kept, received.reshape(count * rows, -1), edges_all,
            heads, rows,
        )
        token_chain = TokenSum(d_tok_part.reshape(2, 2, 2, rows, width))
        last = other_chain.advance(first_chain.advance(heads_grad))
        last = token_chain.advance(last)
        gate = after(gate, last)
        second_chain = CtxSum(down_gradient(inner_own, d_ffn_all))
    else:
        back_enter = back_entering(edges_all, all_edges(back_edges))
        d_context = matmul_nt(d_attn, w_out).reshape(batch, rows, width)
        d_qkv = jnp.concatenate(
            [
                gathered_attention_back(
                    qkv[i], segment[i], results[i][0], results[i][1], d_context[i]
                )
                for i in range(batch)
            ]
        )
    d_gate_in, bgate_grad = gru_grad(
        gate, cand, decay, cum, state, enter, spread, back_cum, carried, back_enter, char_rows
    )
    d_gate_in = d_gate_in.reshape(batch * padded_rows, -1)
    d_chars = matmul_nt(d_gate_in, w_gru[:, :wide_gru]).astype(BF16)
    d_chars = d_chars.reshape(batch, padded_rows, width)[:, :char_rows]

    if not heads:
        heads_grad = matmul_tn(flat_tokens, d_qkv)
        d_tokens = matmul_nt(d_qkv, w_qkv)

    small = jnp.stack(
        [
            gain1_grad, bias1_grad, gain2_grad, bias2_grad, jnp.sum(bgate_grad, axis=(0, 1)),
            gain3_grad, bias3_grad, gain4_grad, bias4_grad,
        ],
        axis=1,
    )
    up_small = bup_grad.reshape(shards, -1, width // shards)
    up_small = jnp.swapaxes(up_small, 1, 2).reshape(width, -1)
    small = jnp.concatenate([small, up_small], axis=1)
    small = jnp.pad(small, ((0, 0), (0, 128 - small_count)))
    fourth = last_gradients(
        chars_pad.reshape(batch * padded_rows, width), d_gate_in, small, heads_grad
    )
    fourth_sum = reduced(fourth)

    widths = ((width,), (w_up.shape[1],) + (width,) * 3, (wide_gru, 128, width_qkv))
    if routed():
        own_wide = wide_gru + 128
        chains = dict(
            A=first_chain,
            B=other_chain,
            D=second_chain,
            X=token_chain,
            T=CtxSum(third_sum),
            G=CtxSum(fourth_sum[:, :own_wide]),
            K=HeadSum(fourth_sum[:, own_wide:]),
        )
        finish = dict(
            A=lambda value: settle_half(value, STEPS, 0),
            B=lambda value: value,
            D=lambda value: settle(value, widths[0]),
            T=lambda value: settle(value, widths[1]),
            G=lambda value: settle(value, widths[2][:2]),
            K=lambda value: spread_columns(value, heads),
            X=lambda value: value.reshape(total_rows, width),
        )
        done = run_in_order(chains, finish, fourth)
        (down_sum,), third = done["D"], done["T"]
        conv_sum = settle_half(done["B"], OTHER_STEPS, 1, done["A"])
        fourth = [*done["G"], done["K"]]
        d_tokens = done["X"]
    else:
        (down_sum,), third, fourth = (
            jnp.split(value, [sum(split[:i]) for i in range(1, len(split))], axis=1)
            for value, split in zip((second_sum, third_sum, fourth_sum), widths)
        )
    d_tokens = (d_in1 + d_tokens).astype(BF16)
    vector = fourth[1]
    return (
        token_out.astype(BF16).reshape(batch, rows, width),
        char_out.astype(BF16).reshape(batch, rows, width),
        d_tokens.reshape(batch, rows, width),
        d_chars,
        fourth[2],
        third[1],
        vector[:, 0],
        vector[:, 1],
        third[0],
        jnp.swapaxes(vector[:, 9:small_count], 0, 1).reshape(-1),
        down_sum,
        vector[:, 2],
        vector[:, 3],
        fourth[0],
        vector[:, 4],
        third[2],
        third[3],
        conv_sum,
        vector[:, 5],
        vector[:, 6],
        vector[:, 7],
        vector[:, 8],
    )


def solution(mesh):
    rows = P("fsdp", "ctx", None)
    pairs = P("fsdp", "ctx")
    matrix = P("fsdp", None)
    vector = P("fsdp")
    weights = (
        matrix, matrix, vector, vector, matrix, vector, matrix, vector, vector, matrix, vector,
        matrix, matrix, P(None, "fsdp", None), vector, vector, vector, vector,
    )
    return jax.shard_map(
        local,
        mesh=mesh,
        in_specs=(rows, rows, pairs, pairs) + weights + (rows, rows),
        out_specs=(rows,) * 4 + weights,
        check_vma=False,
    )
```

```python
import functools

import jax
import jax.numpy as jnp
from jax import lax
from jax.experimental import pallas as pl
from jax.experimental.pallas import tpu as pltpu
from jax.sharding import PartitionSpec as P

HEADS = 12
HEAD_DIM = 64
GRU_H = 384
EPSILON = 1e-05
BLOCK_LIMIT = 1024
FAR = 1e9
VMEM_BYTES = 40 * 1024 * 1024

F32 = jnp.float32
BF16 = jnp.bfloat16


def matmul(left, right):
    return jnp.dot(left, right, preferred_element_type=F32)


def matmul_nt(left, right):
    return lax.dot_general(left, right, (((1,), (1,)), ((), ())), preferred_element_type=F32)


def matmul_tn(left, right):
    return lax.dot_general(left, right, (((0,), (0,)), ((), ())), preferred_element_type=F32)


def layer_norm(value, gain, shift):
    center = value - jnp.mean(value, axis=-1, keepdims=True)
    inverse = lax.rsqrt(jnp.mean(center * center, axis=-1, keepdims=True) + EPSILON)
    normed = center * inverse
    return normed * gain + shift, (normed, inverse)


def layer_norm_back(grad, gain, kept):
    normed, inverse = kept
    scaled = grad * gain
    into = inverse * (
        scaled
        - jnp.mean(scaled, axis=-1, keepdims=True)
        - normed * jnp.mean(scaled * normed, axis=-1, keepdims=True)
    )
    return into, jnp.sum(grad * normed, axis=0), jnp.sum(grad, axis=0)


def params(**more):
    return pltpu.CompilerParams(vmem_limit_bytes=VMEM_BYTES, **more)


def cost(flops, moved, transcendentals=0):
    return pl.CostEstimate(
        flops=1, bytes_accessed=1, transcendentals=0
    )


def two_parts(value):
    high = value.astype(BF16)
    return high, (value - high.astype(F32)).astype(BF16)


KINDS = 4


def store_edges(edge_ref, cols, rows):
    parts = [half.astype(F32) for row in rows for half in two_parts(row)]
    parts = parts + [jnp.zeros_like(parts[0])] * (KINDS - len(parts))
    parts = jnp.concatenate(parts, axis=0)
    for sequence in range(edge_ref.shape[0] // KINDS):

        @pl.when(pl.program_id(0) == sequence)
        def store():
            edge_ref[pl.ds(sequence * KINDS, KINDS), cols] = parts


def edges_to_block(edges, rows):
    count = edges.shape[1] // HEAD_DIM
    pieces = [edges[:, i * HEAD_DIM : (i + 1) * HEAD_DIM] for i in range(count)]
    pieces.append(jnp.zeros((rows - count * edges.shape[0], HEAD_DIM), F32))
    return jnp.concatenate(pieces, axis=0).astype(BF16)


def edges_of_block(block):
    block = block.astype(F32)
    count = 2 * GRU_H // HEAD_DIM
    return jnp.concatenate([block[i * 8 : (i + 1) * 8] for i in range(count)], axis=1)


def entering_row(decays, drives, sequence, count, flip):
    me = lax.axis_index("ctx")
    halves = []
    for side in (0, 1):
        cols = slice(side * GRU_H, (side + 1) * GRU_H)
        total = jnp.zeros((1, GRU_H), F32)
        backward = (side == 1) != flip
        order = range(count - 1, 0, -1) if backward else range(count - 1)
        for other in order:
            decay, drive = decays(other, sequence, cols), drives(other, sequence, cols)
            there = me < other if backward else me > other
            total = jnp.where(there, decay * total + drive, total)
        halves.append(total)
    return jnp.concatenate(halves, axis=1)


def edge_reader(ref, kind):
    def read(other, sequence, cols):
        at = sequence * KINDS + 2 * kind
        return ref[other, at : at + 1, cols] + ref[other, at + 1 : at + 2, cols]

    return read


def shift_rows(value, by, fill, up):
    rows = value.shape[0]
    row = lax.broadcasted_iota(jnp.int32, value.shape, 0)
    if up:
        return jnp.where(row < rows - by, pltpu.roll(value, rows - by, 0), fill)
    return jnp.where(row >= by, pltpu.roll(value, by, 0), fill)


def scan_rows(decay, drive, up):
    by = 1
    while by < decay.shape[0]:
        drive = drive + decay * shift_rows(drive, by, 0.0, up)
        decay = decay * shift_rows(decay, by, 1.0, up)
        by = by * 2
    return decay, drive


def gru_forward_kernel(
    real, chars_ref, w_ref, bias_ref, start_ref, first_ref, end_ref, last_ref,
    gate_ref, cand_ref, decay_ref, cum_ref, state_ref, edge_ref,
):
    columns = matmul(chars_ref[0], w_ref[:, : 4 * GRU_H])
    rows = columns.shape[0]
    tokens = start_ref.shape[2]
    place = lax.broadcasted_iota(jnp.int32, (rows, tokens), 0)
    inside = lax.broadcasted_iota(jnp.int32, (rows, GRU_H), 0) < real
    resets = [
        jnp.sum(jnp.where(place == at[0], flag[0], 0.0), axis=1, keepdims=True)
        for at, flag in ((start_ref, first_ref), (end_ref, last_ref))
    ]
    for side in (0, 1):
        cols = pl.ds(side * GRU_H, GRU_H)
        base = 2 * side * GRU_H
        gate = jax.nn.sigmoid(columns[:, base : base + GRU_H] + bias_ref[:, cols])
        cand = jnp.tanh(columns[:, base + GRU_H : base + 2 * GRU_H])
        decay = jnp.where(inside, gate * (1.0 - resets[side]), 1.0)
        drive = jnp.where(inside, (1.0 - gate) * cand, 0.0)
        gate_ref[0, :, cols] = gate
        cand_ref[0, :, cols] = cand
        decay_ref[0, :, cols] = decay
        cum, state = scan_rows(decay, drive, side == 1)
        cum_ref[0, :, cols] = cum
        state_ref[0, :, cols] = state
        at = 0 if side else real - 1
        store_edges(edge_ref, cols, (cum[at : at + 1], state[at : at + 1]))


def char_tok_kernel(state_ref, cum_ref, edges_ref, end_ref, start_ref, out_ref, enter_ref):
    batch, tokens = end_ref.shape[:2]
    for sequence in range(batch):
        enter = entering_row(
            edge_reader(edges_ref, 0), edge_reader(edges_ref, 1), sequence, edges_ref.shape[0],
            False,
        )
        enter_ref[sequence] = enter
        state = state_ref[sequence] + cum_ref[sequence] * enter
        high, low = two_parts(state)
        place = lax.broadcasted_iota(jnp.int32, (tokens, state.shape[0]), 1)
        for side, at in ((0, end_ref), (1, start_ref)):
            pick = jnp.where(place == at[sequence], 1.0, 0.0).astype(BF16)
            cols = slice(side * GRU_H, (side + 1) * GRU_H)
            out_ref[pl.ds(sequence * tokens, tokens), pl.ds(side * GRU_H, GRU_H)] = matmul(
                pick, high[:, cols]
            ) + matmul(pick, low[:, cols])


def gru_back_kernel(
    real, grad_ref, decay_ref, end_ref, start_ref, spread_ref, cum_ref, carried_ref, edge_ref
):
    rows = decay_ref.shape[1]
    tokens = end_ref.shape[2]
    place = lax.broadcasted_iota(jnp.int32, (rows, tokens), 0)
    high, low = two_parts(grad_ref[0])
    for side, at in ((0, end_ref), (1, start_ref)):
        put = jnp.where(place == at[0], 1.0, 0.0).astype(BF16)
        cols = slice(side * GRU_H, (side + 1) * GRU_H)
        there = pl.ds(side * GRU_H, GRU_H)
        spread = matmul(put, high[:, cols]) + matmul(put, low[:, cols])
        decay = decay_ref[0, :, there]
        cum, carried = scan_rows(decay, decay * spread, side == 0)
        spread_ref[0, :, there] = spread
        cum_ref[0, :, there] = cum
        carried_ref[0, :, there] = carried
        at = real - 1 if side else 0
        store_edges(edge_ref, there, (carried[at : at + 1],))


def gru_grad_kernel(
    real, gate_ref, cand_ref, decay_ref, cum_ref, state_ref, enter_ref,
    spread_ref, back_cum_ref, carried_ref, back_enter_ref, out_ref, bias_ref,
):
    rows = gate_ref.shape[1]
    inside = lax.broadcasted_iota(jnp.int32, (rows, GRU_H), 0) < real
    for side in (0, 1):
        there = pl.ds(side * GRU_H, GRU_H)
        gate = gate_ref[0, :, there]
        cand = cand_ref[0, :, there]
        decay = decay_ref[0, :, there]
        enter = enter_ref[0, :, there]
        back_enter = back_enter_ref[0, :, there]
        state = state_ref[0, :, there] + cum_ref[0, :, there] * enter
        carried = carried_ref[0, :, there] + back_cum_ref[0, :, there] * back_enter
        previous = shift_rows(state, 1, enter, side == 1)
        adjoint = spread_ref[0, :, there] + shift_rows(carried, 1, back_enter, side == 0)
        adjoint = jnp.where(inside, adjoint, 0.0)
        rest = adjoint * (1.0 - gate)
        to_gate = rest * (previous * decay - cand * gate)
        to_cand = rest * (1.0 - cand * cand)
        out_ref[0, :, pl.ds(2 * side * GRU_H, GRU_H)] = to_gate.astype(BF16)
        out_ref[0, :, pl.ds((2 * side + 1) * GRU_H, GRU_H)] = to_cand.astype(BF16)
        bias_ref[0, :, there] = jnp.sum(to_gate, axis=0, keepdims=True)


def per_sequence(*tail):
    return pl.BlockSpec((1,) + tail, lambda s: (s,) + (0,) * len(tail))


def whole_block(*shape):
    return pl.BlockSpec(shape, lambda s: (0,) * len(shape))


def gru_forward(chars, w_gru, bias, start, first, end, last, real):
    batch, rows, width = chars.shape
    tokens = start.shape[2]
    two = 2 * GRU_H
    kept = jax.ShapeDtypeStruct((batch, rows, two), F32)
    return pl.pallas_call(
        functools.partial(gru_forward_kernel, real),
        grid=(batch,),
        in_specs=[per_sequence(rows, width), whole_block(width, w_gru.shape[1]), whole_block(1, two)]
        + [per_sequence(1, tokens)] * 4,
        out_specs=[per_sequence(rows, two)] * 5 + [whole_block(KINDS * batch, two)],
        out_shape=[kept] * 5 + [jax.ShapeDtypeStruct((KINDS * batch, two), F32)],
        compiler_params=params(),
        cost_estimate=cost(
            2 * batch * rows * width * 2 * two,
            chars.size * 2 + w_gru.size * 2 + 20 * batch * rows * two,
            2 * batch * rows * two,
        ),
        name="gru_forward",
    )(chars, w_gru, bias, start, first, end, last)


def gather_states(state, cum, edges, end, start):
    batch, rows, two = state.shape
    tokens = end.shape[1]
    return pl.pallas_call(
        char_tok_kernel,
        out_shape=[
            jax.ShapeDtypeStruct((batch * tokens, two), F32),
            jax.ShapeDtypeStruct((batch, 1, two), F32),
        ],
        compiler_params=params(),
        cost_estimate=cost(
            4 * batch * rows * tokens * two, 8 * batch * rows * two + 4 * batch * tokens * two
        ),
        name="gather_states",
    )(state, cum, edges, end, start)


def gru_back(grad, decay, end, start, real):
    batch, rows, two = decay.shape
    tokens = end.shape[2]
    kept = jax.ShapeDtypeStruct((batch, rows, two), F32)
    return pl.pallas_call(
        functools.partial(gru_back_kernel, real),
        grid=(batch,),
        in_specs=[per_sequence(tokens, two), per_sequence(rows, two)]
        + [per_sequence(1, tokens)] * 2,
        out_specs=[per_sequence(rows, two)] * 3 + [whole_block(KINDS * batch, two)],
        out_shape=[kept] * 3 + [jax.ShapeDtypeStruct((KINDS * batch, two), F32)],
        compiler_params=params(),
        cost_estimate=cost(
            4 * batch * rows * tokens * two, 16 * batch * rows * two + 4 * batch * tokens * two
        ),
        name="gru_back",
    )(grad, decay, end, start)


def gru_grad(gate, cand, decay, cum, state, enter, spread, back_cum, carried, back_enter, real):
    batch, rows, two = decay.shape
    big = per_sequence(rows, two)
    row = per_sequence(1, two)
    return pl.pallas_call(
        functools.partial(gru_grad_kernel, real),
        grid=(batch,),
        in_specs=[big] * 5 + [row] + [big] * 3 + [row],
        out_specs=[per_sequence(rows, 2 * two), row],
        out_shape=[
            jax.ShapeDtypeStruct((batch, rows, 2 * two), BF16),
            jax.ShapeDtypeStruct((batch, 1, two), F32),
        ],
        compiler_params=params(),
        cost_estimate=cost(20 * batch * rows * two, 36 * batch * rows * two),
        name="gru_grad",
    )(gate, cand, decay, cum, state, enter, spread, back_cum, carried, back_enter)


def all_edges(edges):
    return lax.all_gather(edges, "ctx", axis=0)


def entering_kernel(decay_ref, drive_ref, out_ref):
    for sequence in range(out_ref.shape[0]):
        out_ref[sequence] = entering_row(
            edge_reader(decay_ref, 0), edge_reader(drive_ref, 0), sequence, decay_ref.shape[0],
            True,
        )


def back_entering(decays, drives):
    batch, two = decays.shape[1] // KINDS, decays.shape[2]
    return pl.pallas_call(
        entering_kernel,
        out_shape=jax.ShapeDtypeStruct((batch, 1, two), F32),
        compiler_params=params(),
        name="back_entering",
    )(decays, drives)


def attend_kernel(
    heads, tokens, tok_ref, own_ref, core_ref, far_ref, far_core_ref, edge_ref, out_ref, kept_ref,
    query_ref, key_ref, value_ref, w_ref,
):
    part = heads * HEAD_DIM
    rows = out_ref.shape[0]
    step = pl.program_id(0)

    @pl.when(step == 0)
    def build():
        eye = jnp.where(
            lax.broadcasted_iota(jnp.int32, (HEAD_DIM, HEAD_DIM), 0)
            == lax.broadcasted_iota(jnp.int32, (HEAD_DIM, HEAD_DIM), 1),
            1.0,
            0.0,
        ).astype(BF16)
        number = lax.broadcasted_iota(jnp.int32, (HEAD_DIM, tokens), 0).astype(F32)
        shard = own_ref.shape[0]
        for other, piece_ref in enumerate((own_ref, core_ref, far_ref, far_core_ref)):
            at = jnp.bitwise_xor(lax.axis_index("fsdp"), other) * shard
            w_ref[pl.ds(pl.multiple_of(at, shard), shard)] = piece_ref[...]
        ones = jnp.ones((tokens, HEAD_DIM), BF16)

        def block(source, carry):
            qkv = matmul(tok_ref[source, :tokens], w_ref[...])
            ids = tok_ref[source, tokens:].astype(F32)[0:1, :tokens]
            marks = matmul_tn(jnp.where(number == ids, 1.0, 0.0).astype(BF16), eye)
            blocked = ((marks - 1.0) * FAR).astype(BF16)
            marks = marks.astype(BF16)
            here = pl.ds(pl.multiple_of(source * tokens, tokens), tokens)
            for head in range(heads):
                query, key, value = (
                    qkv[:, kind * part + head * HEAD_DIM : kind * part + (head + 1) * HEAD_DIM]
                    for kind in range(3)
                )
                query = query.astype(BF16) * jnp.asarray(HEAD_DIM ** (-0.5), BF16)
                query_ref[head, here] = jnp.concatenate([query, marks], axis=1)
                key_ref[head, here] = jnp.concatenate([key.astype(BF16), blocked], axis=1)
                value_ref[head, here] = jnp.concatenate([value.astype(BF16), ones], axis=1)
            return carry

        lax.fori_loop(0, tok_ref.shape[0], block, 0)

    here = pl.ds(pl.multiple_of(step * rows, rows), rows)
    outs = []
    for head in range(heads):
        expvals = jnp.exp(matmul_nt(query_ref[head, here], key_ref[head]))
        both = matmul(expvals.astype(BF16), value_ref[head])
        total = both[:, HEAD_DIM:]
        context = both[:, :HEAD_DIM] / total
        kept_ref[:, pl.ds(head * 2 * HEAD_DIM, 2 * HEAD_DIM)] = jnp.concatenate(
            [context, total], axis=1
        )
        outs.append(context.astype(BF16))
    block = edges_to_block(edge_ref[...], tokens)
    outs.append(jnp.concatenate([block] * (rows // tokens), axis=0))
    out_ref[...] = jnp.concatenate(outs, axis=1)


def attend_back_kernel(
    heads, tokens, tok_ref, w_ref, query_ref, key_ref, value_ref, kept_ref, grad_ref, edges_ref,
    out_ref, w_grad_ref, enter_ref, grad_scr, edge_scr,
):
    part = heads * HEAD_DIM
    rows = out_ref.shape[0]
    step = pl.program_id(0)

    @pl.when(step == 0)
    def build():
        lane = lax.broadcasted_iota(jnp.int32, (grad_ref.shape[0], HEAD_DIM), 1)
        for head in range(heads):
            at = head * HEAD_DIM
            context = kept_ref[:, 2 * at : 2 * at + HEAD_DIM]
            total = kept_ref[:, 2 * at + HEAD_DIM : 2 * at + 2 * HEAD_DIM]
            grad = grad_ref[:, at : at + HEAD_DIM].astype(F32) / total
            delta = jnp.sum(grad * context, axis=1, keepdims=True)
            high, low = two_parts(-delta)
            extra = jnp.where(
                lane == 0, high.astype(F32), jnp.where(lane == 1, low.astype(F32), 0.0)
            )
            grad_scr[head] = jnp.concatenate([grad, extra], axis=1).astype(BF16)
        for other in range(edges_ref.shape[0]):
            edge_scr[other] = edges_of_block(
                grad_ref[other * tokens : (other + 1) * tokens, part : part + HEAD_DIM]
            )
        for sequence in range(enter_ref.shape[0]):
            enter_ref[sequence] = entering_row(
                edge_reader(edges_ref, 0), edge_reader(edge_scr, 0), sequence,
                edges_ref.shape[0], True,
            )
        w_grad_ref[...] = jnp.zeros_like(w_grad_ref)

    here = pl.ds(pl.multiple_of(step * rows, rows), rows)
    scale = HEAD_DIM ** (-0.5)
    d_query, d_key, d_value = [], [], []
    for head in range(heads):
        expvals = jnp.exp(matmul_nt(query_ref[head, here], key_ref[head]))
        inner = matmul_nt(grad_scr[head, here], value_ref[head])
        d_scores = (expvals * inner).astype(BF16)
        d_query.append((matmul(d_scores, key_ref[head])[:, :HEAD_DIM] * scale).astype(BF16))
        expvals = jnp.exp(matmul_nt(key_ref[head, here], query_ref[head]))
        inner = matmul_nt(value_ref[head, here], grad_scr[head])
        d_scores = (expvals * inner).astype(BF16)
        d_key.append(matmul(d_scores, query_ref[head])[:, :HEAD_DIM].astype(BF16))
        d_value.append(
            matmul(expvals.astype(BF16), grad_scr[head])[:, :HEAD_DIM].astype(BF16)
        )
    d_qkv = jnp.concatenate(d_query + d_key + d_value, axis=1)
    out_ref[...] = matmul_nt(d_qkv, w_ref[...]).astype(BF16)
    blocks = rows // tokens
    tok = jnp.concatenate(
        [tok_ref[step * blocks + block, :tokens] for block in range(blocks)], axis=0
    )
    w_grad_ref[...] += matmul_tn(tok, d_qkv)


def unpack_kernel(groups, part, in_ref, out_ref, edge_ref):
    for group in range(groups):
        edge_ref[group] = edges_of_block(in_ref[group, :, part:])
    out_ref[...] = jnp.concatenate([in_ref[group, :, :part] for group in range(groups)], axis=1)


def spread_columns_kernel(heads, in_ref, out_ref):
    groups, part = in_ref.shape[0], heads * HEAD_DIM
    width = groups * part
    mine = lax.rem(lax.axis_index("ctx"), groups)
    for case in range(groups):

        @pl.when(mine == case)
        def place():
            for kind in range(3):
                pieces = [
                    in_ref[case ^ group, :, kind * part : (kind + 1) * part].astype(F32)
                    for group in range(groups)
                ]
                out_ref[:, pl.ds(kind * width, width)] = jnp.concatenate(pieces, axis=1)


def send_grad_kernel(groups, part, grad_ref, w_ref, edge_ref, out_ref):
    d_context = matmul_nt(grad_ref[...], w_ref[...]).astype(BF16)
    block = edges_to_block(edge_ref[...], grad_ref.shape[0])
    for group in range(groups):
        out_ref[group] = jnp.concatenate(
            [d_context[:, group * part : (group + 1) * part], block], axis=1
        )


def heads_here(batch, count):
    if batch * HEADS % count != 0 or not routed():
        return 0
    heads = batch * HEADS // count
    if heads > HEADS or HEADS % heads != 0 or heads % 2 == 0 or batch * KINDS != 8:
        return 0
    return heads


def attend(tokens_all, w_pieces, edges, heads, tokens):
    count, rows, width = tokens_all.shape
    length = count * tokens
    block = 256
    part = heads * HEAD_DIM
    out_wide = part + HEAD_DIM
    wide = jax.ShapeDtypeStruct((heads, length, 2 * HEAD_DIM), BF16)
    return pl.pallas_call(
        functools.partial(attend_kernel, heads, tokens),
        grid=(length // block,),
        in_specs=[
            pl.BlockSpec((count, rows, width), lambda i: (0, 0, 0)),
        ]
        + [pl.BlockSpec(w_pieces[0].shape, lambda i: (0, 0))] * 4
        + [pl.BlockSpec(edges.shape, lambda i: (0, 0))],
        out_specs=[
            pl.BlockSpec((block, out_wide), lambda i: (i, 0)),
            pl.BlockSpec((block, 2 * part), lambda i: (i, 0)),
        ]
        + [pl.BlockSpec(wide.shape, lambda i: (0, 0, 0))] * 3
        + [pl.BlockSpec((width, 3 * part), lambda i: (0, 0))],
        out_shape=[
            jax.ShapeDtypeStruct((length, out_wide), BF16),
            jax.ShapeDtypeStruct((length, 2 * part), F32),
            wide,
            wide,
            wide,
            jax.ShapeDtypeStruct((width, 3 * part), BF16),
        ],
        compiler_params=params(),
        cost_estimate=cost(
            8 * heads * length * length * HEAD_DIM,
            length * (width * 2 + out_wide * 2 + 8 * part),
            heads * length * length,
        ),
        name="attend",
    )(tokens_all, *w_pieces, edges)


def attend_back(tokens_all, w_heads, saved, kept, grads, edges, heads, tokens):
    count, rows, width = tokens_all.shape
    length = count * tokens
    block = 256
    part = heads * HEAD_DIM
    batch, two = edges.shape[1] // KINDS, edges.shape[2]
    wide = (heads, length, 2 * HEAD_DIM)
    return pl.pallas_call(
        functools.partial(attend_back_kernel, heads, tokens),
        grid=(length // block,),
        in_specs=[
            pl.BlockSpec((count, rows, width), lambda i: (0, 0, 0)),
            pl.BlockSpec(w_heads.shape, lambda i: (0, 0)),
        ]
        + [pl.BlockSpec(wide, lambda i: (0, 0, 0))] * 3
        + [
            pl.BlockSpec((length, 2 * part), lambda i: (0, 0)),
            pl.BlockSpec((length, part + HEAD_DIM), lambda i: (0, 0)),
            pl.BlockSpec(edges.shape, lambda i: (0, 0, 0)),
        ],
        out_specs=[
            pl.BlockSpec((block, width), lambda i: (i, 0)),
            pl.BlockSpec(w_heads.shape, lambda i: (0, 0)),
            pl.BlockSpec((batch, 1, two), lambda i: (0, 0, 0)),
        ],
        out_shape=[
            jax.ShapeDtypeStruct((length, width), BF16),
            jax.ShapeDtypeStruct(w_heads.shape, F32),
            jax.ShapeDtypeStruct((batch, 1, two), F32),
        ],
        scratch_shapes=[pltpu.VMEM(wide, BF16), pltpu.VMEM(edges.shape, F32)],
        compiler_params=params(),
        cost_estimate=cost(
            28 * heads * length * length * HEAD_DIM,
            length * (width * 4 + 8 * part + 2 * part),
            2 * heads * length * length,
        ),
        name="attend_back",
    )(tokens_all, w_heads, *saved, kept, grads, edges)


def unpack(received, heads, batch):
    count, rows, wide = received.shape
    groups, part = HEADS // heads, heads * HEAD_DIM
    width = groups * part
    return pl.pallas_call(
        functools.partial(unpack_kernel, groups, part),
        grid=(batch,),
        in_specs=[pl.BlockSpec((groups, rows, wide), lambda s: (s, 0, 0))],
        out_specs=[
            pl.BlockSpec((rows, width), lambda s: (s, 0)),
            pl.BlockSpec((groups, KINDS * batch, 2 * GRU_H), lambda s: (s, 0, 0)),
        ],
        out_shape=[
            jax.ShapeDtypeStruct((batch * rows, width), BF16),
            jax.ShapeDtypeStruct((count, KINDS * batch, 2 * GRU_H), F32),
        ],
        compiler_params=params(),
        cost_estimate=cost(0, 2 * received.size + 2 * batch * rows * width),
        name="unpack",
    )(received)


def spread_columns(pieces, heads):
    groups, rows, wide = pieces.shape
    return pl.pallas_call(
        functools.partial(spread_columns_kernel, heads),
        out_shape=jax.ShapeDtypeStruct((rows, groups * wide), F32),
        compiler_params=params(),
        cost_estimate=cost(1, 1),
        name="spread_columns",
    )(pieces)


def send_grad(d_attn, w_out, edges, heads, batch):
    total, width = d_attn.shape
    rows = total // batch
    groups, part = HEADS // heads, heads * HEAD_DIM
    wide = part + HEAD_DIM
    return pl.pallas_call(
        functools.partial(send_grad_kernel, groups, part),
        grid=(batch,),
        in_specs=[
            pl.BlockSpec((rows, width), lambda s: (s, 0)),
            whole_block(width, width),
            whole_block(*edges.shape),
        ],
        out_specs=pl.BlockSpec((groups, rows, wide), lambda s: (s, 0, 0)),
        out_shape=jax.ShapeDtypeStruct((batch * groups, rows, wide), BF16),
        compiler_params=params(),
        cost_estimate=cost(
            2 * total * width * width, 2 * (d_attn.size + w_out.size + total * groups * wide)
        ),
        name="send_grad",
    )(d_attn, w_out, edges)


def feed_forward_kernel(hidden_ref, w_ref, bias_ref, inner_ref, slope_ref):
    pre = matmul(hidden_ref[...], w_ref[...]) + bias_ref[...]
    at = jnp.abs(pre) * (0.5**0.5)
    near = 1.0 / (1.0 + 0.3275911 * at)
    gauss = jnp.exp(-at * at)
    series = 1.061405429
    for term in (-1.453152027, 1.421413741, -0.284496736, 0.254829592):
        series = series * near + term
    tail = 0.5 * series * near * gauss
    below = jnp.where(pre < 0.0, tail, 1.0 - tail)
    inner_ref[...] = (pre * below).astype(BF16)
    slope_ref[...] = (below + pre * gauss * (2.0 * jnp.pi) ** -0.5).astype(BF16)


def feed_forward(hidden, w_up, bias):
    rows, width = hidden.shape
    wide = w_up.shape[1]
    block = 512
    column = pl.BlockSpec((rows, block), lambda i: (0, i))
    return pl.pallas_call(
        feed_forward_kernel,
        grid=(wide // block,),
        in_specs=[
            whole_block(rows, width),
            pl.BlockSpec((width, block), lambda i: (0, i)),
            pl.BlockSpec((1, block), lambda i: (0, i)),
        ],
        out_specs=[column, column],
        out_shape=[jax.ShapeDtypeStruct((rows, wide), BF16)] * 2,
        compiler_params=params(),
        cost_estimate=cost(
            2 * rows * width * wide, 2 * (hidden.size + w_up.size + 2 * rows * wide), rows * wide
        ),
        name="feed_forward",
    )(hidden, w_up, bias)


def gradients_kernel(
    blocks, hidden1_ref, context_ref, hidden2_ref, char_ref, pre_ref, attn_ref, joined_ref, out_ref
):
    step = pl.program_id(0)
    width = hidden2_ref.shape[1]

    def put(at, left_ref, right):
        @pl.when((step < blocks) if at is None else (step == blocks + at))
        def store():
            out_ref[...] = matmul_tn(left_ref[...], right()).astype(BF16)

    put(None, hidden1_ref, lambda: pre_ref[...])
    put(0, context_ref, lambda: attn_ref[...])
    put(1, hidden2_ref, lambda: joined_ref[:, :width])
    put(2, char_ref, lambda: joined_ref[:, width:])


def gradients(hidden1, context, hidden2, chars, d_pre, d_attn, d_joined):
    rows, width = hidden1.shape
    blocks = d_pre.shape[1] // width
    whole = whole_block(rows, width)
    return pl.pallas_call(
        functools.partial(gradients_kernel, blocks),
        grid=(blocks + 3,),
        in_specs=[whole] * 4
        + [
            pl.BlockSpec((rows, width), lambda i: (0, jnp.minimum(i, blocks - 1))),
            whole,
            whole_block(rows, 2 * width),
        ],
        out_specs=pl.BlockSpec((width, width), lambda i: (0, i)),
        out_shape=jax.ShapeDtypeStruct((width, (blocks + 3) * width), BF16),
        compiler_params=params(),
        cost_estimate=cost(1, 1),
        name="gradients",
    )(hidden1, context, hidden2, chars, d_pre, d_attn, d_joined)


def store_halves(total, keep_ref, send_ref, lead):
    half = total.shape[0] // 2
    halves = (total[:half].astype(BF16), total[half:].astype(BF16))
    for mine in (0, 1):

        @pl.when(lax.rem(lax.axis_index("ctx"), 2) == mine)
        def store():
            keep_ref[lead] = halves[mine]
            send_ref[lead] = halves[1 - mine]


def down_grad_kernel(own_ref, core_ref, far_ref, far_core_ref, grad_ref, keep_ref, send_ref):
    total = jnp.zeros((own_ref.shape[1], grad_ref.shape[2]), F32)
    for other, inner_ref in enumerate((own_ref, core_ref, far_ref, far_core_ref)):
        source = jnp.bitwise_xor(lax.axis_index("fsdp"), other)
        total = total + matmul_tn(inner_ref[...], grad_ref[source])
    store_halves(total, keep_ref, send_ref, ...)


def down_gradient(inner, grads):
    half = jax.ShapeDtypeStruct((inner[0].shape[1] // 2, grads.shape[2]), BF16)
    return pl.pallas_call(
        down_grad_kernel,
        out_shape=[half, half],
        compiler_params=params(),
        cost_estimate=cost(1, 1),
        name="down_gradient",
    )(*inner, grads)


def conv_grad_kernel(
    own_ref, core_ref, far_ref, far_core_ref, grad_ref, keep_ref, send_ref, side_scr
):
    tap = pl.program_id(0)
    refs = (own_ref, core_ref, far_ref, far_core_ref)
    batch = grad_ref.shape[0] // len(refs)
    rows = side_scr.shape[0] // batch
    shape = (rows, grad_ref.shape[2])
    row = lax.broadcasted_iota(jnp.int32, shape, 0)
    total = jnp.zeros((own_ref.shape[1], grad_ref.shape[2]), F32)
    for other, joined_ref in enumerate(refs):
        first = jnp.bitwise_xor(lax.axis_index("fsdp"), other) * batch
        for block in range(batch):
            here = pl.ds(block * rows, rows)
            grad = grad_ref[first + block].astype(F32)
            mid = grad[:rows]

            @pl.when(tap == 0)
            def earlier():
                moved = pltpu.roll(mid, rows - 1, 0)
                last = jnp.broadcast_to(grad[rows + 1 : rows + 2], shape)
                side_scr[here] = jnp.where(row == rows - 1, last, moved).astype(BF16)

            @pl.when(tap == 1)
            def same():
                side_scr[here] = mid.astype(BF16)

            @pl.when(tap == 2)
            def later():
                moved = pltpu.roll(mid, 1, 0)
                before = jnp.broadcast_to(grad[rows : rows + 1], shape)
                side_scr[here] = jnp.where(row == 0, before, moved).astype(BF16)

        total = total + matmul_tn(joined_ref[...], side_scr[...])
    store_halves(total, keep_ref, send_ref, 0)


def conv_gradient(joined, grads, rows, part):
    count, tall, wide = grads.shape
    wide = wide // 2
    own = joined[0].shape
    out = jax.ShapeDtypeStruct((3, own[1] // 2, wide), BF16)
    return pl.pallas_call(
        conv_grad_kernel,
        grid=(3,),
        in_specs=[pl.BlockSpec(own, lambda k: (0, 0))] * 4
        + [pl.BlockSpec((count, tall, wide), lambda k: (0, 0, part))],
        out_specs=[pl.BlockSpec((1,) + out.shape[1:], lambda k: (k, 0, 0))] * 2,
        out_shape=[out, out],
        scratch_shapes=[pltpu.VMEM((own[0], wide), BF16)],
        compiler_params=params(),
        cost_estimate=cost(1, 1),
        name="conv_gradient",
    )(*joined, grads)


def last_grads_kernel(chars_ref, gates_ref, small_ref, heads_ref, out_ref):
    wide = gates_ref.shape[1]
    narrow = 128
    out_ref[:, :wide] = matmul_tn(chars_ref[...], gates_ref[...]).astype(BF16)
    count = small_ref.shape[0]
    eye = jnp.where(
        lax.broadcasted_iota(jnp.int32, (count, narrow), 0)
        == lax.broadcasted_iota(jnp.int32, (count, narrow), 1),
        1.0,
        0.0,
    ).astype(BF16)
    out_ref[:, wide : wide + narrow] = matmul_tn(small_ref[...].astype(BF16), eye).astype(BF16)
    out_ref[:, wide + narrow :] = heads_ref[...].astype(BF16)


def last_gradients(chars, d_gates, small, heads_grad):
    width = chars.shape[1]
    wide = d_gates.shape[1] + 128 + heads_grad.shape[1]
    return pl.pallas_call(
        last_grads_kernel,
        out_shape=jax.ShapeDtypeStruct((width, wide), BF16),
        compiler_params=params(),
        cost_estimate=cost(1, 1),
        name="last_gradients",
    )(chars, d_gates, small, heads_grad)


def block_size(rows):
    size = min(rows, BLOCK_LIMIT)
    while rows % size != 0:
        size = size - 1
    return size


def split_blocks(array, size):
    return array.reshape((array.shape[0] // size, size) + array.shape[1:])


def to_heads(matrix):
    return matrix.reshape(matrix.shape[0], HEADS, HEAD_DIM)


def masked_exp(query_heads, key_heads, query_seg, key_seg):
    scores = jnp.einsum(
        "qhd,khd->hqk", query_heads, key_heads, preferred_element_type=F32
    ) * HEAD_DIM ** (-0.5)
    same = (query_seg[:, None] == key_seg[None, :])[None, :, :]
    return jnp.where(same, jnp.exp(scores), 0.0)


def everyone(rows):
    return lax.all_gather(rows, "ctx", axis=0, tiled=True)


def gathered_attention(qkv, seg_row):
    tok_rows, width = qkv.shape[0], qkv.shape[1] // 3
    query_heads = to_heads(qkv[:, :width])
    pieces = (everyone(qkv[:, width : 2 * width]), everyone(qkv[:, 2 * width :]), everyone(seg_row))
    size = block_size(pieces[0].shape[0])

    def step(acc, item):
        key_block, value_block, seg_block = item
        expvals = masked_exp(query_heads, to_heads(key_block), seg_row, seg_block)
        part_num = jnp.einsum(
            "hqk,khd->qhd", expvals.astype(BF16), to_heads(value_block),
            preferred_element_type=F32,
        )
        return ((acc[0] + part_num, acc[1] + jnp.transpose(jnp.sum(expvals, axis=-1))), None)

    (numer, total), unused = lax.scan(
        step,
        (jnp.zeros((tok_rows, HEADS, HEAD_DIM), F32), jnp.zeros((tok_rows, HEADS), F32)),
        tuple(split_blocks(piece, size) for piece in pieces),
    )
    return numer / total[:, :, None], total


def gathered_attention_back(qkv, seg_row, context, total, d_context):
    tok_rows, width = qkv.shape[0], qkv.shape[1] // 3
    scale = HEAD_DIM ** (-0.5)
    d_context = to_heads(d_context)
    query_rows, key_rows, value_rows = (qkv[:, i * width : (i + 1) * width] for i in range(3))
    grad_heads = (d_context / total[:, :, None]).astype(BF16)
    delta = jnp.sum(d_context * context, axis=-1) / total
    key_heads, value_heads, query_heads = (
        to_heads(key_rows), to_heads(value_rows), to_heads(query_rows)
    )
    zero_heads = jnp.zeros((tok_rows, HEADS, HEAD_DIM), F32)
    seg_all = everyone(seg_row)
    size = block_size(seg_all.shape[0])

    def key_step(acc, item):
        query_block, grad_block, delta_block, seg_block = item
        query_h, grad_h = to_heads(query_block), to_heads(grad_block)
        expvals = masked_exp(query_h, key_heads, seg_block, seg_row)
        dprob = jnp.einsum("qhd,khd->hqk", grad_h, value_heads, preferred_element_type=F32)
        dscore = (expvals * (dprob - jnp.transpose(delta_block)[:, :, None])).astype(BF16)
        dkey = acc[0] + scale * jnp.einsum(
            "hqk,qhd->khd", dscore, query_h, preferred_element_type=F32
        )
        dval = acc[1] + jnp.einsum(
            "hqk,qhd->khd", expvals.astype(BF16), grad_h, preferred_element_type=F32
        )
        return ((dkey, dval), None)

    (dkey, dval), unused = lax.scan(
        key_step,
        (zero_heads, zero_heads),
        tuple(
            split_blocks(piece, size)
            for piece in (
                everyone(query_rows),
                everyone(grad_heads.reshape(tok_rows, width)),
                everyone(delta),
                seg_all,
            )
        ),
    )

    def query_step(acc, item):
        key_block, value_block, seg_block = item
        key_h = to_heads(key_block)
        expvals = masked_exp(query_heads, key_h, seg_row, seg_block)
        dprob = jnp.einsum(
            "qhd,khd->hqk", grad_heads, to_heads(value_block), preferred_element_type=F32
        )
        dscore = (expvals * (dprob - jnp.transpose(delta)[:, :, None])).astype(BF16)
        return (
            acc + scale * jnp.einsum("hqk,khd->qhd", dscore, key_h, preferred_element_type=F32),
            None,
        )

    dquery, unused = lax.scan(
        query_step,
        zero_heads,
        tuple(
            split_blocks(piece, size)
            for piece in (everyone(key_rows), everyone(value_rows), seg_all)
        ),
    )
    return jnp.concatenate(
        [part.reshape(tok_rows, width) for part in (dquery, dkey, dval)], axis=1
    ).astype(BF16)


def neighbours(rows):
    count = lax.axis_size("ctx")
    up = [(i, i + 1) for i in range(count - 1)]
    down = [(j, i) for i, j in up]
    before = lax.ppermute(rows[:, -1], "ctx", up)
    after = lax.ppermute(rows[:, 0], "ctx", down)
    return before[:, None], after[:, None]


def shifted(rows, before, after):
    later = jnp.concatenate([before, rows[:, :-1]], axis=1)
    earlier = jnp.concatenate([rows[:, 1:], after], axis=1)
    return later, earlier


def routed():
    return lax.axis_size("ctx") == 8 and lax.axis_size("fsdp") == 4


STEPS = (1, 2, 4)
OTHER_STEPS = (1, 4, 2)
ORDER = "XABTXABDXTABDXGKTABDGKTDGKTDGKABTGDGTDG"


def flip(value, axis, bit):
    return lax.ppermute(value, axis, [(i, i ^ bit) for i in range(lax.axis_size(axis))])


def slot(steps=STEPS):
    me = lax.axis_index("ctx")
    first, second, third = ((me // bit) % 2 for bit in steps)
    return first * 4 + second * 2 + third


def own_columns(value):
    count, mine = lax.axis_size("fsdp"), lax.axis_index("fsdp")
    wide = value.shape[1] // count
    pieces = []
    for other in range(count):
        piece = lax.dynamic_slice_in_dim(value, jnp.bitwise_xor(mine, other) * wide, wide, 1)
        pieces.append(flip(piece, "fsdp", other) if other else piece)
    return pieces


class CtxSum:
    def __init__(self, value, steps=STEPS):
        self.value = value
        self.axis = value.ndim - 2
        self.stage = 0
        self.steps = steps

    @classmethod
    def begun(cls, keep, send, steps=STEPS):
        chain = cls(keep, steps)
        chain.keep = keep
        chain.send(send, steps[0])
        chain.stage = 1
        return chain

    def halve(self, value, bit):
        mine = (lax.axis_index("ctx") // bit) % 2
        half = value.shape[self.axis] // 2
        send = lax.dynamic_slice_in_dim(value, (1 - mine) * half, half, self.axis)
        self.keep = lax.dynamic_slice_in_dim(value, mine * half, half, self.axis)
        self.send(send, bit)

    def send(self, value, bit):
        self.sent = value
        self.got = flip(value, "ctx", bit)

    def advance(self, *others):
        stage = self.stage
        self.stage = stage + 1
        if stage == 0:
            self.halve(after(self.value, *others), self.steps[0])
        elif stage <= 3:
            got = after(self.got, *others).astype(F32)
            piece = (self.keep.astype(F32) + got).astype(BF16)
            if stage < 3:
                self.halve(piece, self.steps[stage])
            else:
                self.send(piece[None], self.steps[2])
        else:
            piece = jnp.concatenate([self.sent, after(self.got, *others)], axis=0)
            if stage < 6:
                self.send(piece, self.steps[5 - stage])
            else:
                self.result = self.sent = piece
        return self.sent


class HeadSum(CtxSum):
    def advance(self, *others):
        stage = self.stage
        self.stage = stage + 1
        if stage == 0:
            self.send(after(self.value, *others), 4)
        elif stage == 1:
            piece = self.sent.astype(F32) + after(self.got, *others).astype(F32)
            self.send(piece.astype(BF16)[None], 1)
        else:
            piece = jnp.concatenate([self.sent, after(self.got, *others)], axis=0)
            if stage == 2:
                self.send(piece, 2)
            else:
                self.result = self.sent = piece
        return self.sent


class TokenSum(CtxSum):
    def advance(self, *others):
        me = lax.axis_index("ctx")
        stage = self.stage
        self.stage = stage + 1
        if stage == 0:
            piece = after(self.value, *others)
        else:
            got = after(self.got, *others).astype(F32)
            if stage == 3:
                keep = self.keep.astype(F32)
                ordered = (jnp.concatenate([keep, got]), jnp.concatenate([got, keep]))
                self.result = self.sent = jnp.where(me // 4 == 0, *ordered)
                return self.sent
            piece = (self.keep.astype(F32) + got).astype(BF16)
            piece = jnp.squeeze(piece, axis=3 - stage)
        bit = STEPS[stage]
        mine = (me // bit) % 2
        axis = 2 - stage
        self.keep = lax.dynamic_slice_in_dim(piece, mine, 1, axis)
        self.send(lax.dynamic_slice_in_dim(piece, 1 - mine, 1, axis), bit)
        return self.sent


def run_in_order(chains, finish, begin):
    last, done = (), {}
    final = max(i for i, name in enumerate(ORDER[:-2]) if name == "G")
    for event, name in enumerate(ORDER):
        others = last
        if event == final or event == len(ORDER) - 1:
            ready = [done[other] for other in "ABKDT" if other in done]
            others = others + tuple(jax.tree.leaves(ready))
        step = chains[name].advance if name in chains else begin[name]
        last = (step(*others),)
        chain = chains[name]
        if event == ORDER.index("T"):
            begin["last"](*last)
        if hasattr(chain, "result"):
            done[name] = finish[name](chain.result, done)
    return done


def settle_kernel(order_ref, in_ref, *out_refs):
    at = 0
    for out_ref in out_refs:
        wide = out_ref.shape[-1]
        out_ref[...] = in_ref[0, ..., at : at + wide].astype(F32)
        at = at + wide


def settle_half_kernel(order_ref, in_ref, *refs):
    refs[-1][...] = in_ref[0].astype(F32)


def settle_half(pieces, steps, part, whole=None):
    lead = pieces.shape[1:-2]
    rows, width = pieces.shape[-2:]
    none = (0,) * len(lead)
    order = jnp.bitwise_xor(slot(steps), jnp.arange(8, dtype=jnp.int32))
    given = [] if whole is None else [whole]
    return pl.pallas_call(
        settle_half_kernel,
        grid_spec=pltpu.PrefetchScalarGridSpec(
            num_scalar_prefetch=1,
            grid=(8,),
            in_specs=[
                pl.BlockSpec((1,) + lead + (rows, width), lambda r, o: (r,) + none + (0, 0))
            ]
            + [pl.BlockSpec(memory_space=pl.ANY)] * len(given),
            out_specs=pl.BlockSpec(lead + (rows, width), lambda r, o: none + (o[r], part)),
        ),
        out_shape=jax.ShapeDtypeStruct(lead + (8 * rows, 2 * width), F32),
        input_output_aliases={2: 0} if given else {},
        compiler_params=params(),
        cost_estimate=cost(1, 1),
        name="settle_half",
    )(order, pieces, *given)


def settle(pieces, widths):
    lead = pieces.shape[1:-2]
    rows, total = pieces.shape[-2:]
    order = jnp.bitwise_xor(slot(), jnp.arange(8, dtype=jnp.int32))
    none = (0,) * len(lead)
    return pl.pallas_call(
        settle_kernel,
        grid_spec=pltpu.PrefetchScalarGridSpec(
            num_scalar_prefetch=1,
            grid=(8,),
            in_specs=[
                pl.BlockSpec((1,) + lead + (rows, total), lambda r, o: (r,) + none + (0, 0))
            ],
            out_specs=[
                pl.BlockSpec(lead + (rows, width), lambda r, o: none + (o[r], 0))
                for width in widths
            ],
        ),
        out_shape=[jax.ShapeDtypeStruct(lead + (8 * rows, width), F32) for width in widths],
        compiler_params=params(),
        cost_estimate=cost(pieces.size, 6 * pieces.size),
        name="settle",
    )(order, pieces)


def move(sources, stages, targets, arrived, left):
    ins = [
        pltpu.make_async_copy(source, stage, arrived.at[i])
        for i, (source, stage) in enumerate(zip(sources, stages))
    ]
    for copy in ins:
        copy.start()
    outs = []
    for i, (copy, stage, target) in enumerate(zip(ins, stages, targets)):
        copy.wait()
        outs.append(pltpu.make_async_copy(stage, target, left.at[i]))
        outs[-1].start()
    for copy in outs:
        copy.wait()


def place_own_kernel(spans, own_ref, core_ref, *rest):
    outs, (own_scr, core_scr, arrived, left) = rest[:-4], rest[-4:]
    mine = lax.axis_index("fsdp")
    sources, stages, targets, at = [], [], [], 0
    for span, out_ref in zip(spans, outs):
        there = pl.ds(at, span)
        for ref, scr, shard in (
            (own_ref, own_scr, mine),
            (core_ref, core_scr, jnp.bitwise_xor(mine, 1)),
        ):
            sources.append(ref.at[there])
            stages.append(scr.at[there])
            targets.append(out_ref.at[shard])
        at = at + span
    move(sources, stages, targets, arrived, left)


def place_kernel(spans, order, piece_ref, core_ref, *rest):
    outs, (piece_scr, core_scr, arrived, left) = rest[len(spans) : -4], rest[-4:]
    place = slot()
    mine = lax.axis_index("fsdp")
    sources, stages, targets = [], [], []
    for ref, scr, shard in (
        (piece_ref, piece_scr, jnp.bitwise_xor(mine, 2)),
        (core_ref, core_scr, jnp.bitwise_xor(mine, 3)),
    ):
        for position, other in enumerate(order):
            at = 0
            for span, out_ref in zip(spans, outs):
                part = span // 8
                there = pl.multiple_of(jnp.bitwise_xor(place, other) * part, part)
                sources.append(ref.at[position, pl.ds(at, part)])
                stages.append(scr.at[position, pl.ds(at, part)])
                targets.append(out_ref.at[shard, pl.ds(there, part)])
                at = at + part
    move(sources, stages, targets, arrived, left)


def after(value, *others):
    return lax.optimization_barrier((value,) + others)[0]


class SpreadGather:
    def __init__(self, shards):
        self.spans = tuple(shard.shape[0] for shard in shards)
        self.width = shards[0].shape[1]
        place = slot()
        self.own = jnp.concatenate(shards, axis=0) if len(shards) > 1 else shards[0]
        piece = [
            lax.dynamic_slice_in_dim(shard, place * (span // 8), span // 8, 0)
            for shard, span in zip(shards, self.spans)
        ]
        self.base = None
        self.got = flip(jnp.concatenate(piece, axis=0), "fsdp", 2)[None]
        self.core = flip(self.own, "fsdp", 1)
        self.order = [0]

    def take(self, others):
        got = after(self.got, *others) if others else self.got
        return got if self.base is None else jnp.concatenate([self.base, got], axis=0)

    def double(self, bit, *others):
        self.base = self.take(others)
        self.got = flip(self.base, "ctx", bit)
        self.order = self.order + [other ^ (4 // bit) for other in self.order]

    def cores(self, *others):
        self.piece = self.take(others)
        self.core_piece = flip(self.piece, "fsdp", 1)

    def place_own(self, *others):
        spans, width = self.spans, self.own.shape[1]
        self.whole = pl.pallas_call(
            functools.partial(place_own_kernel, spans),
            in_specs=[pl.BlockSpec(memory_space=pl.ANY)] * 2,
            out_specs=[pl.BlockSpec(memory_space=pl.ANY)] * len(spans),
            out_shape=[jax.ShapeDtypeStruct((4, span, width), BF16) for span in spans],
            scratch_shapes=[pltpu.VMEM(self.own.shape, BF16)] * 2
            + [pltpu.SemaphoreType.DMA((2 * len(spans),))] * 2,
            compiler_params=params(),
            cost_estimate=cost(0, 8 * sum(spans) * width),
            name="place_own",
        )(after(self.own, *others), self.core)

    def finish(self):
        spans, width = self.spans, self.own.shape[1]
        anywhere = [pl.BlockSpec(memory_space=pl.ANY)] * len(spans)
        return pl.pallas_call(
            functools.partial(place_kernel, spans, self.order),
            in_specs=[pl.BlockSpec(memory_space=pl.ANY)] * 2 + anywhere,
            out_specs=anywhere,
            out_shape=[jax.ShapeDtypeStruct((4, span, width), BF16) for span in spans],
            scratch_shapes=[pltpu.VMEM(self.piece.shape, BF16)] * 2
            + [pltpu.SemaphoreType.DMA((16 * len(spans),))] * 2,
            input_output_aliases={2 + i: i for i in range(len(spans))},
            compiler_params=params(),
            cost_estimate=cost(0, 8 * sum(spans) * width),
            name="place",
        )(self.piece, self.core_piece, *self.whole)


def over_fsdp(grads):
    return lax.psum_scatter(grads, "fsdp", scatter_dimension=0, tiled=True)


def plain_sum(grads, axis=0):
    share = lax.psum_scatter(grads, "fsdp", scatter_dimension=axis, tiled=True)
    return lax.psum(share.astype(F32), "ctx")


def local(
    tokens, chars, segment, char_end, w_qkv, w_out, norm1_gain, norm1_bias, w_up, b_up, w_down,
    norm2_gain, norm2_bias, w_gru, b_gate, w_ftok, w_fchr, w_conv, norm3_gain, norm3_bias,
    norm4_gain, norm4_bias, d_token, d_char,
):
    count, me = lax.axis_size("ctx"), lax.axis_index("ctx")
    shards = lax.axis_size("fsdp")
    batch, rows, width = tokens.shape
    char_rows = chars.shape[1]
    total_rows = batch * rows
    heads = heads_here(batch, count)
    padded_rows = -(-char_rows // 8) * 8

    def gather(weight, axis=0):
        return lax.all_gather(weight, "fsdp", axis=axis, tiled=True)

    own_width = norm1_gain.shape[0]
    vectors = (
        norm1_gain, norm1_bias, norm2_gain, norm2_bias, b_gate, norm3_gain, norm3_bias,
        norm4_gain, norm4_bias,
    )
    columns = jnp.stack(vectors, axis=1)
    columns = jnp.concatenate([columns, b_up.reshape(-1, own_width).T], axis=1)
    small_count = columns.shape[1]
    wide_gru = w_gru.shape[1]
    columns = jnp.pad(columns, ((0, 0), (0, 128 - small_count)))
    width_qkv = w_qkv.shape[1]
    if heads:
        group, part = me % (HEADS // heads), heads * HEAD_DIM
        w_heads = jnp.concatenate(
            [
                lax.dynamic_slice_in_dim(w_qkv, kind * width + group * part, part, 1)
                for kind in range(3)
            ],
            axis=1,
        )
        w_pieces = [w_heads] + [flip(w_heads, "fsdp", other) for other in (1, 2, 3)]
    else:
        w_qkv = gather(w_qkv)
    w_gru = gather(jnp.concatenate([w_gru, columns], axis=1))
    w_out = gather(w_out)
    w_up = gather(w_up)
    columns = w_gru[:, wide_gru : wide_gru + small_count].astype(F32)
    (
        norm1_gain, norm1_bias, norm2_gain, norm2_bias, b_gate, norm3_gain, norm3_bias,
        norm4_gain, norm4_bias,
    ) = (columns[:, i][None, :] for i in range(9))
    b_up = jnp.swapaxes(columns[:, 9:].reshape(shards, own_width, -1), 1, 2).reshape(1, -1)
    w_down = gather(w_down)
    if routed():
        first_taps = SpreadGather([w_conv[0], w_conv[1]])
        last_tap = SpreadGather([w_conv[2], jnp.concatenate([w_ftok, w_fchr], axis=1)])
    else:
        w_ftok = gather(w_ftok)
        w_fchr = gather(w_fchr)
        w_conv = gather(w_conv, 1)

    start = jnp.concatenate([jnp.zeros((batch, 1), jnp.int32), char_end[:, :-1] + 1], axis=1)
    change = (segment[:, 1:] != segment[:, :-1]).astype(F32)
    first = jnp.concatenate([jnp.broadcast_to((me == 0).astype(F32), (batch, 1)), change], axis=1)
    last = jnp.concatenate(
        [change, jnp.broadcast_to((me == count - 1).astype(F32), (batch, 1))], axis=1
    )
    flat_tokens = tokens.reshape(total_rows, width)
    chars_pad = jnp.pad(chars, ((0, 0), (0, padded_rows - char_rows), (0, 0)))
    if routed():
        first_taps.double(4)
        last_tap.double(1)
    gate, cand, decay, cum, state, edges = gru_forward(
        chars_pad, w_gru, b_gate, start[:, None], first[:, None], char_end[:, None],
        last[:, None], char_rows,
    )

    if heads:
        ids = segment.astype(BF16)[:, None, :]
        ids = jnp.pad(ids, ((0, 0), (0, 7), (0, width - rows)))
        sent = jnp.repeat(jnp.concatenate([tokens, ids], axis=1), HEADS // heads, axis=0)
        tokens_all = lax.all_to_all(sent, "ctx", 0, 0, tiled=True)
        packed_context, kept, *saved, w_heads = attend(tokens_all, w_pieces, edges, heads, rows)
        first_taps.double(2, state)
        last_tap.double(4, state)
        first_taps.place_own(packed_context)
        last_tap.place_own(packed_context)
        received = lax.all_to_all(packed_context.reshape(count, rows, -1), "ctx", 0, 0, tiled=True)
        received = after(received, *first_taps.whole, *last_tap.whole)
        context_b, edges_all = unpack(received, heads, batch)
    else:
        qkv = matmul(flat_tokens, w_qkv).astype(BF16).reshape(batch, rows, -1)
        results = [gathered_attention(qkv[i], segment[i]) for i in range(batch)]
        context_b = jnp.concatenate([r[0].reshape(rows, width) for r in results]).astype(BF16)
        edges_all = all_edges(edges)

    attn = matmul(context_b, w_out)
    hidden1, kept1 = layer_norm(flat_tokens.astype(F32) + attn, norm1_gain, norm1_bias)
    hidden1_b = hidden1.astype(BF16)
    inner_b, slope = feed_forward(hidden1_b, w_up, b_up)
    ffn = matmul(inner_b, w_down)
    hidden2, kept2 = layer_norm(hidden1 + ffn, norm2_gain, norm2_bias)
    hidden2_b = hidden2.astype(BF16)
    if routed():
        first_taps.double(1, context_b)
        last_tap.double(2, context_b)
        first_taps.cores(inner_b)
        last_tap.cores(inner_b)
        w_conv = [
            weight.reshape(-1, 2 * width) for weight in first_taps.finish() + last_tap.finish()
        ]
        w_ftok, w_fchr = w_conv[3][:, :width], w_conv[3][:, width:]

    char_tok, enter = gather_states(
        state, cum, edges_all, char_end[:, :, None], start[:, :, None]
    )
    char_tok_b = char_tok.astype(BF16)
    joined = jnp.concatenate(
        [matmul(hidden2_b, w_ftok), matmul(char_tok_b, w_fchr)], axis=1
    ).astype(BF16)

    two = 2 * width
    if routed():
        inner_own = own_columns(inner_b)
        joined = after(joined, *inner_own[1:])
        joined_own = own_columns(joined)
    blocks = joined.reshape(batch, rows, two)
    later, earlier = shifted(blocks, *neighbours(blocks))
    taps = (later.reshape(total_rows, two), joined, earlier.reshape(total_rows, two))
    conv = matmul(taps[1], w_conv[1]) + matmul(taps[0], w_conv[0]) + matmul(taps[2], w_conv[2])
    token_out, kept3 = layer_norm(hidden2 + conv[:, :width], norm3_gain, norm3_bias)
    char_out, kept4 = layer_norm(char_tok + conv[:, width:], norm4_gain, norm4_bias)

    d_in3, gain3_grad, bias3_grad = layer_norm_back(
        d_token.reshape(total_rows, width).astype(F32), norm3_gain, kept3
    )
    d_in4, gain4_grad, bias4_grad = layer_norm_back(
        d_char.reshape(total_rows, width).astype(F32), norm4_gain, kept4
    )
    d_conv = jnp.concatenate([d_in3, d_in4], axis=1).astype(BF16)
    d_before, d_after = neighbours(d_conv.reshape(batch, rows, two))
    if routed():
        d_conv = after(d_conv, *joined_own[1:])
    d_later, d_earlier = shifted(d_conv.reshape(batch, rows, two), d_before, d_after)
    d_joined = (
        matmul_nt(d_conv, w_conv[1])
        + matmul_nt(d_earlier.reshape(total_rows, two), w_conv[0])
        + matmul_nt(d_later.reshape(total_rows, two), w_conv[2])
    ).astype(BF16)
    if routed():
        d_all = gather(
            jnp.concatenate([d_conv.reshape(batch, rows, two), d_before, d_after], axis=1)
        )
    else:
        conv_sum = plain_sum(jnp.stack([matmul_tn(tap, d_conv).astype(BF16) for tap in taps]), 1)

    d_tok_part, d_chr_part = d_joined[:, :width], d_joined[:, width:]
    d_hidden2 = d_in3 + matmul_nt(d_tok_part, w_ftok)
    d_char_tok = d_in4 + matmul_nt(d_chr_part, w_fchr)

    end_line, start_line = char_end[:, None], start[:, None]
    spread, back_cum, carried, back_edges = gru_back(
        d_char_tok.reshape(batch, rows, width), decay, end_line, start_line, char_rows
    )

    d_in2, gain2_grad, bias2_grad = layer_norm_back(d_hidden2, norm2_gain, kept2)
    d_ffn = d_in2.astype(BF16)
    reduced = over_fsdp if routed() else plain_sum
    if routed():
        d_ffn_all = gather(d_ffn[None])
    else:
        second_sum = plain_sum(matmul_tn(inner_b, d_ffn).astype(BF16))
    d_pre = matmul_nt(d_ffn, w_down) * slope.astype(F32)
    bup_grad = jnp.sum(d_pre, axis=0)
    d_pre_low = d_pre.astype(BF16)
    d_hidden1 = d_in2 + matmul_nt(d_pre_low, w_up)
    d_in1, gain1_grad, bias1_grad = layer_norm_back(d_hidden1, norm1_gain, kept1)
    d_attn = d_in1.astype(BF16)
    if heads:
        sent = send_grad(d_attn, w_out, back_edges, heads, batch)
        hidden1_b = after(hidden1_b, sent)
    third = gradients(hidden1_b, context_b, hidden2_b, char_tok_b, d_pre_low, d_attn, d_joined)
    third_sum = reduced(third)

    if heads:
        conv_pieces = [after(joined_own[0], sent, third)] + joined_own[1:]
        first_chain = CtxSum.begun(*conv_gradient(conv_pieces, d_all, rows, 0))
        other_chain = CtxSum.begun(*conv_gradient(conv_pieces, d_all, rows, 1), OTHER_STEPS)
        received = lax.all_to_all(sent, "ctx", 0, 0, tiled=True)
        received = after(received, first_chain.sent, other_chain.sent)
        d_tok_part, heads_grad, back_enter = attend_back(
            tokens_all, w_heads, saved, kept, received.reshape(count * rows, -1), edges_all,
            heads, rows,
        )
        token_chain = TokenSum(d_tok_part.reshape(2, 2, 2, rows, width))
        last = other_chain.advance(first_chain.advance(heads_grad))
        gate = after(gate, last)
    else:
        back_enter = back_entering(edges_all, all_edges(back_edges))
        d_context = matmul_nt(d_attn, w_out).reshape(batch, rows, width)
        d_qkv = jnp.concatenate(
            [
                gathered_attention_back(
                    qkv[i], segment[i], results[i][0], results[i][1], d_context[i]
                )
                for i in range(batch)
            ]
        )
    d_gate_in, bgate_grad = gru_grad(
        gate, cand, decay, cum, state, enter, spread, back_cum, carried, back_enter, char_rows
    )
    d_gate_in = d_gate_in.reshape(batch * padded_rows, -1)
    d_chars = matmul_nt(d_gate_in, w_gru[:, :wide_gru]).astype(BF16)
    d_chars = d_chars.reshape(batch, padded_rows, width)[:, :char_rows]

    if not heads:
        heads_grad = matmul_tn(flat_tokens, d_qkv)
        d_tokens = matmul_nt(d_qkv, w_qkv)

    small = [
        gain1_grad, bias1_grad, gain2_grad, bias2_grad, jnp.sum(bgate_grad, axis=(0, 1)),
        gain3_grad, bias3_grad, gain4_grad, bias4_grad,
    ]
    up_small = jnp.swapaxes(bup_grad.reshape(shards, -1, width // shards), 0, 1)
    small = jnp.concatenate([value[None] for value in small] + [up_small.reshape(-1, width)])
    small = jnp.pad(small, ((0, 16 - small_count), (0, 0)))

    def last_sum(*others):
        gates = after(d_gate_in, *others) if others else d_gate_in
        return last_gradients(
            chars_pad.reshape(batch * padded_rows, width), gates, small, heads_grad
        )

    widths = ((width,), (w_up.shape[1],) + (width,) * 3, (wide_gru, 128, width_qkv))
    if routed():
        own_wide = wide_gru + 128
        chains = dict(
            A=first_chain,
            B=other_chain,
            X=token_chain,
            T=CtxSum(third_sum),
        )

        def begin_down(*others):
            chains["D"] = CtxSum.begun(*down_gradient(after(inner_own, *others), d_ffn_all))
            return chains["D"].sent

        def begin_last(*others):
            chains["last"] = reduced(last_sum(*others))

        def begin_G(*others):
            value = after(chains["last"], *others)
            chains["G"] = CtxSum(value[:, :own_wide])
            chains["K"] = HeadSum(value[:, own_wide:])
            return chains["G"].advance()

        finish = dict(
            A=lambda value, done: settle_half(value, STEPS, 0),
            B=lambda value, done: settle_half(value, OTHER_STEPS, 1, done.pop("A")),
            D=lambda value, done: settle(value, widths[0]),
            T=lambda value, done: settle(value, widths[1]),
            G=lambda value, done: settle(value, widths[2][:2]),
            K=lambda value, done: spread_columns(value, heads),
            X=lambda value, done: value.reshape(total_rows, width),
        )
        done = run_in_order(chains, finish, dict(D=begin_down, G=begin_G, last=begin_last))
        (down_sum,), third = done["D"], done["T"]
        conv_sum = done["B"]
        fourth = [*done["G"], done["K"]]
        d_tokens = done["X"]
    else:
        (down_sum,), third, fourth = (
            jnp.split(value, [sum(split[:i]) for i in range(1, len(split))], axis=1)
            for value, split in zip((second_sum, third_sum, reduced(last_sum())), widths)
        )
    d_tokens = (d_in1 + d_tokens).astype(BF16)
    vector = fourth[1]
    return (
        token_out.astype(BF16).reshape(batch, rows, width),
        char_out.astype(BF16).reshape(batch, rows, width),
        d_tokens.reshape(batch, rows, width),
        d_chars,
        fourth[2],
        third[1],
        vector[:, 0],
        vector[:, 1],
        third[0],
        jnp.swapaxes(vector[:, 9:small_count], 0, 1).reshape(-1),
        down_sum,
        vector[:, 2],
        vector[:, 3],
        fourth[0],
        vector[:, 4],
        third[2],
        third[3],
        conv_sum,
        vector[:, 5],
        vector[:, 6],
        vector[:, 7],
        vector[:, 8],
    )


def solution(mesh):
    rows = P("fsdp", "ctx", None)
    pairs = P("fsdp", "ctx")
    matrix = P("fsdp", None)
    vector = P("fsdp")
    weights = (
        matrix, matrix, vector, vector, matrix, vector, matrix, vector, vector, matrix, vector,
        matrix, matrix, P(None, "fsdp", None), vector, vector, vector, vector,
    )
    return jax.shard_map(
        local,
        mesh=mesh,
        in_specs=(rows, rows, pairs, pairs) + weights + (rows, rows),
        out_specs=(rows,) * 4 + weights,
        check_vma=False,
    )
```

```python
import functools

import jax
import jax.numpy as jnp
from jax import lax
from jax.experimental import pallas as pl
from jax.experimental.pallas import tpu as pltpu
from jax.sharding import PartitionSpec as P

HEADS = 12
HEAD_DIM = 64
GRU_H = 384
EPSILON = 1e-05
BLOCK_LIMIT = 1024
FAR = 1e9
VMEM_BYTES = 32 * 1024 * 1024

F32 = jnp.float32
BF16 = jnp.bfloat16


def matmul(left, right):
    return jnp.dot(left, right, preferred_element_type=F32)


def matmul_nt(left, right):
    return lax.dot_general(left, right, (((1,), (1,)), ((), ())), preferred_element_type=F32)


def matmul_tn(left, right):
    return lax.dot_general(left, right, (((0,), (0,)), ((), ())), preferred_element_type=F32)


def layer_norm(value, gain, shift):
    center = value - jnp.mean(value, axis=-1, keepdims=True)
    inverse = lax.rsqrt(jnp.mean(center * center, axis=-1, keepdims=True) + EPSILON)
    normed = center * inverse
    return normed * gain + shift, (normed, inverse)


def layer_norm_back(grad, gain, kept):
    normed, inverse = kept
    scaled = grad * gain
    into = inverse * (
        scaled
        - jnp.mean(scaled, axis=-1, keepdims=True)
        - normed * jnp.mean(scaled * normed, axis=-1, keepdims=True)
    )
    return into, jnp.sum(grad * normed, axis=0), jnp.sum(grad, axis=0)


def params(**more):
    return pltpu.CompilerParams(vmem_limit_bytes=VMEM_BYTES, **more)


def cost(flops, moved, transcendentals=0):
    return pl.CostEstimate(
        flops=1, bytes_accessed=1, transcendentals=0
    )


def two_parts(value):
    high = value.astype(BF16)
    return high, (value - high.astype(F32)).astype(BF16)


KINDS = 4


def store_edges(edge_ref, cols, rows):
    parts = [half.astype(F32) for row in rows for half in two_parts(row)]
    parts = parts + [jnp.zeros_like(parts[0])] * (KINDS - len(parts))
    parts = jnp.concatenate(parts, axis=0)
    for sequence in range(edge_ref.shape[0] // KINDS):

        @pl.when(pl.program_id(0) == sequence)
        def store():
            edge_ref[pl.ds(sequence * KINDS, KINDS), cols] = parts


def edges_to_block(edges, rows):
    count = edges.shape[1] // HEAD_DIM
    pieces = [edges[:, i * HEAD_DIM : (i + 1) * HEAD_DIM] for i in range(count)]
    pieces.append(jnp.zeros((rows - count * edges.shape[0], HEAD_DIM), F32))
    return jnp.concatenate(pieces, axis=0).astype(BF16)


def edges_of_block(block):
    block = block.astype(F32)
    count = 2 * GRU_H // HEAD_DIM
    return jnp.concatenate([block[i * 8 : (i + 1) * 8] for i in range(count)], axis=1)


def entering_row(decays, drives, sequence, count, flip):
    me = lax.axis_index("ctx")
    halves = []
    for side in (0, 1):
        cols = slice(side * GRU_H, (side + 1) * GRU_H)
        total = jnp.zeros((1, GRU_H), F32)
        backward = (side == 1) != flip
        order = range(count - 1, 0, -1) if backward else range(count - 1)
        for other in order:
            decay, drive = decays(other, sequence, cols), drives(other, sequence, cols)
            there = me < other if backward else me > other
            total = jnp.where(there, decay * total + drive, total)
        halves.append(total)
    return jnp.concatenate(halves, axis=1)


def edge_reader(ref, kind):
    def read(other, sequence, cols):
        at = sequence * KINDS + 2 * kind
        return ref[other, at : at + 1, cols] + ref[other, at + 1 : at + 2, cols]

    return read


def shift_rows(value, by, fill, up):
    rows = value.shape[0]
    row = lax.broadcasted_iota(jnp.int32, value.shape, 0)
    if up:
        return jnp.where(row < rows - by, pltpu.roll(value, rows - by, 0), fill)
    return jnp.where(row >= by, pltpu.roll(value, by, 0), fill)


def scan_rows(decay, drive, up):
    by = 1
    while by < decay.shape[0]:
        drive = drive + decay * shift_rows(drive, by, 0.0, up)
        decay = decay * shift_rows(decay, by, 1.0, up)
        by = by * 2
    return decay, drive


def gru_forward_kernel(
    real, chars_ref, w_ref, bias_ref, start_ref, first_ref, end_ref, last_ref,
    gate_ref, cand_ref, decay_ref, cum_ref, state_ref, edge_ref,
):
    columns = matmul(chars_ref[0], w_ref[:, : 4 * GRU_H])
    rows = columns.shape[0]
    tokens = start_ref.shape[2]
    place = lax.broadcasted_iota(jnp.int32, (rows, tokens), 0)
    inside = lax.broadcasted_iota(jnp.int32, (rows, GRU_H), 0) < real
    resets = [
        jnp.sum(jnp.where(place == at[0], flag[0], 0.0), axis=1, keepdims=True)
        for at, flag in ((start_ref, first_ref), (end_ref, last_ref))
    ]
    for side in (0, 1):
        cols = pl.ds(side * GRU_H, GRU_H)
        base = 2 * side * GRU_H
        gate = jax.nn.sigmoid(columns[:, base : base + GRU_H] + bias_ref[:, cols])
        cand = jnp.tanh(columns[:, base + GRU_H : base + 2 * GRU_H])
        decay = jnp.where(inside, gate * (1.0 - resets[side]), 1.0)
        drive = jnp.where(inside, (1.0 - gate) * cand, 0.0)
        gate_ref[0, :, cols] = gate
        cand_ref[0, :, cols] = cand
        decay_ref[0, :, cols] = decay
        cum, state = scan_rows(decay, drive, side == 1)
        cum_ref[0, :, cols] = cum
        state_ref[0, :, cols] = state
        at = 0 if side else real - 1
        store_edges(edge_ref, cols, (cum[at : at + 1], state[at : at + 1]))


def char_tok_kernel(state_ref, cum_ref, edges_ref, end_ref, start_ref, out_ref, enter_ref):
    batch, tokens = end_ref.shape[:2]
    for sequence in range(batch):
        enter = entering_row(
            edge_reader(edges_ref, 0), edge_reader(edges_ref, 1), sequence, edges_ref.shape[0],
            False,
        )
        enter_ref[sequence] = enter
        state = state_ref[sequence] + cum_ref[sequence] * enter
        high, low = two_parts(state)
        place = lax.broadcasted_iota(jnp.int32, (tokens, state.shape[0]), 1)
        for side, at in ((0, end_ref), (1, start_ref)):
            pick = jnp.where(place == at[sequence], 1.0, 0.0).astype(BF16)
            cols = slice(side * GRU_H, (side + 1) * GRU_H)
            out_ref[pl.ds(sequence * tokens, tokens), pl.ds(side * GRU_H, GRU_H)] = matmul(
                pick, high[:, cols]
            ) + matmul(pick, low[:, cols])


def gru_back_kernel(
    real, grad_ref, decay_ref, end_ref, start_ref, spread_ref, cum_ref, carried_ref, edge_ref
):
    rows = decay_ref.shape[1]
    tokens = end_ref.shape[2]
    place = lax.broadcasted_iota(jnp.int32, (rows, tokens), 0)
    high, low = two_parts(grad_ref[0])
    for side, at in ((0, end_ref), (1, start_ref)):
        put = jnp.where(place == at[0], 1.0, 0.0).astype(BF16)
        cols = slice(side * GRU_H, (side + 1) * GRU_H)
        there = pl.ds(side * GRU_H, GRU_H)
        spread = matmul(put, high[:, cols]) + matmul(put, low[:, cols])
        decay = decay_ref[0, :, there]
        cum, carried = scan_rows(decay, decay * spread, side == 0)
        spread_ref[0, :, there] = spread
        cum_ref[0, :, there] = cum
        carried_ref[0, :, there] = carried
        at = real - 1 if side else 0
        store_edges(edge_ref, there, (carried[at : at + 1],))


def gru_grad_kernel(
    real, gate_ref, cand_ref, decay_ref, cum_ref, state_ref, enter_ref,
    spread_ref, back_cum_ref, carried_ref, back_enter_ref, out_ref, bias_ref,
):
    rows = gate_ref.shape[1]
    inside = lax.broadcasted_iota(jnp.int32, (rows, GRU_H), 0) < real
    for side in (0, 1):
        there = pl.ds(side * GRU_H, GRU_H)
        gate = gate_ref[0, :, there]
        cand = cand_ref[0, :, there]
        decay = decay_ref[0, :, there]
        enter = enter_ref[0, :, there]
        back_enter = back_enter_ref[0, :, there]
        state = state_ref[0, :, there] + cum_ref[0, :, there] * enter
        carried = carried_ref[0, :, there] + back_cum_ref[0, :, there] * back_enter
        previous = shift_rows(state, 1, enter, side == 1)
        adjoint = spread_ref[0, :, there] + shift_rows(carried, 1, back_enter, side == 0)
        adjoint = jnp.where(inside, adjoint, 0.0)
        rest = adjoint * (1.0 - gate)
        to_gate = rest * (previous * decay - cand * gate)
        to_cand = rest * (1.0 - cand * cand)
        out_ref[0, :, pl.ds(2 * side * GRU_H, GRU_H)] = to_gate.astype(BF16)
        out_ref[0, :, pl.ds((2 * side + 1) * GRU_H, GRU_H)] = to_cand.astype(BF16)
        bias_ref[0, :, there] = jnp.sum(to_gate, axis=0, keepdims=True)


def per_sequence(*tail):
    return pl.BlockSpec((1,) + tail, lambda s: (s,) + (0,) * len(tail))


def whole_block(*shape):
    return pl.BlockSpec(shape, lambda s: (0,) * len(shape))


def gru_forward(chars, w_gru, bias, start, first, end, last, real):
    batch, rows, width = chars.shape
    tokens = start.shape[2]
    two = 2 * GRU_H
    kept = jax.ShapeDtypeStruct((batch, rows, two), F32)
    return pl.pallas_call(
        functools.partial(gru_forward_kernel, real),
        grid=(batch,),
        in_specs=[per_sequence(rows, width), whole_block(width, w_gru.shape[1]), whole_block(1, two)]
        + [per_sequence(1, tokens)] * 4,
        out_specs=[per_sequence(rows, two)] * 5 + [whole_block(KINDS * batch, two)],
        out_shape=[kept] * 5 + [jax.ShapeDtypeStruct((KINDS * batch, two), F32)],
        compiler_params=params(),
        cost_estimate=cost(
            2 * batch * rows * width * 2 * two,
            chars.size * 2 + w_gru.size * 2 + 20 * batch * rows * two,
            2 * batch * rows * two,
        ),
        name="gru_forward",
    )(chars, w_gru, bias, start, first, end, last)


def gather_states(state, cum, edges, end, start):
    batch, rows, two = state.shape
    tokens = end.shape[1]
    return pl.pallas_call(
        char_tok_kernel,
        out_shape=[
            jax.ShapeDtypeStruct((batch * tokens, two), F32),
            jax.ShapeDtypeStruct((batch, 1, two), F32),
        ],
        compiler_params=params(),
        cost_estimate=cost(
            4 * batch * rows * tokens * two, 8 * batch * rows * two + 4 * batch * tokens * two
        ),
        name="gather_states",
    )(state, cum, edges, end, start)


def gru_back(grad, decay, end, start, real):
    batch, rows, two = decay.shape
    tokens = end.shape[2]
    kept = jax.ShapeDtypeStruct((batch, rows, two), F32)
    return pl.pallas_call(
        functools.partial(gru_back_kernel, real),
        grid=(batch,),
        in_specs=[per_sequence(tokens, two), per_sequence(rows, two)]
        + [per_sequence(1, tokens)] * 2,
        out_specs=[per_sequence(rows, two)] * 3 + [whole_block(KINDS * batch, two)],
        out_shape=[kept] * 3 + [jax.ShapeDtypeStruct((KINDS * batch, two), F32)],
        compiler_params=params(),
        cost_estimate=cost(
            4 * batch * rows * tokens * two, 16 * batch * rows * two + 4 * batch * tokens * two
        ),
        name="gru_back",
    )(grad, decay, end, start)


def gru_grad(gate, cand, decay, cum, state, enter, spread, back_cum, carried, back_enter, real):
    batch, rows, two = decay.shape
    big = per_sequence(rows, two)
    row = per_sequence(1, two)
    return pl.pallas_call(
        functools.partial(gru_grad_kernel, real),
        grid=(batch,),
        in_specs=[big] * 5 + [row] + [big] * 3 + [row],
        out_specs=[per_sequence(rows, 2 * two), row],
        out_shape=[
            jax.ShapeDtypeStruct((batch, rows, 2 * two), BF16),
            jax.ShapeDtypeStruct((batch, 1, two), F32),
        ],
        compiler_params=params(),
        cost_estimate=cost(20 * batch * rows * two, 36 * batch * rows * two),
        name="gru_grad",
    )(gate, cand, decay, cum, state, enter, spread, back_cum, carried, back_enter)


def all_edges(edges):
    return lax.all_gather(edges, "ctx", axis=0)


def entering_kernel(decay_ref, drive_ref, out_ref):
    for sequence in range(out_ref.shape[0]):
        out_ref[sequence] = entering_row(
            edge_reader(decay_ref, 0), edge_reader(drive_ref, 0), sequence, decay_ref.shape[0],
            True,
        )


def back_entering(decays, drives):
    batch, two = decays.shape[1] // KINDS, decays.shape[2]
    return pl.pallas_call(
        entering_kernel,
        out_shape=jax.ShapeDtypeStruct((batch, 1, two), F32),
        compiler_params=params(),
        name="back_entering",
    )(decays, drives)


def attend_kernel(
    heads, tokens, tok_ref, own_ref, core_ref, far_ref, far_core_ref, edge_ref, out_ref, kept_ref,
    query_ref, key_ref, value_ref, w_ref,
):
    part = heads * HEAD_DIM
    rows = out_ref.shape[0]
    step = pl.program_id(0)

    @pl.when(step == 0)
    def build():
        eye = jnp.where(
            lax.broadcasted_iota(jnp.int32, (HEAD_DIM, HEAD_DIM), 0)
            == lax.broadcasted_iota(jnp.int32, (HEAD_DIM, HEAD_DIM), 1),
            1.0,
            0.0,
        ).astype(BF16)
        number = lax.broadcasted_iota(jnp.int32, (HEAD_DIM, tokens), 0).astype(F32)
        shard = own_ref.shape[0]
        for other, piece_ref in enumerate((own_ref, core_ref, far_ref, far_core_ref)):
            at = jnp.bitwise_xor(lax.axis_index("fsdp"), other) * shard
            w_ref[pl.ds(pl.multiple_of(at, shard), shard)] = piece_ref[...]
        ones = jnp.ones((tokens, HEAD_DIM), BF16)

        def block(source, carry):
            qkv = matmul(tok_ref[source, :tokens], w_ref[...])
            ids = tok_ref[source, tokens:].astype(F32)[0:1, :tokens]
            marks = matmul_tn(jnp.where(number == ids, 1.0, 0.0).astype(BF16), eye)
            blocked = ((marks - 1.0) * FAR).astype(BF16)
            marks = marks.astype(BF16)
            here = pl.ds(pl.multiple_of(source * tokens, tokens), tokens)
            for head in range(heads):
                query, key, value = (
                    qkv[:, kind * part + head * HEAD_DIM : kind * part + (head + 1) * HEAD_DIM]
                    for kind in range(3)
                )
                query = query.astype(BF16) * jnp.asarray(HEAD_DIM ** (-0.5), BF16)
                query_ref[head, here] = jnp.concatenate([query, marks], axis=1)
                key_ref[head, here] = jnp.concatenate([key.astype(BF16), blocked], axis=1)
                value_ref[head, here] = jnp.concatenate([value.astype(BF16), ones], axis=1)
            return carry

        lax.fori_loop(0, tok_ref.shape[0], block, 0)

    here = pl.ds(pl.multiple_of(step * rows, rows), rows)
    outs = []
    for head in range(heads):
        expvals = jnp.exp(matmul_nt(query_ref[head, here], key_ref[head]))
        both = matmul(expvals.astype(BF16), value_ref[head])
        total = both[:, HEAD_DIM:]
        context = both[:, :HEAD_DIM] / total
        kept_ref[:, pl.ds(head * 2 * HEAD_DIM, 2 * HEAD_DIM)] = jnp.concatenate(
            [context, total], axis=1
        )
        outs.append(context.astype(BF16))
    block = edges_to_block(edge_ref[...], tokens)
    outs.append(jnp.concatenate([block] * (rows // tokens), axis=0))
    out_ref[...] = jnp.concatenate(outs, axis=1)


def attend_back_kernel(
    heads, tokens, tok_ref, w_ref, query_ref, key_ref, value_ref, kept_ref, grad_ref, edges_ref,
    out_ref, w_grad_ref, enter_ref, grad_scr, edge_scr,
):
    part = heads * HEAD_DIM
    rows = out_ref.shape[0]
    step = pl.program_id(0)

    @pl.when(step == 0)
    def build():
        lane = lax.broadcasted_iota(jnp.int32, (grad_ref.shape[0], HEAD_DIM), 1)
        for head in range(heads):
            at = head * HEAD_DIM
            context = kept_ref[:, 2 * at : 2 * at + HEAD_DIM]
            total = kept_ref[:, 2 * at + HEAD_DIM : 2 * at + 2 * HEAD_DIM]
            grad = grad_ref[:, at : at + HEAD_DIM].astype(F32) / total
            delta = jnp.sum(grad * context, axis=1, keepdims=True)
            high, low = two_parts(-delta)
            extra = jnp.where(
                lane == 0, high.astype(F32), jnp.where(lane == 1, low.astype(F32), 0.0)
            )
            grad_scr[head] = jnp.concatenate([grad, extra], axis=1).astype(BF16)
        for other in range(edges_ref.shape[0]):
            edge_scr[other] = edges_of_block(
                grad_ref[other * tokens : (other + 1) * tokens, part : part + HEAD_DIM]
            )
        for sequence in range(enter_ref.shape[0]):
            enter_ref[sequence] = entering_row(
                edge_reader(edges_ref, 0), edge_reader(edge_scr, 0), sequence,
                edges_ref.shape[0], True,
            )
        w_grad_ref[...] = jnp.zeros_like(w_grad_ref)

    here = pl.ds(pl.multiple_of(step * rows, rows), rows)
    scale = HEAD_DIM ** (-0.5)
    d_query, d_key, d_value = [], [], []
    for head in range(heads):
        expvals = jnp.exp(matmul_nt(query_ref[head, here], key_ref[head]))
        inner = matmul_nt(grad_scr[head, here], value_ref[head])
        d_scores = (expvals * inner).astype(BF16)
        d_query.append((matmul(d_scores, key_ref[head])[:, :HEAD_DIM] * scale).astype(BF16))
        expvals = jnp.exp(matmul_nt(key_ref[head, here], query_ref[head]))
        inner = matmul_nt(value_ref[head, here], grad_scr[head])
        d_scores = (expvals * inner).astype(BF16)
        d_key.append(matmul(d_scores, query_ref[head])[:, :HEAD_DIM].astype(BF16))
        d_value.append(
            matmul(expvals.astype(BF16), grad_scr[head])[:, :HEAD_DIM].astype(BF16)
        )
    d_qkv = jnp.concatenate(d_query + d_key + d_value, axis=1)
    out_ref[...] = matmul_nt(d_qkv, w_ref[...]).astype(BF16)
    blocks = rows // tokens
    tok = jnp.concatenate(
        [tok_ref[step * blocks + block, :tokens] for block in range(blocks)], axis=0
    )
    w_grad_ref[...] += matmul_tn(tok, d_qkv)


def unpack_kernel(groups, part, in_ref, out_ref, edge_ref):
    for group in range(groups):
        edge_ref[group] = edges_of_block(in_ref[group, :, part:])
    out_ref[...] = jnp.concatenate([in_ref[group, :, :part] for group in range(groups)], axis=1)


def spread_columns_kernel(heads, in_ref, out_ref):
    groups, part = in_ref.shape[0], heads * HEAD_DIM
    width = groups * part
    mine = lax.rem(lax.axis_index("ctx"), groups)
    for case in range(groups):

        @pl.when(mine == case)
        def place():
            for kind in range(3):
                pieces = [
                    in_ref[case ^ group, :, kind * part : (kind + 1) * part].astype(F32)
                    for group in range(groups)
                ]
                out_ref[:, pl.ds(kind * width, width)] = jnp.concatenate(pieces, axis=1)


def send_grad_kernel(groups, part, grad_ref, w_ref, edge_ref, out_ref):
    d_context = matmul_nt(grad_ref[...], w_ref[...]).astype(BF16)
    block = edges_to_block(edge_ref[...], grad_ref.shape[0])
    for group in range(groups):
        out_ref[group] = jnp.concatenate(
            [d_context[:, group * part : (group + 1) * part], block], axis=1
        )


def heads_here(batch, count):
    if batch * HEADS % count != 0 or not routed():
        return 0
    heads = batch * HEADS // count
    if heads > HEADS or HEADS % heads != 0 or heads % 2 == 0 or batch * KINDS != 8:
        return 0
    return heads


def attend(tokens_all, w_pieces, edges, heads, tokens):
    count, rows, width = tokens_all.shape
    length = count * tokens
    block = 256
    part = heads * HEAD_DIM
    out_wide = part + HEAD_DIM
    wide = jax.ShapeDtypeStruct((heads, length, 2 * HEAD_DIM), BF16)
    return pl.pallas_call(
        functools.partial(attend_kernel, heads, tokens),
        grid=(length // block,),
        in_specs=[
            pl.BlockSpec((count, rows, width), lambda i: (0, 0, 0)),
        ]
        + [pl.BlockSpec(w_pieces[0].shape, lambda i: (0, 0))] * 4
        + [pl.BlockSpec(edges.shape, lambda i: (0, 0))],
        out_specs=[
            pl.BlockSpec((block, out_wide), lambda i: (i, 0)),
            pl.BlockSpec((block, 2 * part), lambda i: (i, 0)),
        ]
        + [pl.BlockSpec(wide.shape, lambda i: (0, 0, 0))] * 3
        + [pl.BlockSpec((width, 3 * part), lambda i: (0, 0))],
        out_shape=[
            jax.ShapeDtypeStruct((length, out_wide), BF16),
            jax.ShapeDtypeStruct((length, 2 * part), F32),
            wide,
            wide,
            wide,
            jax.ShapeDtypeStruct((width, 3 * part), BF16),
        ],
        compiler_params=params(),
        cost_estimate=cost(
            8 * heads * length * length * HEAD_DIM,
            length * (width * 2 + out_wide * 2 + 8 * part),
            heads * length * length,
        ),
        name="attend",
    )(tokens_all, *w_pieces, edges)


def attend_back(tokens_all, w_heads, saved, kept, grads, edges, heads, tokens):
    count, rows, width = tokens_all.shape
    length = count * tokens
    block = 256
    part = heads * HEAD_DIM
    batch, two = edges.shape[1] // KINDS, edges.shape[2]
    wide = (heads, length, 2 * HEAD_DIM)
    return pl.pallas_call(
        functools.partial(attend_back_kernel, heads, tokens),
        grid=(length // block,),
        in_specs=[
            pl.BlockSpec((count, rows, width), lambda i: (0, 0, 0)),
            pl.BlockSpec(w_heads.shape, lambda i: (0, 0)),
        ]
        + [pl.BlockSpec(wide, lambda i: (0, 0, 0))] * 3
        + [
            pl.BlockSpec((length, 2 * part), lambda i: (0, 0)),
            pl.BlockSpec((length, part + HEAD_DIM), lambda i: (0, 0)),
            pl.BlockSpec(edges.shape, lambda i: (0, 0, 0)),
        ],
        out_specs=[
            pl.BlockSpec((block, width), lambda i: (i, 0)),
            pl.BlockSpec(w_heads.shape, lambda i: (0, 0)),
            pl.BlockSpec((batch, 1, two), lambda i: (0, 0, 0)),
        ],
        out_shape=[
            jax.ShapeDtypeStruct((length, width), BF16),
            jax.ShapeDtypeStruct(w_heads.shape, F32),
            jax.ShapeDtypeStruct((batch, 1, two), F32),
        ],
        scratch_shapes=[pltpu.VMEM(wide, BF16), pltpu.VMEM(edges.shape, F32)],
        compiler_params=params(),
        cost_estimate=cost(
            28 * heads * length * length * HEAD_DIM,
            length * (width * 4 + 8 * part + 2 * part),
            2 * heads * length * length,
        ),
        name="attend_back",
    )(tokens_all, w_heads, *saved, kept, grads, edges)


def unpack(received, heads, batch):
    count, rows, wide = received.shape
    groups, part = HEADS // heads, heads * HEAD_DIM
    width = groups * part
    return pl.pallas_call(
        functools.partial(unpack_kernel, groups, part),
        grid=(batch,),
        in_specs=[pl.BlockSpec((groups, rows, wide), lambda s: (s, 0, 0))],
        out_specs=[
            pl.BlockSpec((rows, width), lambda s: (s, 0)),
            pl.BlockSpec((groups, KINDS * batch, 2 * GRU_H), lambda s: (s, 0, 0)),
        ],
        out_shape=[
            jax.ShapeDtypeStruct((batch * rows, width), BF16),
            jax.ShapeDtypeStruct((count, KINDS * batch, 2 * GRU_H), F32),
        ],
        compiler_params=params(),
        cost_estimate=cost(0, 2 * received.size + 2 * batch * rows * width),
        name="unpack",
    )(received)


def spread_columns(pieces, heads):
    groups, rows, wide = pieces.shape
    return pl.pallas_call(
        functools.partial(spread_columns_kernel, heads),
        out_shape=jax.ShapeDtypeStruct((rows, groups * wide), F32),
        compiler_params=params(),
        cost_estimate=cost(1, 1),
        name="spread_columns",
    )(pieces)


def send_grad(d_attn, w_out, edges, heads, batch):
    total, width = d_attn.shape
    rows = total // batch
    groups, part = HEADS // heads, heads * HEAD_DIM
    wide = part + HEAD_DIM
    return pl.pallas_call(
        functools.partial(send_grad_kernel, groups, part),
        grid=(batch,),
        in_specs=[
            pl.BlockSpec((rows, width), lambda s: (s, 0)),
            whole_block(width, width),
            whole_block(*edges.shape),
        ],
        out_specs=pl.BlockSpec((groups, rows, wide), lambda s: (s, 0, 0)),
        out_shape=jax.ShapeDtypeStruct((batch * groups, rows, wide), BF16),
        compiler_params=params(),
        cost_estimate=cost(
            2 * total * width * width, 2 * (d_attn.size + w_out.size + total * groups * wide)
        ),
        name="send_grad",
    )(d_attn, w_out, edges)


def feed_forward_kernel(hidden_ref, w_ref, bias_ref, inner_ref, slope_ref):
    pre = matmul(hidden_ref[...], w_ref[...]) + bias_ref[...]
    at = jnp.abs(pre) * (0.5**0.5)
    near = 1.0 / (1.0 + 0.3275911 * at)
    gauss = jnp.exp(-at * at)
    series = 1.061405429
    for term in (-1.453152027, 1.421413741, -0.284496736, 0.254829592):
        series = series * near + term
    tail = 0.5 * series * near * gauss
    below = jnp.where(pre < 0.0, tail, 1.0 - tail)
    inner_ref[...] = (pre * below).astype(BF16)
    slope_ref[...] = (below + pre * gauss * (2.0 * jnp.pi) ** -0.5).astype(BF16)


def feed_forward(hidden, w_up, bias):
    rows, width = hidden.shape
    wide = w_up.shape[1]
    block = 512
    column = pl.BlockSpec((rows, block), lambda i: (0, i))
    return pl.pallas_call(
        feed_forward_kernel,
        grid=(wide // block,),
        in_specs=[
            whole_block(rows, width),
            pl.BlockSpec((width, block), lambda i: (0, i)),
            pl.BlockSpec((1, block), lambda i: (0, i)),
        ],
        out_specs=[column, column],
        out_shape=[jax.ShapeDtypeStruct((rows, wide), BF16)] * 2,
        compiler_params=params(),
        cost_estimate=cost(
            2 * rows * width * wide, 2 * (hidden.size + w_up.size + 2 * rows * wide), rows * wide
        ),
        name="feed_forward",
    )(hidden, w_up, bias)


def gradients_kernel(
    blocks, hidden1_ref, context_ref, hidden2_ref, char_ref, pre_ref, attn_ref, joined_ref, out_ref
):
    step = pl.program_id(0)
    width = hidden2_ref.shape[1]

    def put(at, left_ref, right):
        @pl.when((step < blocks) if at is None else (step == blocks + at))
        def store():
            out_ref[...] = matmul_tn(left_ref[...], right()).astype(BF16)

    put(None, hidden1_ref, lambda: pre_ref[...])
    put(0, context_ref, lambda: attn_ref[...])
    put(1, hidden2_ref, lambda: joined_ref[:, :width])
    put(2, char_ref, lambda: joined_ref[:, width:])


def gradients(hidden1, context, hidden2, chars, d_pre, d_attn, d_joined):
    rows, width = hidden1.shape
    blocks = d_pre.shape[1] // width
    whole = whole_block(rows, width)
    return pl.pallas_call(
        functools.partial(gradients_kernel, blocks),
        grid=(blocks + 3,),
        in_specs=[whole] * 4
        + [
            pl.BlockSpec((rows, width), lambda i: (0, jnp.minimum(i, blocks - 1))),
            whole,
            whole_block(rows, 2 * width),
        ],
        out_specs=pl.BlockSpec((width, width), lambda i: (0, i)),
        out_shape=jax.ShapeDtypeStruct((width, (blocks + 3) * width), BF16),
        compiler_params=params(),
        cost_estimate=cost(1, 1),
        name="gradients",
    )(hidden1, context, hidden2, chars, d_pre, d_attn, d_joined)


def store_halves(total, keep_ref, send_ref, lead):
    half = total.shape[0] // 2
    halves = (total[:half].astype(BF16), total[half:].astype(BF16))
    for mine in (0, 1):

        @pl.when(lax.rem(lax.axis_index("ctx"), 2) == mine)
        def store():
            keep_ref[lead] = halves[mine]
            send_ref[lead] = halves[1 - mine]


def down_grad_kernel(own_ref, core_ref, far_ref, far_core_ref, grad_ref, keep_ref, send_ref):
    total = jnp.zeros((own_ref.shape[1], grad_ref.shape[2]), F32)
    for other, inner_ref in enumerate((own_ref, core_ref, far_ref, far_core_ref)):
        source = jnp.bitwise_xor(lax.axis_index("fsdp"), other)
        total = total + matmul_tn(inner_ref[...], grad_ref[source])
    store_halves(total, keep_ref, send_ref, ...)


def down_gradient(inner, grads):
    half = jax.ShapeDtypeStruct((inner[0].shape[1] // 2, grads.shape[2]), BF16)
    return pl.pallas_call(
        down_grad_kernel,
        out_shape=[half, half],
        compiler_params=params(),
        cost_estimate=cost(1, 1),
        name="down_gradient",
    )(*inner, grads)


def conv_grad_kernel(
    own_ref, core_ref, far_ref, far_core_ref, grad_ref, keep_ref, send_ref, side_scr
):
    tap = pl.program_id(0)
    refs = (own_ref, core_ref, far_ref, far_core_ref)
    batch = grad_ref.shape[0] // len(refs)
    rows = side_scr.shape[0] // batch
    shape = (rows, grad_ref.shape[2])
    row = lax.broadcasted_iota(jnp.int32, shape, 0)
    total = jnp.zeros((own_ref.shape[1], grad_ref.shape[2]), F32)
    for other, joined_ref in enumerate(refs):
        first = jnp.bitwise_xor(lax.axis_index("fsdp"), other) * batch
        for block in range(batch):
            here = pl.ds(block * rows, rows)
            grad = grad_ref[first + block].astype(F32)
            mid = grad[:rows]

            @pl.when(tap == 0)
            def earlier():
                moved = pltpu.roll(mid, rows - 1, 0)
                last = jnp.broadcast_to(grad[rows + 1 : rows + 2], shape)
                side_scr[here] = jnp.where(row == rows - 1, last, moved).astype(BF16)

            @pl.when(tap == 1)
            def same():
                side_scr[here] = mid.astype(BF16)

            @pl.when(tap == 2)
            def later():
                moved = pltpu.roll(mid, 1, 0)
                before = jnp.broadcast_to(grad[rows : rows + 1], shape)
                side_scr[here] = jnp.where(row == 0, before, moved).astype(BF16)

        total = total + matmul_tn(joined_ref[...], side_scr[...])
    store_halves(total, keep_ref, send_ref, 0)


def conv_gradient(joined, grads, rows, part):
    count, tall, wide = grads.shape
    wide = wide // 2
    own = joined[0].shape
    out = jax.ShapeDtypeStruct((3, own[1] // 2, wide), BF16)
    return pl.pallas_call(
        conv_grad_kernel,
        grid=(3,),
        in_specs=[pl.BlockSpec(own, lambda k: (0, 0))] * 4
        + [pl.BlockSpec((count, tall, wide), lambda k: (0, 0, part))],
        out_specs=[pl.BlockSpec((1,) + out.shape[1:], lambda k: (k, 0, 0))] * 2,
        out_shape=[out, out],
        scratch_shapes=[pltpu.VMEM((own[0], wide), BF16)],
        compiler_params=params(),
        cost_estimate=cost(1, 1),
        name="conv_gradient",
    )(*joined, grads)


def last_grads_kernel(chars_ref, gates_ref, small_ref, heads_ref, out_ref):
    wide = gates_ref.shape[1]
    narrow = 128
    out_ref[:, :wide] = matmul_tn(chars_ref[...], gates_ref[...]).astype(BF16)
    count = small_ref.shape[0]
    eye = jnp.where(
        lax.broadcasted_iota(jnp.int32, (count, narrow), 0)
        == lax.broadcasted_iota(jnp.int32, (count, narrow), 1),
        1.0,
        0.0,
    ).astype(BF16)
    out_ref[:, wide : wide + narrow] = matmul_tn(small_ref[...].astype(BF16), eye).astype(BF16)
    out_ref[:, wide + narrow :] = heads_ref[...].astype(BF16)


def last_gradients(chars, d_gates, small, heads_grad):
    width = chars.shape[1]
    wide = d_gates.shape[1] + 128 + heads_grad.shape[1]
    return pl.pallas_call(
        last_grads_kernel,
        out_shape=jax.ShapeDtypeStruct((width, wide), BF16),
        compiler_params=params(),
        cost_estimate=cost(1, 1),
        name="last_gradients",
    )(chars, d_gates, small, heads_grad)


def block_size(rows):
    size = min(rows, BLOCK_LIMIT)
    while rows % size != 0:
        size = size - 1
    return size


def split_blocks(array, size):
    return array.reshape((array.shape[0] // size, size) + array.shape[1:])


def to_heads(matrix):
    return matrix.reshape(matrix.shape[0], HEADS, HEAD_DIM)


def masked_exp(query_heads, key_heads, query_seg, key_seg):
    scores = jnp.einsum(
        "qhd,khd->hqk", query_heads, key_heads, preferred_element_type=F32
    ) * HEAD_DIM ** (-0.5)
    same = (query_seg[:, None] == key_seg[None, :])[None, :, :]
    return jnp.where(same, jnp.exp(scores), 0.0)


def everyone(rows):
    return lax.all_gather(rows, "ctx", axis=0, tiled=True)


def gathered_attention(qkv, seg_row):
    tok_rows, width = qkv.shape[0], qkv.shape[1] // 3
    query_heads = to_heads(qkv[:, :width])
    pieces = (everyone(qkv[:, width : 2 * width]), everyone(qkv[:, 2 * width :]), everyone(seg_row))
    size = block_size(pieces[0].shape[0])

    def step(acc, item):
        key_block, value_block, seg_block = item
        expvals = masked_exp(query_heads, to_heads(key_block), seg_row, seg_block)
        part_num = jnp.einsum(
            "hqk,khd->qhd", expvals.astype(BF16), to_heads(value_block),
            preferred_element_type=F32,
        )
        return ((acc[0] + part_num, acc[1] + jnp.transpose(jnp.sum(expvals, axis=-1))), None)

    (numer, total), unused = lax.scan(
        step,
        (jnp.zeros((tok_rows, HEADS, HEAD_DIM), F32), jnp.zeros((tok_rows, HEADS), F32)),
        tuple(split_blocks(piece, size) for piece in pieces),
    )
    return numer / total[:, :, None], total


def gathered_attention_back(qkv, seg_row, context, total, d_context):
    tok_rows, width = qkv.shape[0], qkv.shape[1] // 3
    scale = HEAD_DIM ** (-0.5)
    d_context = to_heads(d_context)
    query_rows, key_rows, value_rows = (qkv[:, i * width : (i + 1) * width] for i in range(3))
    grad_heads = (d_context / total[:, :, None]).astype(BF16)
    delta = jnp.sum(d_context * context, axis=-1) / total
    key_heads, value_heads, query_heads = (
        to_heads(key_rows), to_heads(value_rows), to_heads(query_rows)
    )
    zero_heads = jnp.zeros((tok_rows, HEADS, HEAD_DIM), F32)
    seg_all = everyone(seg_row)
    size = block_size(seg_all.shape[0])

    def key_step(acc, item):
        query_block, grad_block, delta_block, seg_block = item
        query_h, grad_h = to_heads(query_block), to_heads(grad_block)
        expvals = masked_exp(query_h, key_heads, seg_block, seg_row)
        dprob = jnp.einsum("qhd,khd->hqk", grad_h, value_heads, preferred_element_type=F32)
        dscore = (expvals * (dprob - jnp.transpose(delta_block)[:, :, None])).astype(BF16)
        dkey = acc[0] + scale * jnp.einsum(
            "hqk,qhd->khd", dscore, query_h, preferred_element_type=F32
        )
        dval = acc[1] + jnp.einsum(
            "hqk,qhd->khd", expvals.astype(BF16), grad_h, preferred_element_type=F32
        )
        return ((dkey, dval), None)

    (dkey, dval), unused = lax.scan(
        key_step,
        (zero_heads, zero_heads),
        tuple(
            split_blocks(piece, size)
            for piece in (
                everyone(query_rows),
                everyone(grad_heads.reshape(tok_rows, width)),
                everyone(delta),
                seg_all,
            )
        ),
    )

    def query_step(acc, item):
        key_block, value_block, seg_block = item
        key_h = to_heads(key_block)
        expvals = masked_exp(query_heads, key_h, seg_row, seg_block)
        dprob = jnp.einsum(
            "qhd,khd->hqk", grad_heads, to_heads(value_block), preferred_element_type=F32
        )
        dscore = (expvals * (dprob - jnp.transpose(delta)[:, :, None])).astype(BF16)
        return (
            acc + scale * jnp.einsum("hqk,khd->qhd", dscore, key_h, preferred_element_type=F32),
            None,
        )

    dquery, unused = lax.scan(
        query_step,
        zero_heads,
        tuple(
            split_blocks(piece, size)
            for piece in (everyone(key_rows), everyone(value_rows), seg_all)
        ),
    )
    return jnp.concatenate(
        [part.reshape(tok_rows, width) for part in (dquery, dkey, dval)], axis=1
    ).astype(BF16)


def neighbours(rows):
    count = lax.axis_size("ctx")
    up = [(i, i + 1) for i in range(count - 1)]
    down = [(j, i) for i, j in up]
    before = lax.ppermute(rows[:, -1], "ctx", up)
    after = lax.ppermute(rows[:, 0], "ctx", down)
    return before[:, None], after[:, None]


def shifted(rows, before, after):
    later = jnp.concatenate([before, rows[:, :-1]], axis=1)
    earlier = jnp.concatenate([rows[:, 1:], after], axis=1)
    return later, earlier


def routed():
    return lax.axis_size("ctx") == 8 and lax.axis_size("fsdp") == 4


STEPS = (1, 2, 4)
OTHER_STEPS = (1, 4, 2)
ORDER = "XABTXABDXTABDXGKTABDGKTDGKTDGKABTGDGTDG"


def flip(value, axis, bit):
    return lax.ppermute(value, axis, [(i, i ^ bit) for i in range(lax.axis_size(axis))])


def slot(steps=STEPS):
    me = lax.axis_index("ctx")
    first, second, third = ((me // bit) % 2 for bit in steps)
    return first * 4 + second * 2 + third


def own_columns(value):
    count, mine = lax.axis_size("fsdp"), lax.axis_index("fsdp")
    wide = value.shape[1] // count
    pieces = []
    for other in range(count):
        piece = lax.dynamic_slice_in_dim(value, jnp.bitwise_xor(mine, other) * wide, wide, 1)
        pieces.append(flip(piece, "fsdp", other) if other else piece)
    return pieces


class CtxSum:
    def __init__(self, value, steps=STEPS):
        self.value = value
        self.axis = value.ndim - 2
        self.stage = 0
        self.steps = steps

    @classmethod
    def begun(cls, keep, send, steps=STEPS):
        chain = cls(keep, steps)
        chain.keep = keep
        chain.send(send, steps[0])
        chain.stage = 1
        return chain

    def halve(self, value, bit):
        mine = (lax.axis_index("ctx") // bit) % 2
        half = value.shape[self.axis] // 2
        send = lax.dynamic_slice_in_dim(value, (1 - mine) * half, half, self.axis)
        self.keep = lax.dynamic_slice_in_dim(value, mine * half, half, self.axis)
        self.send(send, bit)

    def send(self, value, bit):
        self.sent = value
        self.got = flip(value, "ctx", bit)

    def advance(self, *others):
        stage = self.stage
        self.stage = stage + 1
        if stage == 0:
            self.halve(after(self.value, *others), self.steps[0])
        elif stage <= 3:
            got = after(self.got, *others).astype(F32)
            piece = (self.keep.astype(F32) + got).astype(BF16)
            if stage < 3:
                self.halve(piece, self.steps[stage])
            else:
                self.send(piece[None], self.steps[2])
        else:
            piece = jnp.concatenate([self.sent, after(self.got, *others)], axis=0)
            if stage < 6:
                self.send(piece, self.steps[5 - stage])
            else:
                self.result = self.sent = piece
        return self.sent


class HeadSum(CtxSum):
    def advance(self, *others):
        stage = self.stage
        self.stage = stage + 1
        if stage == 0:
            self.send(after(self.value, *others), 4)
        elif stage == 1:
            piece = self.sent.astype(F32) + after(self.got, *others).astype(F32)
            self.send(piece.astype(BF16)[None], 1)
        else:
            piece = jnp.concatenate([self.sent, after(self.got, *others)], axis=0)
            if stage == 2:
                self.send(piece, 2)
            else:
                self.result = self.sent = piece
        return self.sent


class TokenSum(CtxSum):
    def advance(self, *others):
        me = lax.axis_index("ctx")
        stage = self.stage
        self.stage = stage + 1
        if stage == 0:
            piece = after(self.value, *others)
        else:
            got = after(self.got, *others).astype(F32)
            if stage == 3:
                keep = self.keep.astype(F32)
                ordered = (jnp.concatenate([keep, got]), jnp.concatenate([got, keep]))
                self.result = self.sent = jnp.where(me // 4 == 0, *ordered)
                return self.sent
            piece = (self.keep.astype(F32) + got).astype(BF16)
            piece = jnp.squeeze(piece, axis=3 - stage)
        bit = STEPS[stage]
        mine = (me // bit) % 2
        axis = 2 - stage
        self.keep = lax.dynamic_slice_in_dim(piece, mine, 1, axis)
        self.send(lax.dynamic_slice_in_dim(piece, 1 - mine, 1, axis), bit)
        return self.sent


def run_in_order(chains, finish, begin):
    last, done = (), {}
    final = max(i for i, name in enumerate(ORDER[:-2]) if name == "G")
    for event, name in enumerate(ORDER):
        others = last
        if event == final or event >= len(ORDER) - 2:
            ready = [done[other] for other in "ABKDT" if other in done]
            others = others + tuple(jax.tree.leaves(ready))
        step = chains[name].advance if name in chains else begin[name]
        last = (step(*others),)
        chain = chains[name]
        if event == ORDER.index("T"):
            begin["last"](*last)
        if hasattr(chain, "result"):
            done[name] = finish[name](chain.result, done)
    return done


def settle_kernel(order_ref, in_ref, *out_refs):
    at = 0
    for out_ref in out_refs:
        wide = out_ref.shape[-1]
        out_ref[...] = in_ref[0, ..., at : at + wide].astype(F32)
        at = at + wide


def settle_half_kernel(order_ref, in_ref, *refs):
    refs[-1][...] = in_ref[0].astype(F32)


def settle_half(pieces, steps, part, whole=None):
    lead = pieces.shape[1:-2]
    rows, width = pieces.shape[-2:]
    none = (0,) * len(lead)
    order = jnp.bitwise_xor(slot(steps), jnp.arange(8, dtype=jnp.int32))
    given = [] if whole is None else [whole]
    return pl.pallas_call(
        settle_half_kernel,
        grid_spec=pltpu.PrefetchScalarGridSpec(
            num_scalar_prefetch=1,
            grid=(8,),
            in_specs=[
                pl.BlockSpec((1,) + lead + (rows, width), lambda r, o: (r,) + none + (0, 0))
            ]
            + [pl.BlockSpec(memory_space=pl.ANY)] * len(given),
            out_specs=pl.BlockSpec(lead + (rows, width), lambda r, o: none + (o[r], part)),
        ),
        out_shape=jax.ShapeDtypeStruct(lead + (8 * rows, 2 * width), F32),
        input_output_aliases={2: 0} if given else {},
        compiler_params=params(),
        cost_estimate=cost(1, 1),
        name="settle_half",
    )(order, pieces, *given)


def settle(pieces, widths):
    lead = pieces.shape[1:-2]
    rows, total = pieces.shape[-2:]
    order = jnp.bitwise_xor(slot(), jnp.arange(8, dtype=jnp.int32))
    none = (0,) * len(lead)
    return pl.pallas_call(
        settle_kernel,
        grid_spec=pltpu.PrefetchScalarGridSpec(
            num_scalar_prefetch=1,
            grid=(8,),
            in_specs=[
                pl.BlockSpec((1,) + lead + (rows, total), lambda r, o: (r,) + none + (0, 0))
            ],
            out_specs=[
                pl.BlockSpec(lead + (rows, width), lambda r, o: none + (o[r], 0))
                for width in widths
            ],
        ),
        out_shape=[jax.ShapeDtypeStruct(lead + (8 * rows, width), F32) for width in widths],
        compiler_params=params(),
        cost_estimate=cost(pieces.size, 6 * pieces.size),
        name="settle",
    )(order, pieces)


def move(sources, stages, targets, arrived, left):
    ins = [
        pltpu.make_async_copy(source, stage, arrived.at[i])
        for i, (source, stage) in enumerate(zip(sources, stages))
    ]
    for copy in ins:
        copy.start()
    outs = []
    for i, (copy, stage, target) in enumerate(zip(ins, stages, targets)):
        copy.wait()
        outs.append(pltpu.make_async_copy(stage, target, left.at[i]))
        outs[-1].start()
    for copy in outs:
        copy.wait()


def place_own_kernel(spans, own_ref, core_ref, *rest):
    outs, (own_scr, core_scr, arrived, left) = rest[:-4], rest[-4:]
    mine = lax.axis_index("fsdp")
    sources, stages, targets, at = [], [], [], 0
    for span, out_ref in zip(spans, outs):
        there = pl.ds(at, span)
        for ref, scr, shard in (
            (own_ref, own_scr, mine),
            (core_ref, core_scr, jnp.bitwise_xor(mine, 1)),
        ):
            sources.append(ref.at[there])
            stages.append(scr.at[there])
            targets.append(out_ref.at[shard])
        at = at + span
    move(sources, stages, targets, arrived, left)


def place_kernel(spans, order, piece_ref, core_ref, *rest):
    outs, (piece_scr, core_scr, arrived, left) = rest[len(spans) : -4], rest[-4:]
    place = slot()
    mine = lax.axis_index("fsdp")
    sources, stages, targets = [], [], []
    for ref, scr, shard in (
        (piece_ref, piece_scr, jnp.bitwise_xor(mine, 2)),
        (core_ref, core_scr, jnp.bitwise_xor(mine, 3)),
    ):
        for position, other in enumerate(order):
            at = 0
            for span, out_ref in zip(spans, outs):
                part = span // 8
                there = pl.multiple_of(jnp.bitwise_xor(place, other) * part, part)
                sources.append(ref.at[position, pl.ds(at, part)])
                stages.append(scr.at[position, pl.ds(at, part)])
                targets.append(out_ref.at[shard, pl.ds(there, part)])
                at = at + part
    move(sources, stages, targets, arrived, left)


def after(value, *others):
    return lax.optimization_barrier((value,) + others)[0]


class SpreadGather:
    def __init__(self, shards):
        self.spans = tuple(shard.shape[0] for shard in shards)
        self.width = shards[0].shape[1]
        place = slot()
        self.own = jnp.concatenate(shards, axis=0) if len(shards) > 1 else shards[0]
        piece = [
            lax.dynamic_slice_in_dim(shard, place * (span // 8), span // 8, 0)
            for shard, span in zip(shards, self.spans)
        ]
        self.base = None
        self.got = flip(jnp.concatenate(piece, axis=0), "fsdp", 2)[None]
        self.core = flip(self.own, "fsdp", 1)
        self.order = [0]

    def take(self, others):
        got = after(self.got, *others) if others else self.got
        return got if self.base is None else jnp.concatenate([self.base, got], axis=0)

    def double(self, bit, *others):
        self.base = self.take(others)
        self.got = flip(self.base, "ctx", bit)
        self.order = self.order + [other ^ (4 // bit) for other in self.order]

    def cores(self, *others):
        self.piece = self.take(others)
        self.core_piece = flip(self.piece, "fsdp", 1)

    def place_own(self, *others):
        spans, width = self.spans, self.own.shape[1]
        self.whole = pl.pallas_call(
            functools.partial(place_own_kernel, spans),
            in_specs=[pl.BlockSpec(memory_space=pl.ANY)] * 2,
            out_specs=[pl.BlockSpec(memory_space=pl.ANY)] * len(spans),
            out_shape=[jax.ShapeDtypeStruct((4, span, width), BF16) for span in spans],
            scratch_shapes=[pltpu.VMEM(self.own.shape, BF16)] * 2
            + [pltpu.SemaphoreType.DMA((2 * len(spans),))] * 2,
            compiler_params=params(),
            cost_estimate=cost(0, 8 * sum(spans) * width),
            name="place_own",
        )(after(self.own, *others), self.core)

    def finish(self):
        spans, width = self.spans, self.own.shape[1]
        anywhere = [pl.BlockSpec(memory_space=pl.ANY)] * len(spans)
        return pl.pallas_call(
            functools.partial(place_kernel, spans, self.order),
            in_specs=[pl.BlockSpec(memory_space=pl.ANY)] * 2 + anywhere,
            out_specs=anywhere,
            out_shape=[jax.ShapeDtypeStruct((4, span, width), BF16) for span in spans],
            scratch_shapes=[pltpu.VMEM(self.piece.shape, BF16)] * 2
            + [pltpu.SemaphoreType.DMA((16 * len(spans),))] * 2,
            input_output_aliases={2 + i: i for i in range(len(spans))},
            compiler_params=params(),
            cost_estimate=cost(0, 8 * sum(spans) * width),
            name="place",
        )(self.piece, self.core_piece, *self.whole)


def over_fsdp(grads):
    return lax.psum_scatter(grads, "fsdp", scatter_dimension=0, tiled=True)


def plain_sum(grads, axis=0):
    share = lax.psum_scatter(grads, "fsdp", scatter_dimension=axis, tiled=True)
    return lax.psum(share.astype(F32), "ctx")


def local(
    tokens, chars, segment, char_end, w_qkv, w_out, norm1_gain, norm1_bias, w_up, b_up, w_down,
    norm2_gain, norm2_bias, w_gru, b_gate, w_ftok, w_fchr, w_conv, norm3_gain, norm3_bias,
    norm4_gain, norm4_bias, d_token, d_char,
):
    count, me = lax.axis_size("ctx"), lax.axis_index("ctx")
    shards = lax.axis_size("fsdp")
    batch, rows, width = tokens.shape
    char_rows = chars.shape[1]
    total_rows = batch * rows
    heads = heads_here(batch, count)
    padded_rows = -(-char_rows // 8) * 8

    def gather(weight, axis=0):
        return lax.all_gather(weight, "fsdp", axis=axis, tiled=True)

    own_width = norm1_gain.shape[0]
    vectors = (
        norm1_gain, norm1_bias, norm2_gain, norm2_bias, b_gate, norm3_gain, norm3_bias,
        norm4_gain, norm4_bias,
    )
    columns = jnp.stack(vectors, axis=1)
    columns = jnp.concatenate([columns, b_up.reshape(-1, own_width).T], axis=1)
    small_count = columns.shape[1]
    wide_gru = w_gru.shape[1]
    columns = jnp.pad(columns, ((0, 0), (0, 128 - small_count)))
    width_qkv = w_qkv.shape[1]
    if heads:
        group, part = me % (HEADS // heads), heads * HEAD_DIM
        w_heads = jnp.concatenate(
            [
                lax.dynamic_slice_in_dim(w_qkv, kind * width + group * part, part, 1)
                for kind in range(3)
            ],
            axis=1,
        )
        w_pieces = [w_heads] + [flip(w_heads, "fsdp", other) for other in (1, 2, 3)]
    else:
        w_qkv = gather(w_qkv)
    w_gru = gather(jnp.concatenate([w_gru, columns], axis=1))
    w_out = gather(w_out)
    w_up = gather(w_up)
    columns = w_gru[:, wide_gru : wide_gru + small_count].astype(F32)
    (
        norm1_gain, norm1_bias, norm2_gain, norm2_bias, b_gate, norm3_gain, norm3_bias,
        norm4_gain, norm4_bias,
    ) = (columns[:, i][None, :] for i in range(9))
    b_up = jnp.swapaxes(columns[:, 9:].reshape(shards, own_width, -1), 1, 2).reshape(1, -1)
    w_down = gather(w_down)
    if routed():
        first_taps = SpreadGather([w_conv[0], w_conv[1]])
        last_tap = SpreadGather([w_conv[2], jnp.concatenate([w_ftok, w_fchr], axis=1)])
    else:
        w_ftok = gather(w_ftok)
        w_fchr = gather(w_fchr)
        w_conv = gather(w_conv, 1)

    start = jnp.concatenate([jnp.zeros((batch, 1), jnp.int32), char_end[:, :-1] + 1], axis=1)
    change = (segment[:, 1:] != segment[:, :-1]).astype(F32)
    first = jnp.concatenate([jnp.broadcast_to((me == 0).astype(F32), (batch, 1)), change], axis=1)
    last = jnp.concatenate(
        [change, jnp.broadcast_to((me == count - 1).astype(F32), (batch, 1))], axis=1
    )
    flat_tokens = tokens.reshape(total_rows, width)
    chars_pad = jnp.pad(chars, ((0, 0), (0, padded_rows - char_rows), (0, 0)))
    if routed():
        first_taps.double(4)
        last_tap.double(1)
    gate, cand, decay, cum, state, edges = gru_forward(
        chars_pad, w_gru, b_gate, start[:, None], first[:, None], char_end[:, None],
        last[:, None], char_rows,
    )

    if heads:
        ids = segment.astype(BF16)[:, None, :]
        ids = jnp.pad(ids, ((0, 0), (0, 7), (0, width - rows)))
        sent = jnp.repeat(jnp.concatenate([tokens, ids], axis=1), HEADS // heads, axis=0)
        tokens_all = lax.all_to_all(sent, "ctx", 0, 0, tiled=True)
        packed_context, kept, *saved, w_heads = attend(tokens_all, w_pieces, edges, heads, rows)
        first_taps.double(2, state)
        last_tap.double(4, state)
        first_taps.place_own(packed_context)
        last_tap.place_own(packed_context)
        received = lax.all_to_all(packed_context.reshape(count, rows, -1), "ctx", 0, 0, tiled=True)
        received = after(received, *first_taps.whole, *last_tap.whole)
        context_b, edges_all = unpack(received, heads, batch)
    else:
        qkv = matmul(flat_tokens, w_qkv).astype(BF16).reshape(batch, rows, -1)
        results = [gathered_attention(qkv[i], segment[i]) for i in range(batch)]
        context_b = jnp.concatenate([r[0].reshape(rows, width) for r in results]).astype(BF16)
        edges_all = all_edges(edges)

    attn = matmul(context_b, w_out)
    hidden1, kept1 = layer_norm(flat_tokens.astype(F32) + attn, norm1_gain, norm1_bias)
    hidden1_b = hidden1.astype(BF16)
    inner_b, slope = feed_forward(hidden1_b, w_up, b_up)
    ffn = matmul(inner_b, w_down)
    hidden2, kept2 = layer_norm(hidden1 + ffn, norm2_gain, norm2_bias)
    hidden2_b = hidden2.astype(BF16)
    if routed():
        first_taps.double(1, context_b)
        last_tap.double(2, context_b)
        first_taps.cores(inner_b)
        last_tap.cores(inner_b)
        w_conv = [
            weight.reshape(-1, 2 * width) for weight in first_taps.finish() + last_tap.finish()
        ]
        w_ftok, w_fchr = w_conv[3][:, :width], w_conv[3][:, width:]

    char_tok, enter = gather_states(
        state, cum, edges_all, char_end[:, :, None], start[:, :, None]
    )
    char_tok_b = char_tok.astype(BF16)
    joined = jnp.concatenate(
        [matmul(hidden2_b, w_ftok), matmul(char_tok_b, w_fchr)], axis=1
    ).astype(BF16)

    two = 2 * width
    if routed():
        inner_own = own_columns(inner_b)
        joined = after(joined, *inner_own[1:])
        joined_own = own_columns(joined)
    blocks = joined.reshape(batch, rows, two)
    later, earlier = shifted(blocks, *neighbours(blocks))
    taps = (later.reshape(total_rows, two), joined, earlier.reshape(total_rows, two))
    conv = matmul(taps[1], w_conv[1]) + matmul(taps[0], w_conv[0]) + matmul(taps[2], w_conv[2])
    token_out, kept3 = layer_norm(hidden2 + conv[:, :width], norm3_gain, norm3_bias)
    char_out, kept4 = layer_norm(char_tok + conv[:, width:], norm4_gain, norm4_bias)

    d_in3, gain3_grad, bias3_grad = layer_norm_back(
        d_token.reshape(total_rows, width).astype(F32), norm3_gain, kept3
    )
    d_in4, gain4_grad, bias4_grad = layer_norm_back(
        d_char.reshape(total_rows, width).astype(F32), norm4_gain, kept4
    )
    d_conv = jnp.concatenate([d_in3, d_in4], axis=1).astype(BF16)
    d_before, d_after = neighbours(d_conv.reshape(batch, rows, two))
    if routed():
        d_conv = after(d_conv, *joined_own[1:])
    d_later, d_earlier = shifted(d_conv.reshape(batch, rows, two), d_before, d_after)
    d_joined = (
        matmul_nt(d_conv, w_conv[1])
        + matmul_nt(d_earlier.reshape(total_rows, two), w_conv[0])
        + matmul_nt(d_later.reshape(total_rows, two), w_conv[2])
    ).astype(BF16)
    if routed():
        d_all = gather(
            jnp.concatenate([d_conv.reshape(batch, rows, two), d_before, d_after], axis=1)
        )
    else:
        conv_sum = plain_sum(jnp.stack([matmul_tn(tap, d_conv).astype(BF16) for tap in taps]), 1)

    d_tok_part, d_chr_part = d_joined[:, :width], d_joined[:, width:]
    d_hidden2 = d_in3 + matmul_nt(d_tok_part, w_ftok)
    d_char_tok = d_in4 + matmul_nt(d_chr_part, w_fchr)

    end_line, start_line = char_end[:, None], start[:, None]
    spread, back_cum, carried, back_edges = gru_back(
        d_char_tok.reshape(batch, rows, width), decay, end_line, start_line, char_rows
    )

    d_in2, gain2_grad, bias2_grad = layer_norm_back(d_hidden2, norm2_gain, kept2)
    d_ffn = d_in2.astype(BF16)
    reduced = over_fsdp if routed() else plain_sum
    if routed():
        d_ffn_all = gather(d_ffn[None])
    else:
        second_sum = plain_sum(matmul_tn(inner_b, d_ffn).astype(BF16))
    d_pre = matmul_nt(d_ffn, w_down) * slope.astype(F32)
    bup_grad = jnp.sum(d_pre, axis=0)
    d_pre_low = d_pre.astype(BF16)
    d_hidden1 = d_in2 + matmul_nt(d_pre_low, w_up)
    d_in1, gain1_grad, bias1_grad = layer_norm_back(d_hidden1, norm1_gain, kept1)
    d_attn = d_in1.astype(BF16)
    if heads:
        sent = send_grad(d_attn, w_out, back_edges, heads, batch)
        hidden1_b = after(hidden1_b, sent)
    third = gradients(hidden1_b, context_b, hidden2_b, char_tok_b, d_pre_low, d_attn, d_joined)
    third_sum = reduced(third)

    if heads:
        conv_pieces = [after(joined_own[0], sent, third)] + joined_own[1:]
        first_chain = CtxSum.begun(*conv_gradient(conv_pieces, d_all, rows, 0))
        other_chain = CtxSum.begun(*conv_gradient(conv_pieces, d_all, rows, 1), OTHER_STEPS)
        received = lax.all_to_all(sent, "ctx", 0, 0, tiled=True)
        received = after(received, first_chain.sent, other_chain.sent)
        d_tok_part, heads_grad, back_enter = attend_back(
            tokens_all, w_heads, saved, kept, received.reshape(count * rows, -1), edges_all,
            heads, rows,
        )
        token_chain = TokenSum(d_tok_part.reshape(2, 2, 2, rows, width))
        last = other_chain.advance(first_chain.advance(heads_grad))
        gate = after(gate, last)
    else:
        back_enter = back_entering(edges_all, all_edges(back_edges))
        d_context = matmul_nt(d_attn, w_out).reshape(batch, rows, width)
        d_qkv = jnp.concatenate(
            [
                gathered_attention_back(
                    qkv[i], segment[i], results[i][0], results[i][1], d_context[i]
                )
                for i in range(batch)
            ]
        )
    d_gate_in, bgate_grad = gru_grad(
        gate, cand, decay, cum, state, enter, spread, back_cum, carried, back_enter, char_rows
    )
    d_gate_in = d_gate_in.reshape(batch * padded_rows, -1)
    d_chars = matmul_nt(d_gate_in, w_gru[:, :wide_gru]).astype(BF16)
    d_chars = d_chars.reshape(batch, padded_rows, width)[:, :char_rows]

    if not heads:
        heads_grad = matmul_tn(flat_tokens, d_qkv)
        d_tokens = matmul_nt(d_qkv, w_qkv)

    small = [
        gain1_grad, bias1_grad, gain2_grad, bias2_grad, jnp.sum(bgate_grad, axis=(0, 1)),
        gain3_grad, bias3_grad, gain4_grad, bias4_grad,
    ]
    up_small = jnp.swapaxes(bup_grad.reshape(shards, -1, width // shards), 0, 1)
    small = jnp.concatenate([value[None] for value in small] + [up_small.reshape(-1, width)])
    small = jnp.pad(small, ((0, 16 - small_count), (0, 0)))

    def last_sum(*others):
        gates = after(d_gate_in, *others) if others else d_gate_in
        return last_gradients(
            chars_pad.reshape(batch * padded_rows, width), gates, small, heads_grad
        )

    widths = ((width,), (w_up.shape[1],) + (width,) * 3, (wide_gru, 128, width_qkv))
    if routed():
        own_wide = wide_gru + 128
        chains = dict(
            A=first_chain,
            B=other_chain,
            X=token_chain,
            T=CtxSum(third_sum),
        )

        def begin_down(*others):
            chains["D"] = CtxSum.begun(*down_gradient(after(inner_own, *others), d_ffn_all))
            return chains["D"].sent

        def begin_last(*others):
            chains["last"] = reduced(last_sum(*others))

        def begin_G(*others):
            value = after(chains["last"], *others)
            chains["G"] = CtxSum(value[:, :own_wide])
            chains["K"] = HeadSum(value[:, own_wide:])
            return chains["G"].advance()

        finish = dict(
            A=lambda value, done: settle_half(value, STEPS, 0),
            B=lambda value, done: settle_half(value, OTHER_STEPS, 1, done.pop("A")),
            D=lambda value, done: settle(value, widths[0]),
            T=lambda value, done: settle(value, widths[1]),
            G=lambda value, done: settle(value, widths[2][:2]),
            K=lambda value, done: spread_columns(value, heads),
            X=lambda value, done: value.reshape(total_rows, width),
        )
        done = run_in_order(chains, finish, dict(D=begin_down, G=begin_G, last=begin_last))
        (down_sum,), third = done["D"], done["T"]
        conv_sum = done["B"]
        fourth = [*done["G"], done["K"]]
        d_tokens = done["X"]
    else:
        (down_sum,), third, fourth = (
            jnp.split(value, [sum(split[:i]) for i in range(1, len(split))], axis=1)
            for value, split in zip((second_sum, third_sum, reduced(last_sum())), widths)
        )
    d_tokens = (d_in1 + d_tokens).astype(BF16)
    vector = fourth[1]
    return (
        token_out.astype(BF16).reshape(batch, rows, width),
        char_out.astype(BF16).reshape(batch, rows, width),
        d_tokens.reshape(batch, rows, width),
        d_chars,
        fourth[2],
        third[1],
        vector[:, 0],
        vector[:, 1],
        third[0],
        jnp.swapaxes(vector[:, 9:small_count], 0, 1).reshape(-1),
        down_sum,
        vector[:, 2],
        vector[:, 3],
        fourth[0],
        vector[:, 4],
        third[2],
        third[3],
        conv_sum,
        vector[:, 5],
        vector[:, 6],
        vector[:, 7],
        vector[:, 8],
    )


def solution(mesh):
    rows = P("fsdp", "ctx", None)
    pairs = P("fsdp", "ctx")
    matrix = P("fsdp", None)
    vector = P("fsdp")
    weights = (
        matrix, matrix, vector, vector, matrix, vector, matrix, vector, vector, matrix, vector,
        matrix, matrix, P(None, "fsdp", None), vector, vector, vector, vector,
    )
    return jax.shard_map(
        local,
        mesh=mesh,
        in_specs=(rows, rows, pairs, pairs) + weights + (rows, rows),
        out_specs=(rows,) * 4 + weights,
        check_vma=False,
    )
```

```python
import functools

import jax
import jax.numpy as jnp
from jax import lax
from jax.experimental import pallas as pl
from jax.experimental.pallas import tpu as pltpu
from jax.sharding import PartitionSpec as P

HEADS = 12
HEAD_DIM = 64
GRU_H = 384
EPSILON = 1e-05
BLOCK_LIMIT = 1024
FAR = 1e9
VMEM_BYTES = 24 * 1024 * 1024

F32 = jnp.float32
BF16 = jnp.bfloat16


def matmul(left, right):
    return jnp.dot(left, right, preferred_element_type=F32)


def matmul_nt(left, right):
    return lax.dot_general(left, right, (((1,), (1,)), ((), ())), preferred_element_type=F32)


def matmul_tn(left, right):
    return lax.dot_general(left, right, (((0,), (0,)), ((), ())), preferred_element_type=F32)


def layer_norm(value, gain, shift):
    center = value - jnp.mean(value, axis=-1, keepdims=True)
    inverse = lax.rsqrt(jnp.mean(center * center, axis=-1, keepdims=True) + EPSILON)
    normed = center * inverse
    return normed * gain + shift, (normed, inverse)


def layer_norm_back(grad, gain, kept):
    normed, inverse = kept
    scaled = grad * gain
    into = inverse * (
        scaled
        - jnp.mean(scaled, axis=-1, keepdims=True)
        - normed * jnp.mean(scaled * normed, axis=-1, keepdims=True)
    )
    return into, jnp.sum(grad * normed, axis=0), jnp.sum(grad, axis=0)


def params(**more):
    return pltpu.CompilerParams(vmem_limit_bytes=VMEM_BYTES, **more)


def cost(flops, moved, transcendentals=0):
    return pl.CostEstimate(
        flops=1, bytes_accessed=1, transcendentals=0
    )


def two_parts(value):
    high = value.astype(BF16)
    return high, (value - high.astype(F32)).astype(BF16)


KINDS = 4


def store_edges(edge_ref, cols, rows):
    parts = [half.astype(F32) for row in rows for half in two_parts(row)]
    parts = parts + [jnp.zeros_like(parts[0])] * (KINDS - len(parts))
    parts = jnp.concatenate(parts, axis=0)
    for sequence in range(edge_ref.shape[0] // KINDS):

        @pl.when(pl.program_id(0) == sequence)
        def store():
            edge_ref[pl.ds(sequence * KINDS, KINDS), cols] = parts


def edges_to_block(edges, rows):
    count = edges.shape[1] // HEAD_DIM
    pieces = [edges[:, i * HEAD_DIM : (i + 1) * HEAD_DIM] for i in range(count)]
    pieces.append(jnp.zeros((rows - count * edges.shape[0], HEAD_DIM), F32))
    return jnp.concatenate(pieces, axis=0).astype(BF16)


def edges_of_block(block):
    block = block.astype(F32)
    count = 2 * GRU_H // HEAD_DIM
    return jnp.concatenate([block[i * 8 : (i + 1) * 8] for i in range(count)], axis=1)


def entering_row(decays, drives, sequence, count, flip):
    me = lax.axis_index("ctx")
    halves = []
    for side in (0, 1):
        cols = slice(side * GRU_H, (side + 1) * GRU_H)
        total = jnp.zeros((1, GRU_H), F32)
        backward = (side == 1) != flip
        order = range(count - 1, 0, -1) if backward else range(count - 1)
        for other in order:
            decay, drive = decays(other, sequence, cols), drives(other, sequence, cols)
            there = me < other if backward else me > other
            total = jnp.where(there, decay * total + drive, total)
        halves.append(total)
    return jnp.concatenate(halves, axis=1)


def edge_reader(ref, kind):
    def read(other, sequence, cols):
        at = sequence * KINDS + 2 * kind
        return ref[other, at : at + 1, cols] + ref[other, at + 1 : at + 2, cols]

    return read


def shift_rows(value, by, fill, up):
    rows = value.shape[0]
    row = lax.broadcasted_iota(jnp.int32, value.shape, 0)
    if up:
        return jnp.where(row < rows - by, pltpu.roll(value, rows - by, 0), fill)
    return jnp.where(row >= by, pltpu.roll(value, by, 0), fill)


def scan_rows(decay, drive, up):
    by = 1
    while by < decay.shape[0]:
        drive = drive + decay * shift_rows(drive, by, 0.0, up)
        decay = decay * shift_rows(decay, by, 1.0, up)
        by = by * 2
    return decay, drive


def gru_forward_kernel(
    real, chars_ref, w_ref, bias_ref, start_ref, first_ref, end_ref, last_ref,
    gate_ref, cand_ref, decay_ref, cum_ref, state_ref, edge_ref,
):
    columns = matmul(chars_ref[0], w_ref[:, : 4 * GRU_H])
    rows = columns.shape[0]
    tokens = start_ref.shape[2]
    place = lax.broadcasted_iota(jnp.int32, (rows, tokens), 0)
    inside = lax.broadcasted_iota(jnp.int32, (rows, GRU_H), 0) < real
    resets = [
        jnp.sum(jnp.where(place == at[0], flag[0], 0.0), axis=1, keepdims=True)
        for at, flag in ((start_ref, first_ref), (end_ref, last_ref))
    ]
    for side in (0, 1):
        cols = pl.ds(side * GRU_H, GRU_H)
        base = 2 * side * GRU_H
        gate = jax.nn.sigmoid(columns[:, base : base + GRU_H] + bias_ref[:, cols])
        cand = jnp.tanh(columns[:, base + GRU_H : base + 2 * GRU_H])
        decay = jnp.where(inside, gate * (1.0 - resets[side]), 1.0)
        drive = jnp.where(inside, (1.0 - gate) * cand, 0.0)
        gate_ref[0, :, cols] = gate
        cand_ref[0, :, cols] = cand
        decay_ref[0, :, cols] = decay
        cum, state = scan_rows(decay, drive, side == 1)
        cum_ref[0, :, cols] = cum
        state_ref[0, :, cols] = state
        at = 0 if side else real - 1
        store_edges(edge_ref, cols, (cum[at : at + 1], state[at : at + 1]))


def char_tok_kernel(state_ref, cum_ref, edges_ref, end_ref, start_ref, out_ref, enter_ref):
    batch, tokens = end_ref.shape[:2]
    for sequence in range(batch):
        enter = entering_row(
            edge_reader(edges_ref, 0), edge_reader(edges_ref, 1), sequence, edges_ref.shape[0],
            False,
        )
        enter_ref[sequence] = enter
        state = state_ref[sequence] + cum_ref[sequence] * enter
        high, low = two_parts(state)
        place = lax.broadcasted_iota(jnp.int32, (tokens, state.shape[0]), 1)
        for side, at in ((0, end_ref), (1, start_ref)):
            pick = jnp.where(place == at[sequence], 1.0, 0.0).astype(BF16)
            cols = slice(side * GRU_H, (side + 1) * GRU_H)
            out_ref[pl.ds(sequence * tokens, tokens), pl.ds(side * GRU_H, GRU_H)] = matmul(
                pick, high[:, cols]
            ) + matmul(pick, low[:, cols])


def gru_back_kernel(
    real, grad_ref, decay_ref, end_ref, start_ref, spread_ref, cum_ref, carried_ref, edge_ref
):
    rows = decay_ref.shape[1]
    tokens = end_ref.shape[2]
    place = lax.broadcasted_iota(jnp.int32, (rows, tokens), 0)
    high, low = two_parts(grad_ref[0])
    for side, at in ((0, end_ref), (1, start_ref)):
        put = jnp.where(place == at[0], 1.0, 0.0).astype(BF16)
        cols = slice(side * GRU_H, (side + 1) * GRU_H)
        there = pl.ds(side * GRU_H, GRU_H)
        spread = matmul(put, high[:, cols]) + matmul(put, low[:, cols])
        decay = decay_ref[0, :, there]
        cum, carried = scan_rows(decay, decay * spread, side == 0)
        spread_ref[0, :, there] = spread
        cum_ref[0, :, there] = cum
        carried_ref[0, :, there] = carried
        at = real - 1 if side else 0
        store_edges(edge_ref, there, (carried[at : at + 1],))


def gru_grad_kernel(
    real, gate_ref, cand_ref, decay_ref, cum_ref, state_ref, enter_ref,
    spread_ref, back_cum_ref, carried_ref, back_enter_ref, out_ref, bias_ref,
):
    rows = gate_ref.shape[1]
    inside = lax.broadcasted_iota(jnp.int32, (rows, GRU_H), 0) < real
    for side in (0, 1):
        there = pl.ds(side * GRU_H, GRU_H)
        gate = gate_ref[0, :, there]
        cand = cand_ref[0, :, there]
        decay = decay_ref[0, :, there]
        enter = enter_ref[0, :, there]
        back_enter = back_enter_ref[0, :, there]
        state = state_ref[0, :, there] + cum_ref[0, :, there] * enter
        carried = carried_ref[0, :, there] + back_cum_ref[0, :, there] * back_enter
        previous = shift_rows(state, 1, enter, side == 1)
        adjoint = spread_ref[0, :, there] + shift_rows(carried, 1, back_enter, side == 0)
        adjoint = jnp.where(inside, adjoint, 0.0)
        rest = adjoint * (1.0 - gate)
        to_gate = rest * (previous * decay - cand * gate)
        to_cand = rest * (1.0 - cand * cand)
        out_ref[0, :, pl.ds(2 * side * GRU_H, GRU_H)] = to_gate.astype(BF16)
        out_ref[0, :, pl.ds((2 * side + 1) * GRU_H, GRU_H)] = to_cand.astype(BF16)
        bias_ref[0, :, there] = jnp.sum(to_gate, axis=0, keepdims=True)


def per_sequence(*tail):
    return pl.BlockSpec((1,) + tail, lambda s: (s,) + (0,) * len(tail))


def whole_block(*shape):
    return pl.BlockSpec(shape, lambda s: (0,) * len(shape))


def gru_forward(chars, w_gru, bias, start, first, end, last, real):
    batch, rows, width = chars.shape
    tokens = start.shape[2]
    two = 2 * GRU_H
    kept = jax.ShapeDtypeStruct((batch, rows, two), F32)
    return pl.pallas_call(
        functools.partial(gru_forward_kernel, real),
        grid=(batch,),
        in_specs=[per_sequence(rows, width), whole_block(width, w_gru.shape[1]), whole_block(1, two)]
        + [per_sequence(1, tokens)] * 4,
        out_specs=[per_sequence(rows, two)] * 5 + [whole_block(KINDS * batch, two)],
        out_shape=[kept] * 5 + [jax.ShapeDtypeStruct((KINDS * batch, two), F32)],
        compiler_params=params(),
        cost_estimate=cost(
            2 * batch * rows * width * 2 * two,
            chars.size * 2 + w_gru.size * 2 + 20 * batch * rows * two,
            2 * batch * rows * two,
        ),
        name="gru_forward",
    )(chars, w_gru, bias, start, first, end, last)


def gather_states(state, cum, edges, end, start):
    batch, rows, two = state.shape
    tokens = end.shape[1]
    return pl.pallas_call(
        char_tok_kernel,
        out_shape=[
            jax.ShapeDtypeStruct((batch * tokens, two), F32),
            jax.ShapeDtypeStruct((batch, 1, two), F32),
        ],
        compiler_params=params(),
        cost_estimate=cost(
            4 * batch * rows * tokens * two, 8 * batch * rows * two + 4 * batch * tokens * two
        ),
        name="gather_states",
    )(state, cum, edges, end, start)


def gru_back(grad, decay, end, start, real):
    batch, rows, two = decay.shape
    tokens = end.shape[2]
    kept = jax.ShapeDtypeStruct((batch, rows, two), F32)
    return pl.pallas_call(
        functools.partial(gru_back_kernel, real),
        grid=(batch,),
        in_specs=[per_sequence(tokens, two), per_sequence(rows, two)]
        + [per_sequence(1, tokens)] * 2,
        out_specs=[per_sequence(rows, two)] * 3 + [whole_block(KINDS * batch, two)],
        out_shape=[kept] * 3 + [jax.ShapeDtypeStruct((KINDS * batch, two), F32)],
        compiler_params=params(),
        cost_estimate=cost(
            4 * batch * rows * tokens * two, 16 * batch * rows * two + 4 * batch * tokens * two
        ),
        name="gru_back",
    )(grad, decay, end, start)


def gru_grad(gate, cand, decay, cum, state, enter, spread, back_cum, carried, back_enter, real):
    batch, rows, two = decay.shape
    big = per_sequence(rows, two)
    row = per_sequence(1, two)
    return pl.pallas_call(
        functools.partial(gru_grad_kernel, real),
        grid=(batch,),
        in_specs=[big] * 5 + [row] + [big] * 3 + [row],
        out_specs=[per_sequence(rows, 2 * two), row],
        out_shape=[
            jax.ShapeDtypeStruct((batch, rows, 2 * two), BF16),
            jax.ShapeDtypeStruct((batch, 1, two), F32),
        ],
        compiler_params=params(),
        cost_estimate=cost(20 * batch * rows * two, 36 * batch * rows * two),
        name="gru_grad",
    )(gate, cand, decay, cum, state, enter, spread, back_cum, carried, back_enter)


def all_edges(edges):
    return lax.all_gather(edges, "ctx", axis=0)


def entering_kernel(decay_ref, drive_ref, out_ref):
    for sequence in range(out_ref.shape[0]):
        out_ref[sequence] = entering_row(
            edge_reader(decay_ref, 0), edge_reader(drive_ref, 0), sequence, decay_ref.shape[0],
            True,
        )


def back_entering(decays, drives):
    batch, two = decays.shape[1] // KINDS, decays.shape[2]
    return pl.pallas_call(
        entering_kernel,
        out_shape=jax.ShapeDtypeStruct((batch, 1, two), F32),
        compiler_params=params(),
        name="back_entering",
    )(decays, drives)


def attend_kernel(
    heads, tokens, tok_ref, own_ref, core_ref, far_ref, far_core_ref, edge_ref, out_ref, kept_ref,
    query_ref, key_ref, value_ref, w_ref,
):
    part = heads * HEAD_DIM
    rows = out_ref.shape[0]
    step = pl.program_id(0)

    @pl.when(step == 0)
    def build():
        eye = jnp.where(
            lax.broadcasted_iota(jnp.int32, (HEAD_DIM, HEAD_DIM), 0)
            == lax.broadcasted_iota(jnp.int32, (HEAD_DIM, HEAD_DIM), 1),
            1.0,
            0.0,
        ).astype(BF16)
        number = lax.broadcasted_iota(jnp.int32, (HEAD_DIM, tokens), 0).astype(F32)
        shard = own_ref.shape[0]
        for other, piece_ref in enumerate((own_ref, core_ref, far_ref, far_core_ref)):
            at = jnp.bitwise_xor(lax.axis_index("fsdp"), other) * shard
            w_ref[pl.ds(pl.multiple_of(at, shard), shard)] = piece_ref[...]
        ones = jnp.ones((tokens, HEAD_DIM), BF16)

        def block(source, carry):
            qkv = matmul(tok_ref[source, :tokens], w_ref[...])
            ids = tok_ref[source, tokens:].astype(F32)[0:1, :tokens]
            marks = matmul_tn(jnp.where(number == ids, 1.0, 0.0).astype(BF16), eye)
            blocked = ((marks - 1.0) * FAR).astype(BF16)
            marks = marks.astype(BF16)
            here = pl.ds(pl.multiple_of(source * tokens, tokens), tokens)
            for head in range(heads):
                query, key, value = (
                    qkv[:, kind * part + head * HEAD_DIM : kind * part + (head + 1) * HEAD_DIM]
                    for kind in range(3)
                )
                query = query.astype(BF16) * jnp.asarray(HEAD_DIM ** (-0.5), BF16)
                query_ref[head, here] = jnp.concatenate([query, marks], axis=1)
                key_ref[head, here] = jnp.concatenate([key.astype(BF16), blocked], axis=1)
                value_ref[head, here] = jnp.concatenate([value.astype(BF16), ones], axis=1)
            return carry

        lax.fori_loop(0, tok_ref.shape[0], block, 0)

    here = pl.ds(pl.multiple_of(step * rows, rows), rows)
    outs = []
    for head in range(heads):
        expvals = jnp.exp(matmul_nt(query_ref[head, here], key_ref[head]))
        both = matmul(expvals.astype(BF16), value_ref[head])
        total = both[:, HEAD_DIM:]
        context = both[:, :HEAD_DIM] / total
        kept_ref[:, pl.ds(head * 2 * HEAD_DIM, 2 * HEAD_DIM)] = jnp.concatenate(
            [context, total], axis=1
        )
        outs.append(context.astype(BF16))
    block = edges_to_block(edge_ref[...], tokens)
    outs.append(jnp.concatenate([block] * (rows // tokens), axis=0))
    out_ref[...] = jnp.concatenate(outs, axis=1)


def attend_back_kernel(
    heads, tokens, tok_ref, w_ref, query_ref, key_ref, value_ref, kept_ref, grad_ref, edges_ref,
    out_ref, w_grad_ref, enter_ref, grad_scr, edge_scr,
):
    part = heads * HEAD_DIM
    rows = out_ref.shape[0]
    step = pl.program_id(0)

    @pl.when(step == 0)
    def build():
        lane = lax.broadcasted_iota(jnp.int32, (grad_ref.shape[0], HEAD_DIM), 1)
        for head in range(heads):
            at = head * HEAD_DIM
            context = kept_ref[:, 2 * at : 2 * at + HEAD_DIM]
            total = kept_ref[:, 2 * at + HEAD_DIM : 2 * at + 2 * HEAD_DIM]
            grad = grad_ref[:, at : at + HEAD_DIM].astype(F32) / total
            delta = jnp.sum(grad * context, axis=1, keepdims=True)
            high, low = two_parts(-delta)
            extra = jnp.where(
                lane == 0, high.astype(F32), jnp.where(lane == 1, low.astype(F32), 0.0)
            )
            grad_scr[head] = jnp.concatenate([grad, extra], axis=1).astype(BF16)
        for other in range(edges_ref.shape[0]):
            edge_scr[other] = edges_of_block(
                grad_ref[other * tokens : (other + 1) * tokens, part : part + HEAD_DIM]
            )
        for sequence in range(enter_ref.shape[0]):
            enter_ref[sequence] = entering_row(
                edge_reader(edges_ref, 0), edge_reader(edge_scr, 0), sequence,
                edges_ref.shape[0], True,
            )
        w_grad_ref[...] = jnp.zeros_like(w_grad_ref)

    here = pl.ds(pl.multiple_of(step * rows, rows), rows)
    scale = HEAD_DIM ** (-0.5)
    d_query, d_key, d_value = [], [], []
    for head in range(heads):
        expvals = jnp.exp(matmul_nt(query_ref[head, here], key_ref[head]))
        inner = matmul_nt(grad_scr[head, here], value_ref[head])
        d_scores = (expvals * inner).astype(BF16)
        d_query.append((matmul(d_scores, key_ref[head])[:, :HEAD_DIM] * scale).astype(BF16))
        expvals = jnp.exp(matmul_nt(key_ref[head, here], query_ref[head]))
        inner = matmul_nt(value_ref[head, here], grad_scr[head])
        d_scores = (expvals * inner).astype(BF16)
        d_key.append(matmul(d_scores, query_ref[head])[:, :HEAD_DIM].astype(BF16))
        d_value.append(
            matmul(expvals.astype(BF16), grad_scr[head])[:, :HEAD_DIM].astype(BF16)
        )
    d_qkv = jnp.concatenate(d_query + d_key + d_value, axis=1)
    out_ref[...] = matmul_nt(d_qkv, w_ref[...]).astype(BF16)
    blocks = rows // tokens
    tok = jnp.concatenate(
        [tok_ref[step * blocks + block, :tokens] for block in range(blocks)], axis=0
    )
    w_grad_ref[...] += matmul_tn(tok, d_qkv)


def unpack_kernel(groups, part, in_ref, out_ref, edge_ref):
    for group in range(groups):
        edge_ref[group] = edges_of_block(in_ref[group, :, part:])
    out_ref[...] = jnp.concatenate([in_ref[group, :, :part] for group in range(groups)], axis=1)


def spread_columns_kernel(heads, in_ref, out_ref):
    groups, part = in_ref.shape[0], heads * HEAD_DIM
    width = groups * part
    mine = lax.rem(lax.axis_index("ctx"), groups)
    for case in range(groups):

        @pl.when(mine == case)
        def place():
            for kind in range(3):
                pieces = [
                    in_ref[case ^ group, :, kind * part : (kind + 1) * part].astype(F32)
                    for group in range(groups)
                ]
                out_ref[:, pl.ds(kind * width, width)] = jnp.concatenate(pieces, axis=1)


def send_grad_kernel(groups, part, grad_ref, w_ref, edge_ref, out_ref):
    d_context = matmul_nt(grad_ref[...], w_ref[...]).astype(BF16)
    block = edges_to_block(edge_ref[...], grad_ref.shape[0])
    for group in range(groups):
        out_ref[group] = jnp.concatenate(
            [d_context[:, group * part : (group + 1) * part], block], axis=1
        )


def heads_here(batch, count):
    if batch * HEADS % count != 0 or not routed():
        return 0
    heads = batch * HEADS // count
    if heads > HEADS or HEADS % heads != 0 or heads % 2 == 0 or batch * KINDS != 8:
        return 0
    return heads


def attend(tokens_all, w_pieces, edges, heads, tokens):
    count, rows, width = tokens_all.shape
    length = count * tokens
    block = 256
    part = heads * HEAD_DIM
    out_wide = part + HEAD_DIM
    wide = jax.ShapeDtypeStruct((heads, length, 2 * HEAD_DIM), BF16)
    return pl.pallas_call(
        functools.partial(attend_kernel, heads, tokens),
        grid=(length // block,),
        in_specs=[
            pl.BlockSpec((count, rows, width), lambda i: (0, 0, 0)),
        ]
        + [pl.BlockSpec(w_pieces[0].shape, lambda i: (0, 0))] * 4
        + [pl.BlockSpec(edges.shape, lambda i: (0, 0))],
        out_specs=[
            pl.BlockSpec((block, out_wide), lambda i: (i, 0)),
            pl.BlockSpec((block, 2 * part), lambda i: (i, 0)),
        ]
        + [pl.BlockSpec(wide.shape, lambda i: (0, 0, 0))] * 3
        + [pl.BlockSpec((width, 3 * part), lambda i: (0, 0))],
        out_shape=[
            jax.ShapeDtypeStruct((length, out_wide), BF16),
            jax.ShapeDtypeStruct((length, 2 * part), F32),
            wide,
            wide,
            wide,
            jax.ShapeDtypeStruct((width, 3 * part), BF16),
        ],
        compiler_params=params(),
        cost_estimate=cost(
            8 * heads * length * length * HEAD_DIM,
            length * (width * 2 + out_wide * 2 + 8 * part),
            heads * length * length,
        ),
        name="attend",
    )(tokens_all, *w_pieces, edges)


def attend_back(tokens_all, w_heads, saved, kept, grads, edges, heads, tokens):
    count, rows, width = tokens_all.shape
    length = count * tokens
    block = 256
    part = heads * HEAD_DIM
    batch, two = edges.shape[1] // KINDS, edges.shape[2]
    wide = (heads, length, 2 * HEAD_DIM)
    return pl.pallas_call(
        functools.partial(attend_back_kernel, heads, tokens),
        grid=(length // block,),
        in_specs=[
            pl.BlockSpec((count, rows, width), lambda i: (0, 0, 0)),
            pl.BlockSpec(w_heads.shape, lambda i: (0, 0)),
        ]
        + [pl.BlockSpec(wide, lambda i: (0, 0, 0))] * 3
        + [
            pl.BlockSpec((length, 2 * part), lambda i: (0, 0)),
            pl.BlockSpec((length, part + HEAD_DIM), lambda i: (0, 0)),
            pl.BlockSpec(edges.shape, lambda i: (0, 0, 0)),
        ],
        out_specs=[
            pl.BlockSpec((block, width), lambda i: (i, 0)),
            pl.BlockSpec(w_heads.shape, lambda i: (0, 0)),
            pl.BlockSpec((batch, 1, two), lambda i: (0, 0, 0)),
        ],
        out_shape=[
            jax.ShapeDtypeStruct((length, width), BF16),
            jax.ShapeDtypeStruct(w_heads.shape, F32),
            jax.ShapeDtypeStruct((batch, 1, two), F32),
        ],
        scratch_shapes=[pltpu.VMEM(wide, BF16), pltpu.VMEM(edges.shape, F32)],
        compiler_params=params(),
        cost_estimate=cost(
            28 * heads * length * length * HEAD_DIM,
            length * (width * 4 + 8 * part + 2 * part),
            2 * heads * length * length,
        ),
        name="attend_back",
    )(tokens_all, w_heads, *saved, kept, grads, edges)


def unpack(received, heads, batch):
    count, rows, wide = received.shape
    groups, part = HEADS // heads, heads * HEAD_DIM
    width = groups * part
    return pl.pallas_call(
        functools.partial(unpack_kernel, groups, part),
        grid=(batch,),
        in_specs=[pl.BlockSpec((groups, rows, wide), lambda s: (s, 0, 0))],
        out_specs=[
            pl.BlockSpec((rows, width), lambda s: (s, 0)),
            pl.BlockSpec((groups, KINDS * batch, 2 * GRU_H), lambda s: (s, 0, 0)),
        ],
        out_shape=[
            jax.ShapeDtypeStruct((batch * rows, width), BF16),
            jax.ShapeDtypeStruct((count, KINDS * batch, 2 * GRU_H), F32),
        ],
        compiler_params=params(),
        cost_estimate=cost(0, 2 * received.size + 2 * batch * rows * width),
        name="unpack",
    )(received)


def spread_columns(pieces, heads):
    groups, rows, wide = pieces.shape
    return pl.pallas_call(
        functools.partial(spread_columns_kernel, heads),
        out_shape=jax.ShapeDtypeStruct((rows, groups * wide), F32),
        compiler_params=params(),
        cost_estimate=cost(1, 1),
        name="spread_columns",
    )(pieces)


def send_grad(d_attn, w_out, edges, heads, batch):
    total, width = d_attn.shape
    rows = total // batch
    groups, part = HEADS // heads, heads * HEAD_DIM
    wide = part + HEAD_DIM
    return pl.pallas_call(
        functools.partial(send_grad_kernel, groups, part),
        grid=(batch,),
        in_specs=[
            pl.BlockSpec((rows, width), lambda s: (s, 0)),
            whole_block(width, width),
            whole_block(*edges.shape),
        ],
        out_specs=pl.BlockSpec((groups, rows, wide), lambda s: (s, 0, 0)),
        out_shape=jax.ShapeDtypeStruct((batch * groups, rows, wide), BF16),
        compiler_params=params(),
        cost_estimate=cost(
            2 * total * width * width, 2 * (d_attn.size + w_out.size + total * groups * wide)
        ),
        name="send_grad",
    )(d_attn, w_out, edges)


def feed_forward_kernel(hidden_ref, w_ref, bias_ref, inner_ref, slope_ref):
    pre = matmul(hidden_ref[...], w_ref[...]) + bias_ref[...]
    at = jnp.abs(pre) * (0.5**0.5)
    near = 1.0 / (1.0 + 0.3275911 * at)
    gauss = jnp.exp(-at * at)
    series = 1.061405429
    for term in (-1.453152027, 1.421413741, -0.284496736, 0.254829592):
        series = series * near + term
    tail = 0.5 * series * near * gauss
    below = jnp.where(pre < 0.0, tail, 1.0 - tail)
    inner_ref[...] = (pre * below).astype(BF16)
    slope_ref[...] = (below + pre * gauss * (2.0 * jnp.pi) ** -0.5).astype(BF16)


def feed_forward(hidden, w_up, bias):
    rows, width = hidden.shape
    wide = w_up.shape[1]
    block = 512
    column = pl.BlockSpec((rows, block), lambda i: (0, i))
    return pl.pallas_call(
        feed_forward_kernel,
        grid=(wide // block,),
        in_specs=[
            whole_block(rows, width),
            pl.BlockSpec((width, block), lambda i: (0, i)),
            pl.BlockSpec((1, block), lambda i: (0, i)),
        ],
        out_specs=[column, column],
        out_shape=[jax.ShapeDtypeStruct((rows, wide), BF16)] * 2,
        compiler_params=params(),
        cost_estimate=cost(
            2 * rows * width * wide, 2 * (hidden.size + w_up.size + 2 * rows * wide), rows * wide
        ),
        name="feed_forward",
    )(hidden, w_up, bias)


def gradients_kernel(
    blocks, hidden1_ref, context_ref, hidden2_ref, char_ref, pre_ref, attn_ref, joined_ref, out_ref
):
    step = pl.program_id(0)
    width = hidden2_ref.shape[1]

    def put(at, left_ref, right):
        @pl.when((step < blocks) if at is None else (step == blocks + at))
        def store():
            out_ref[...] = matmul_tn(left_ref[...], right()).astype(BF16)

    put(None, hidden1_ref, lambda: pre_ref[...])
    put(0, context_ref, lambda: attn_ref[...])
    put(1, hidden2_ref, lambda: joined_ref[:, :width])
    put(2, char_ref, lambda: joined_ref[:, width:])


def gradients(hidden1, context, hidden2, chars, d_pre, d_attn, d_joined):
    rows, width = hidden1.shape
    blocks = d_pre.shape[1] // width
    whole = whole_block(rows, width)
    return pl.pallas_call(
        functools.partial(gradients_kernel, blocks),
        grid=(blocks + 3,),
        in_specs=[whole] * 4
        + [
            pl.BlockSpec((rows, width), lambda i: (0, jnp.minimum(i, blocks - 1))),
            whole,
            whole_block(rows, 2 * width),
        ],
        out_specs=pl.BlockSpec((width, width), lambda i: (0, i)),
        out_shape=jax.ShapeDtypeStruct((width, (blocks + 3) * width), BF16),
        compiler_params=params(),
        cost_estimate=cost(1, 1),
        name="gradients",
    )(hidden1, context, hidden2, chars, d_pre, d_attn, d_joined)


def store_halves(total, keep_ref, send_ref, lead):
    half = total.shape[0] // 2
    halves = (total[:half].astype(BF16), total[half:].astype(BF16))
    for mine in (0, 1):

        @pl.when(lax.rem(lax.axis_index("ctx"), 2) == mine)
        def store():
            keep_ref[lead] = halves[mine]
            send_ref[lead] = halves[1 - mine]


def down_grad_kernel(own_ref, core_ref, far_ref, far_core_ref, grad_ref, keep_ref, send_ref):
    total = jnp.zeros((own_ref.shape[1], grad_ref.shape[2]), F32)
    for other, inner_ref in enumerate((own_ref, core_ref, far_ref, far_core_ref)):
        source = jnp.bitwise_xor(lax.axis_index("fsdp"), other)
        total = total + matmul_tn(inner_ref[...], grad_ref[source])
    store_halves(total, keep_ref, send_ref, ...)


def down_gradient(inner, grads):
    half = jax.ShapeDtypeStruct((inner[0].shape[1] // 2, grads.shape[2]), BF16)
    return pl.pallas_call(
        down_grad_kernel,
        out_shape=[half, half],
        compiler_params=params(),
        cost_estimate=cost(1, 1),
        name="down_gradient",
    )(*inner, grads)


def conv_grad_kernel(
    own_ref, core_ref, far_ref, far_core_ref, grad_ref, keep_ref, send_ref, side_scr
):
    tap = pl.program_id(0)
    refs = (own_ref, core_ref, far_ref, far_core_ref)
    batch = grad_ref.shape[0] // len(refs)
    rows = side_scr.shape[0] // batch
    shape = (rows, grad_ref.shape[2])
    row = lax.broadcasted_iota(jnp.int32, shape, 0)
    total = jnp.zeros((own_ref.shape[1], grad_ref.shape[2]), F32)
    for other, joined_ref in enumerate(refs):
        first = jnp.bitwise_xor(lax.axis_index("fsdp"), other) * batch
        for block in range(batch):
            here = pl.ds(block * rows, rows)
            grad = grad_ref[first + block].astype(F32)
            mid = grad[:rows]

            @pl.when(tap == 0)
            def earlier():
                moved = pltpu.roll(mid, rows - 1, 0)
                last = jnp.broadcast_to(grad[rows + 1 : rows + 2], shape)
                side_scr[here] = jnp.where(row == rows - 1, last, moved).astype(BF16)

            @pl.when(tap == 1)
            def same():
                side_scr[here] = mid.astype(BF16)

            @pl.when(tap == 2)
            def later():
                moved = pltpu.roll(mid, 1, 0)
                before = jnp.broadcast_to(grad[rows : rows + 1], shape)
                side_scr[here] = jnp.where(row == 0, before, moved).astype(BF16)

        total = total + matmul_tn(joined_ref[...], side_scr[...])
    store_halves(total, keep_ref, send_ref, 0)


def conv_gradient(joined, grads, rows, part):
    count, tall, wide = grads.shape
    wide = wide // 2
    own = joined[0].shape
    out = jax.ShapeDtypeStruct((3, own[1] // 2, wide), BF16)
    return pl.pallas_call(
        conv_grad_kernel,
        grid=(3,),
        in_specs=[pl.BlockSpec(own, lambda k: (0, 0))] * 4
        + [pl.BlockSpec((count, tall, wide), lambda k: (0, 0, part))],
        out_specs=[pl.BlockSpec((1,) + out.shape[1:], lambda k: (k, 0, 0))] * 2,
        out_shape=[out, out],
        scratch_shapes=[pltpu.VMEM((own[0], wide), BF16)],
        compiler_params=params(),
        cost_estimate=cost(1, 1),
        name="conv_gradient",
    )(*joined, grads)


def last_grads_kernel(chars_ref, gates_ref, small_ref, heads_ref, out_ref):
    wide = gates_ref.shape[1]
    narrow = 128
    out_ref[:, :wide] = matmul_tn(chars_ref[...], gates_ref[...]).astype(BF16)
    count = small_ref.shape[0]
    eye = jnp.where(
        lax.broadcasted_iota(jnp.int32, (count, narrow), 0)
        == lax.broadcasted_iota(jnp.int32, (count, narrow), 1),
        1.0,
        0.0,
    ).astype(BF16)
    out_ref[:, wide : wide + narrow] = matmul_tn(small_ref[...].astype(BF16), eye).astype(BF16)
    out_ref[:, wide + narrow :] = heads_ref[...].astype(BF16)


def last_gradients(chars, d_gates, small, heads_grad):
    width = chars.shape[1]
    wide = d_gates.shape[1] + 128 + heads_grad.shape[1]
    return pl.pallas_call(
        last_grads_kernel,
        out_shape=jax.ShapeDtypeStruct((width, wide), BF16),
        compiler_params=params(),
        cost_estimate=cost(1, 1),
        name="last_gradients",
    )(chars, d_gates, small, heads_grad)


def block_size(rows):
    size = min(rows, BLOCK_LIMIT)
    while rows % size != 0:
        size = size - 1
    return size


def split_blocks(array, size):
    return array.reshape((array.shape[0] // size, size) + array.shape[1:])


def to_heads(matrix):
    return matrix.reshape(matrix.shape[0], HEADS, HEAD_DIM)


def masked_exp(query_heads, key_heads, query_seg, key_seg):
    scores = jnp.einsum(
        "qhd,khd->hqk", query_heads, key_heads, preferred_element_type=F32
    ) * HEAD_DIM ** (-0.5)
    same = (query_seg[:, None] == key_seg[None, :])[None, :, :]
    return jnp.where(same, jnp.exp(scores), 0.0)


def everyone(rows):
    return lax.all_gather(rows, "ctx", axis=0, tiled=True)


def gathered_attention(qkv, seg_row):
    tok_rows, width = qkv.shape[0], qkv.shape[1] // 3
    query_heads = to_heads(qkv[:, :width])
    pieces = (everyone(qkv[:, width : 2 * width]), everyone(qkv[:, 2 * width :]), everyone(seg_row))
    size = block_size(pieces[0].shape[0])

    def step(acc, item):
        key_block, value_block, seg_block = item
        expvals = masked_exp(query_heads, to_heads(key_block), seg_row, seg_block)
        part_num = jnp.einsum(
            "hqk,khd->qhd", expvals.astype(BF16), to_heads(value_block),
            preferred_element_type=F32,
        )
        return ((acc[0] + part_num, acc[1] + jnp.transpose(jnp.sum(expvals, axis=-1))), None)

    (numer, total), unused = lax.scan(
        step,
        (jnp.zeros((tok_rows, HEADS, HEAD_DIM), F32), jnp.zeros((tok_rows, HEADS), F32)),
        tuple(split_blocks(piece, size) for piece in pieces),
    )
    return numer / total[:, :, None], total


def gathered_attention_back(qkv, seg_row, context, total, d_context):
    tok_rows, width = qkv.shape[0], qkv.shape[1] // 3
    scale = HEAD_DIM ** (-0.5)
    d_context = to_heads(d_context)
    query_rows, key_rows, value_rows = (qkv[:, i * width : (i + 1) * width] for i in range(3))
    grad_heads = (d_context / total[:, :, None]).astype(BF16)
    delta = jnp.sum(d_context * context, axis=-1) / total
    key_heads, value_heads, query_heads = (
        to_heads(key_rows), to_heads(value_rows), to_heads(query_rows)
    )
    zero_heads = jnp.zeros((tok_rows, HEADS, HEAD_DIM), F32)
    seg_all = everyone(seg_row)
    size = block_size(seg_all.shape[0])

    def key_step(acc, item):
        query_block, grad_block, delta_block, seg_block = item
        query_h, grad_h = to_heads(query_block), to_heads(grad_block)
        expvals = masked_exp(query_h, key_heads, seg_block, seg_row)
        dprob = jnp.einsum("qhd,khd->hqk", grad_h, value_heads, preferred_element_type=F32)
        dscore = (expvals * (dprob - jnp.transpose(delta_block)[:, :, None])).astype(BF16)
        dkey = acc[0] + scale * jnp.einsum(
            "hqk,qhd->khd", dscore, query_h, preferred_element_type=F32
        )
        dval = acc[1] + jnp.einsum(
            "hqk,qhd->khd", expvals.astype(BF16), grad_h, preferred_element_type=F32
        )
        return ((dkey, dval), None)

    (dkey, dval), unused = lax.scan(
        key_step,
        (zero_heads, zero_heads),
        tuple(
            split_blocks(piece, size)
            for piece in (
                everyone(query_rows),
                everyone(grad_heads.reshape(tok_rows, width)),
                everyone(delta),
                seg_all,
            )
        ),
    )

    def query_step(acc, item):
        key_block, value_block, seg_block = item
        key_h = to_heads(key_block)
        expvals = masked_exp(query_heads, key_h, seg_row, seg_block)
        dprob = jnp.einsum(
            "qhd,khd->hqk", grad_heads, to_heads(value_block), preferred_element_type=F32
        )
        dscore = (expvals * (dprob - jnp.transpose(delta)[:, :, None])).astype(BF16)
        return (
            acc + scale * jnp.einsum("hqk,khd->qhd", dscore, key_h, preferred_element_type=F32),
            None,
        )

    dquery, unused = lax.scan(
        query_step,
        zero_heads,
        tuple(
            split_blocks(piece, size)
            for piece in (everyone(key_rows), everyone(value_rows), seg_all)
        ),
    )
    return jnp.concatenate(
        [part.reshape(tok_rows, width) for part in (dquery, dkey, dval)], axis=1
    ).astype(BF16)


def neighbours(rows):
    count = lax.axis_size("ctx")
    up = [(i, i + 1) for i in range(count - 1)]
    down = [(j, i) for i, j in up]
    before = lax.ppermute(rows[:, -1], "ctx", up)
    after = lax.ppermute(rows[:, 0], "ctx", down)
    return before[:, None], after[:, None]


def shifted(rows, before, after):
    later = jnp.concatenate([before, rows[:, :-1]], axis=1)
    earlier = jnp.concatenate([rows[:, 1:], after], axis=1)
    return later, earlier


def routed():
    return lax.axis_size("ctx") == 8 and lax.axis_size("fsdp") == 4


STEPS = (1, 2, 4)
OTHER_STEPS = (1, 4, 2)
ORDER = "XABTXABDXTABDXGKTABDGKTDGKTDGKABTGDGTDG"


def flip(value, axis, bit):
    return lax.ppermute(value, axis, [(i, i ^ bit) for i in range(lax.axis_size(axis))])


def slot(steps=STEPS):
    me = lax.axis_index("ctx")
    first, second, third = ((me // bit) % 2 for bit in steps)
    return first * 4 + second * 2 + third


def own_columns(value):
    count, mine = lax.axis_size("fsdp"), lax.axis_index("fsdp")
    wide = value.shape[1] // count
    pieces = []
    for other in range(count):
        piece = lax.dynamic_slice_in_dim(value, jnp.bitwise_xor(mine, other) * wide, wide, 1)
        pieces.append(flip(piece, "fsdp", other) if other else piece)
    return pieces


class CtxSum:
    def __init__(self, value, steps=STEPS):
        self.value = value
        self.axis = value.ndim - 2
        self.stage = 0
        self.steps = steps

    @classmethod
    def begun(cls, keep, send, steps=STEPS):
        chain = cls(keep, steps)
        chain.keep = keep
        chain.send(send, steps[0])
        chain.stage = 1
        return chain

    def halve(self, value, bit):
        mine = (lax.axis_index("ctx") // bit) % 2
        half = value.shape[self.axis] // 2
        send = lax.dynamic_slice_in_dim(value, (1 - mine) * half, half, self.axis)
        self.keep = lax.dynamic_slice_in_dim(value, mine * half, half, self.axis)
        self.send(send, bit)

    def send(self, value, bit):
        self.sent = value
        self.got = flip(value, "ctx", bit)

    def advance(self, *others):
        stage = self.stage
        self.stage = stage + 1
        if stage == 0:
            self.halve(after(self.value, *others), self.steps[0])
        elif stage <= 3:
            got = after(self.got, *others).astype(F32)
            piece = (self.keep.astype(F32) + got).astype(BF16)
            if stage < 3:
                self.halve(piece, self.steps[stage])
            else:
                self.send(piece[None], self.steps[2])
        else:
            piece = jnp.concatenate([self.sent, after(self.got, *others)], axis=0)
            if stage < 6:
                self.send(piece, self.steps[5 - stage])
            else:
                self.result = self.sent = piece
        return self.sent


class HeadSum(CtxSum):
    def advance(self, *others):
        stage = self.stage
        self.stage = stage + 1
        if stage == 0:
            self.send(after(self.value, *others), 4)
        elif stage == 1:
            piece = self.sent.astype(F32) + after(self.got, *others).astype(F32)
            self.send(piece.astype(BF16)[None], 1)
        else:
            piece = jnp.concatenate([self.sent, after(self.got, *others)], axis=0)
            if stage == 2:
                self.send(piece, 2)
            else:
                self.result = self.sent = piece
        return self.sent


class TokenSum(CtxSum):
    def advance(self, *others):
        me = lax.axis_index("ctx")
        stage = self.stage
        self.stage = stage + 1
        if stage == 0:
            piece = after(self.value, *others)
        else:
            got = after(self.got, *others).astype(F32)
            if stage == 3:
                keep = self.keep.astype(F32)
                ordered = (jnp.concatenate([keep, got]), jnp.concatenate([got, keep]))
                self.result = self.sent = jnp.where(me // 4 == 0, *ordered)
                return self.sent
            piece = (self.keep.astype(F32) + got).astype(BF16)
            piece = jnp.squeeze(piece, axis=3 - stage)
        bit = STEPS[stage]
        mine = (me // bit) % 2
        axis = 2 - stage
        self.keep = lax.dynamic_slice_in_dim(piece, mine, 1, axis)
        self.send(lax.dynamic_slice_in_dim(piece, 1 - mine, 1, axis), bit)
        return self.sent


def run_in_order(chains, finish, begin):
    last, done = (), {}
    final = max(i for i, name in enumerate(ORDER[:-2]) if name == "G")
    for event, name in enumerate(ORDER):
        others = last
        if event == final or event >= len(ORDER) - 2:
            ready = [done[other] for other in "ABKDT" if other in done]
            others = others + tuple(jax.tree.leaves(ready))
        step = chains[name].advance if name in chains else begin[name]
        last = (step(*others),)
        chain = chains[name]
        if event == ORDER.index("T"):
            begin["last"](*last)
        if hasattr(chain, "result"):
            done[name] = finish[name](chain.result, done)
    return done


def settle_kernel(order_ref, in_ref, *out_refs):
    at = 0
    for out_ref in out_refs:
        wide = out_ref.shape[-1]
        out_ref[...] = in_ref[0, ..., at : at + wide].astype(F32)
        at = at + wide


def settle_half_kernel(order_ref, in_ref, *refs):
    refs[-1][...] = in_ref[0].astype(F32)


def settle_half(pieces, steps, part, whole=None):
    lead = pieces.shape[1:-2]
    rows, width = pieces.shape[-2:]
    none = (0,) * len(lead)
    order = jnp.bitwise_xor(slot(steps), jnp.arange(8, dtype=jnp.int32))
    given = [] if whole is None else [whole]
    return pl.pallas_call(
        settle_half_kernel,
        grid_spec=pltpu.PrefetchScalarGridSpec(
            num_scalar_prefetch=1,
            grid=(8,),
            in_specs=[
                pl.BlockSpec((1,) + lead + (rows, width), lambda r, o: (r,) + none + (0, 0))
            ]
            + [pl.BlockSpec(memory_space=pl.ANY)] * len(given),
            out_specs=pl.BlockSpec(lead + (rows, width), lambda r, o: none + (o[r], part)),
        ),
        out_shape=jax.ShapeDtypeStruct(lead + (8 * rows, 2 * width), F32),
        input_output_aliases={2: 0} if given else {},
        compiler_params=params(),
        cost_estimate=cost(1, 1),
        name="settle_half",
    )(order, pieces, *given)


def settle(pieces, widths):
    lead = pieces.shape[1:-2]
    rows, total = pieces.shape[-2:]
    order = jnp.bitwise_xor(slot(), jnp.arange(8, dtype=jnp.int32))
    none = (0,) * len(lead)
    return pl.pallas_call(
        settle_kernel,
        grid_spec=pltpu.PrefetchScalarGridSpec(
            num_scalar_prefetch=1,
            grid=(8,),
            in_specs=[
                pl.BlockSpec((1,) + lead + (rows, total), lambda r, o: (r,) + none + (0, 0))
            ],
            out_specs=[
                pl.BlockSpec(lead + (rows, width), lambda r, o: none + (o[r], 0))
                for width in widths
            ],
        ),
        out_shape=[jax.ShapeDtypeStruct(lead + (8 * rows, width), F32) for width in widths],
        compiler_params=params(),
        cost_estimate=cost(pieces.size, 6 * pieces.size),
        name="settle",
    )(order, pieces)


def move(sources, stages, targets, arrived, left):
    ins = [
        pltpu.make_async_copy(source, stage, arrived.at[i])
        for i, (source, stage) in enumerate(zip(sources, stages))
    ]
    for copy in ins:
        copy.start()
    outs = []
    for i, (copy, stage, target) in enumerate(zip(ins, stages, targets)):
        copy.wait()
        outs.append(pltpu.make_async_copy(stage, target, left.at[i]))
        outs[-1].start()
    for copy in outs:
        copy.wait()


def place_own_kernel(spans, own_ref, core_ref, *rest):
    outs, (own_scr, core_scr, arrived, left) = rest[:-4], rest[-4:]
    mine = lax.axis_index("fsdp")
    sources, stages, targets, at = [], [], [], 0
    for span, out_ref in zip(spans, outs):
        there = pl.ds(at, span)
        for ref, scr, shard in (
            (own_ref, own_scr, mine),
            (core_ref, core_scr, jnp.bitwise_xor(mine, 1)),
        ):
            sources.append(ref.at[there])
            stages.append(scr.at[there])
            targets.append(out_ref.at[shard])
        at = at + span
    move(sources, stages, targets, arrived, left)


def place_kernel(spans, order, piece_ref, core_ref, *rest):
    outs, (piece_scr, core_scr, arrived, left) = rest[len(spans) : -4], rest[-4:]
    place = slot()
    mine = lax.axis_index("fsdp")
    sources, stages, targets = [], [], []
    for ref, scr, shard in (
        (piece_ref, piece_scr, jnp.bitwise_xor(mine, 2)),
        (core_ref, core_scr, jnp.bitwise_xor(mine, 3)),
    ):
        for position, other in enumerate(order):
            at = 0
            for span, out_ref in zip(spans, outs):
                part = span // 8
                there = pl.multiple_of(jnp.bitwise_xor(place, other) * part, part)
                sources.append(ref.at[position, pl.ds(at, part)])
                stages.append(scr.at[position, pl.ds(at, part)])
                targets.append(out_ref.at[shard, pl.ds(there, part)])
                at = at + part
    move(sources, stages, targets, arrived, left)


def after(value, *others):
    return lax.optimization_barrier((value,) + others)[0]


class SpreadGather:
    def __init__(self, shards):
        self.spans = tuple(shard.shape[0] for shard in shards)
        self.width = shards[0].shape[1]
        place = slot()
        self.own = jnp.concatenate(shards, axis=0) if len(shards) > 1 else shards[0]
        piece = [
            lax.dynamic_slice_in_dim(shard, place * (span // 8), span // 8, 0)
            for shard, span in zip(shards, self.spans)
        ]
        self.base = None
        self.got = flip(jnp.concatenate(piece, axis=0), "fsdp", 2)[None]
        self.core = flip(self.own, "fsdp", 1)
        self.order = [0]

    def take(self, others):
        got = after(self.got, *others) if others else self.got
        return got if self.base is None else jnp.concatenate([self.base, got], axis=0)

    def double(self, bit, *others):
        self.base = self.take(others)
        self.got = flip(self.base, "ctx", bit)
        self.order = self.order + [other ^ (4 // bit) for other in self.order]

    def cores(self, *others):
        self.piece = self.take(others)
        self.core_piece = flip(self.piece, "fsdp", 1)

    def place_own(self, *others):
        spans, width = self.spans, self.own.shape[1]
        self.whole = pl.pallas_call(
            functools.partial(place_own_kernel, spans),
            in_specs=[pl.BlockSpec(memory_space=pl.ANY)] * 2,
            out_specs=[pl.BlockSpec(memory_space=pl.ANY)] * len(spans),
            out_shape=[jax.ShapeDtypeStruct((4, span, width), BF16) for span in spans],
            scratch_shapes=[pltpu.VMEM(self.own.shape, BF16)] * 2
            + [pltpu.SemaphoreType.DMA((2 * len(spans),))] * 2,
            compiler_params=params(),
            cost_estimate=cost(0, 8 * sum(spans) * width),
            name="place_own",
        )(after(self.own, *others), self.core)

    def finish(self):
        spans, width = self.spans, self.own.shape[1]
        anywhere = [pl.BlockSpec(memory_space=pl.ANY)] * len(spans)
        return pl.pallas_call(
            functools.partial(place_kernel, spans, self.order),
            in_specs=[pl.BlockSpec(memory_space=pl.ANY)] * 2 + anywhere,
            out_specs=anywhere,
            out_shape=[jax.ShapeDtypeStruct((4, span, width), BF16) for span in spans],
            scratch_shapes=[pltpu.VMEM(self.piece.shape, BF16)] * 2
            + [pltpu.SemaphoreType.DMA((16 * len(spans),))] * 2,
            input_output_aliases={2 + i: i for i in range(len(spans))},
            compiler_params=params(),
            cost_estimate=cost(0, 8 * sum(spans) * width),
            name="place",
        )(self.piece, self.core_piece, *self.whole)


def over_fsdp(grads):
    return lax.psum_scatter(grads, "fsdp", scatter_dimension=0, tiled=True)


def plain_sum(grads, axis=0):
    share = lax.psum_scatter(grads, "fsdp", scatter_dimension=axis, tiled=True)
    return lax.psum(share.astype(F32), "ctx")


def local(
    tokens, chars, segment, char_end, w_qkv, w_out, norm1_gain, norm1_bias, w_up, b_up, w_down,
    norm2_gain, norm2_bias, w_gru, b_gate, w_ftok, w_fchr, w_conv, norm3_gain, norm3_bias,
    norm4_gain, norm4_bias, d_token, d_char,
):
    count, me = lax.axis_size("ctx"), lax.axis_index("ctx")
    shards = lax.axis_size("fsdp")
    batch, rows, width = tokens.shape
    char_rows = chars.shape[1]
    total_rows = batch * rows
    heads = heads_here(batch, count)
    padded_rows = -(-char_rows // 8) * 8

    def gather(weight, axis=0):
        return lax.all_gather(weight, "fsdp", axis=axis, tiled=True)

    own_width = norm1_gain.shape[0]
    vectors = (
        norm1_gain, norm1_bias, norm2_gain, norm2_bias, b_gate, norm3_gain, norm3_bias,
        norm4_gain, norm4_bias,
    )
    columns = jnp.stack(vectors, axis=1)
    columns = jnp.concatenate([columns, b_up.reshape(-1, own_width).T], axis=1)
    small_count = columns.shape[1]
    wide_gru = w_gru.shape[1]
    columns = jnp.pad(columns, ((0, 0), (0, 128 - small_count)))
    width_qkv = w_qkv.shape[1]
    if heads:
        group, part = me % (HEADS // heads), heads * HEAD_DIM
        w_heads = jnp.concatenate(
            [
                lax.dynamic_slice_in_dim(w_qkv, kind * width + group * part, part, 1)
                for kind in range(3)
            ],
            axis=1,
        )
        w_pieces = [w_heads] + [flip(w_heads, "fsdp", other) for other in (1, 2, 3)]
    else:
        w_qkv = gather(w_qkv)
    w_gru = gather(jnp.concatenate([w_gru, columns], axis=1))
    w_out = gather(w_out)
    w_up = gather(w_up)
    columns = w_gru[:, wide_gru : wide_gru + small_count].astype(F32)
    (
        norm1_gain, norm1_bias, norm2_gain, norm2_bias, b_gate, norm3_gain, norm3_bias,
        norm4_gain, norm4_bias,
    ) = (columns[:, i][None, :] for i in range(9))
    b_up = jnp.swapaxes(columns[:, 9:].reshape(shards, own_width, -1), 1, 2).reshape(1, -1)
    w_down = gather(w_down)
    if routed():
        first_taps = SpreadGather([w_conv[0], w_conv[1]])
        last_tap = SpreadGather([w_conv[2], jnp.concatenate([w_ftok, w_fchr], axis=1)])
    else:
        w_ftok = gather(w_ftok)
        w_fchr = gather(w_fchr)
        w_conv = gather(w_conv, 1)

    start = jnp.concatenate([jnp.zeros((batch, 1), jnp.int32), char_end[:, :-1] + 1], axis=1)
    change = (segment[:, 1:] != segment[:, :-1]).astype(F32)
    first = jnp.concatenate([jnp.broadcast_to((me == 0).astype(F32), (batch, 1)), change], axis=1)
    last = jnp.concatenate(
        [change, jnp.broadcast_to((me == count - 1).astype(F32), (batch, 1))], axis=1
    )
    flat_tokens = tokens.reshape(total_rows, width)
    chars_pad = jnp.pad(chars, ((0, 0), (0, padded_rows - char_rows), (0, 0)))
    if routed():
        first_taps.double(4)
        last_tap.double(1)
    gate, cand, decay, cum, state, edges = gru_forward(
        chars_pad, w_gru, b_gate, start[:, None], first[:, None], char_end[:, None],
        last[:, None], char_rows,
    )

    if heads:
        ids = segment.astype(BF16)[:, None, :]
        ids = jnp.pad(ids, ((0, 0), (0, 7), (0, width - rows)))
        sent = jnp.repeat(jnp.concatenate([tokens, ids], axis=1), HEADS // heads, axis=0)
        tokens_all = lax.all_to_all(sent, "ctx", 0, 0, tiled=True)
        packed_context, kept, *saved, w_heads = attend(tokens_all, w_pieces, edges, heads, rows)
        first_taps.double(2, state)
        last_tap.double(4, state)
        first_taps.place_own(packed_context)
        last_tap.place_own(packed_context)
        received = lax.all_to_all(packed_context.reshape(count, rows, -1), "ctx", 0, 0, tiled=True)
        received = after(received, *first_taps.whole, *last_tap.whole)
        context_b, edges_all = unpack(received, heads, batch)
    else:
        qkv = matmul(flat_tokens, w_qkv).astype(BF16).reshape(batch, rows, -1)
        results = [gathered_attention(qkv[i], segment[i]) for i in range(batch)]
        context_b = jnp.concatenate([r[0].reshape(rows, width) for r in results]).astype(BF16)
        edges_all = all_edges(edges)

    attn = matmul(context_b, w_out)
    hidden1, kept1 = layer_norm(flat_tokens.astype(F32) + attn, norm1_gain, norm1_bias)
    hidden1_b = hidden1.astype(BF16)
    inner_b, slope = feed_forward(hidden1_b, w_up, b_up)
    ffn = matmul(inner_b, w_down)
    hidden2, kept2 = layer_norm(hidden1 + ffn, norm2_gain, norm2_bias)
    hidden2_b = hidden2.astype(BF16)
    if routed():
        first_taps.double(1, context_b)
        last_tap.double(2, context_b)
        first_taps.cores(inner_b)
        last_tap.cores(inner_b)
        w_conv = [
            weight.reshape(-1, 2 * width) for weight in first_taps.finish() + last_tap.finish()
        ]
        w_ftok, w_fchr = w_conv[3][:, :width], w_conv[3][:, width:]

    char_tok, enter = gather_states(
        state, cum, edges_all, char_end[:, :, None], start[:, :, None]
    )
    char_tok_b = char_tok.astype(BF16)
    joined = jnp.concatenate(
        [matmul(hidden2_b, w_ftok), matmul(char_tok_b, w_fchr)], axis=1
    ).astype(BF16)

    two = 2 * width
    if routed():
        inner_own = own_columns(inner_b)
        joined = after(joined, *inner_own[1:])
        joined_own = own_columns(joined)
    blocks = joined.reshape(batch, rows, two)
    later, earlier = shifted(blocks, *neighbours(blocks))
    taps = (later.reshape(total_rows, two), joined, earlier.reshape(total_rows, two))
    conv = matmul(taps[1], w_conv[1]) + matmul(taps[0], w_conv[0]) + matmul(taps[2], w_conv[2])
    token_out, kept3 = layer_norm(hidden2 + conv[:, :width], norm3_gain, norm3_bias)
    char_out, kept4 = layer_norm(char_tok + conv[:, width:], norm4_gain, norm4_bias)

    d_in3, gain3_grad, bias3_grad = layer_norm_back(
        d_token.reshape(total_rows, width).astype(F32), norm3_gain, kept3
    )
    d_in4, gain4_grad, bias4_grad = layer_norm_back(
        d_char.reshape(total_rows, width).astype(F32), norm4_gain, kept4
    )
    d_conv = jnp.concatenate([d_in3, d_in4], axis=1).astype(BF16)
    d_before, d_after = neighbours(d_conv.reshape(batch, rows, two))
    if routed():
        d_conv = after(d_conv, *joined_own[1:])
    d_later, d_earlier = shifted(d_conv.reshape(batch, rows, two), d_before, d_after)
    d_joined = (
        matmul_nt(d_conv, w_conv[1])
        + matmul_nt(d_earlier.reshape(total_rows, two), w_conv[0])
        + matmul_nt(d_later.reshape(total_rows, two), w_conv[2])
    ).astype(BF16)
    if routed():
        d_all = gather(
            jnp.concatenate([d_conv.reshape(batch, rows, two), d_before, d_after], axis=1)
        )
    else:
        conv_sum = plain_sum(jnp.stack([matmul_tn(tap, d_conv).astype(BF16) for tap in taps]), 1)

    d_tok_part, d_chr_part = d_joined[:, :width], d_joined[:, width:]
    d_hidden2 = d_in3 + matmul_nt(d_tok_part, w_ftok)
    d_char_tok = d_in4 + matmul_nt(d_chr_part, w_fchr)

    end_line, start_line = char_end[:, None], start[:, None]
    spread, back_cum, carried, back_edges = gru_back(
        d_char_tok.reshape(batch, rows, width), decay, end_line, start_line, char_rows
    )

    d_in2, gain2_grad, bias2_grad = layer_norm_back(d_hidden2, norm2_gain, kept2)
    d_ffn = d_in2.astype(BF16)
    reduced = over_fsdp if routed() else plain_sum
    if routed():
        d_ffn_all = gather(d_ffn[None])
    else:
        second_sum = plain_sum(matmul_tn(inner_b, d_ffn).astype(BF16))
    d_pre = matmul_nt(d_ffn, w_down) * slope.astype(F32)
    bup_grad = jnp.sum(d_pre, axis=0)
    d_pre_low = d_pre.astype(BF16)
    d_hidden1 = d_in2 + matmul_nt(d_pre_low, w_up)
    d_in1, gain1_grad, bias1_grad = layer_norm_back(d_hidden1, norm1_gain, kept1)
    d_attn = d_in1.astype(BF16)
    if heads:
        sent = send_grad(d_attn, w_out, back_edges, heads, batch)
        hidden1_b = after(hidden1_b, sent)
    third = gradients(hidden1_b, context_b, hidden2_b, char_tok_b, d_pre_low, d_attn, d_joined)
    third_sum = reduced(third)

    if heads:
        conv_pieces = [after(joined_own[0], sent, third)] + joined_own[1:]
        first_chain = CtxSum.begun(*conv_gradient(conv_pieces, d_all, rows, 0))
        other_chain = CtxSum.begun(*conv_gradient(conv_pieces, d_all, rows, 1), OTHER_STEPS)
        received = lax.all_to_all(sent, "ctx", 0, 0, tiled=True)
        received = after(received, first_chain.sent, other_chain.sent)
        d_tok_part, heads_grad, back_enter = attend_back(
            tokens_all, w_heads, saved, kept, received.reshape(count * rows, -1), edges_all,
            heads, rows,
        )
        token_chain = TokenSum(d_tok_part.reshape(2, 2, 2, rows, width))
        last = other_chain.advance(first_chain.advance(heads_grad))
        gate = after(gate, last)
    else:
        back_enter = back_entering(edges_all, all_edges(back_edges))
        d_context = matmul_nt(d_attn, w_out).reshape(batch, rows, width)
        d_qkv = jnp.concatenate(
            [
                gathered_attention_back(
                    qkv[i], segment[i], results[i][0], results[i][1], d_context[i]
                )
                for i in range(batch)
            ]
        )
    d_gate_in, bgate_grad = gru_grad(
        gate, cand, decay, cum, state, enter, spread, back_cum, carried, back_enter, char_rows
    )
    d_gate_in = d_gate_in.reshape(batch * padded_rows, -1)
    d_chars = matmul_nt(d_gate_in, w_gru[:, :wide_gru]).astype(BF16)
    d_chars = d_chars.reshape(batch, padded_rows, width)[:, :char_rows]

    if not heads:
        heads_grad = matmul_tn(flat_tokens, d_qkv)
        d_tokens = matmul_nt(d_qkv, w_qkv)

    small = [
        gain1_grad, bias1_grad, gain2_grad, bias2_grad, jnp.sum(bgate_grad, axis=(0, 1)),
        gain3_grad, bias3_grad, gain4_grad, bias4_grad,
    ]
    up_small = jnp.swapaxes(bup_grad.reshape(shards, -1, width // shards), 0, 1)
    small = jnp.concatenate([value[None] for value in small] + [up_small.reshape(-1, width)])
    small = jnp.pad(small, ((0, 16 - small_count), (0, 0)))

    def last_sum(*others):
        gates = after(d_gate_in, *others) if others else d_gate_in
        return last_gradients(
            chars_pad.reshape(batch * padded_rows, width), gates, small, heads_grad
        )

    widths = ((width,), (w_up.shape[1],) + (width,) * 3, (wide_gru, 128, width_qkv))
    if routed():
        own_wide = wide_gru + 128
        chains = dict(
            A=first_chain,
            B=other_chain,
            X=token_chain,
            T=CtxSum(third_sum),
        )

        def begin_down(*others):
            chains["D"] = CtxSum.begun(*down_gradient(after(inner_own, *others), d_ffn_all))
            return chains["D"].sent

        def begin_last(*others):
            chains["last"] = reduced(last_sum(*others))

        def begin_G(*others):
            value = after(chains["last"], *others)
            chains["G"] = CtxSum(value[:, :own_wide])
            chains["K"] = HeadSum(value[:, own_wide:])
            return chains["G"].advance()

        finish = dict(
            A=lambda value, done: settle_half(value, STEPS, 0),
            B=lambda value, done: settle_half(value, OTHER_STEPS, 1, done.pop("A")),
            D=lambda value, done: settle(value, widths[0]),
            T=lambda value, done: settle(value, widths[1]),
            G=lambda value, done: settle(value, widths[2][:2]),
            K=lambda value, done: spread_columns(value, heads),
            X=lambda value, done: value.reshape(total_rows, width),
        )
        done = run_in_order(chains, finish, dict(D=begin_down, G=begin_G, last=begin_last))
        (down_sum,), third = done["D"], done["T"]
        conv_sum = done["B"]
        fourth = [*done["G"], done["K"]]
        d_tokens = done["X"]
    else:
        (down_sum,), third, fourth = (
            jnp.split(value, [sum(split[:i]) for i in range(1, len(split))], axis=1)
            for value, split in zip((second_sum, third_sum, reduced(last_sum())), widths)
        )
    d_tokens = (d_in1 + d_tokens).astype(BF16)
    vector = fourth[1]
    return (
        token_out.astype(BF16).reshape(batch, rows, width),
        char_out.astype(BF16).reshape(batch, rows, width),
        d_tokens.reshape(batch, rows, width),
        d_chars,
        fourth[2],
        third[1],
        vector[:, 0],
        vector[:, 1],
        third[0],
        jnp.swapaxes(vector[:, 9:small_count], 0, 1).reshape(-1),
        down_sum,
        vector[:, 2],
        vector[:, 3],
        fourth[0],
        vector[:, 4],
        third[2],
        third[3],
        conv_sum,
        vector[:, 5],
        vector[:, 6],
        vector[:, 7],
        vector[:, 8],
    )


def solution(mesh):
    rows = P("fsdp", "ctx", None)
    pairs = P("fsdp", "ctx")
    matrix = P("fsdp", None)
    vector = P("fsdp")
    weights = (
        matrix, matrix, vector, vector, matrix, vector, matrix, vector, vector, matrix, vector,
        matrix, matrix, P(None, "fsdp", None), vector, vector, vector, vector,
    )
    return jax.shard_map(
        local,
        mesh=mesh,
        in_specs=(rows, rows, pairs, pairs) + weights + (rows, rows),
        out_specs=(rows,) * 4 + weights,
        check_vma=False,
    )
```
